128 devices in a mesh: dp: 2 (over core), section: 4 (over z), depth: 16 (over y, x).
Axes of the slice: x: 4, y: 4, z: 4, core: 2. Of those that a mesh axis runs over, the one named last changes fastest.
Arguments:
- volume: bfloat16 [2, 32, 32, 32, 128], P('dp', 'depth'), may hold values from -6 to 6
- weights: bfloat16 [4, 3456, 128], P('section'), may hold values from -0.15625 to 0.15625
- biases: bfloat16 [4, 128], P('section'), may hold values from -3 to 3
- cotangent: bfloat16 [2, 32, 32, 32, 128], P('dp', 'depth'), may hold values from -6 to 6
Outputs:
- section_outputs: bfloat16 [4, 2, 32, 32, 32, 128], P('section', 'dp', 'depth')
- input_grads: bfloat16 [4, 2, 32, 32, 32, 128], P('section', 'dp', 'depth')
- weight_grads: float32 [4, 3456, 128], P('section')
- bias_grads: float32 [4, 128], P('section')
The draws below stay inside these ranges and needn't reach their ends.
All inputs are finite; a program needn't handle non-finite values.
Results may differ from the reference program's by a relative error of at most 0.025.
Values may be sent and summed in bfloat16 or wider, within the bound.
No kernel may reach another device: no remote copies, remote signals or barrier semaphores. Data moves between devices by JAX's collectives and lax.ppermute only.
A program may use at most 128 MiB of HBM per device.

```python
import math
import jax
import jax.numpy as jnp
from jax import lax

CHANNELS = 128
HEIGHT = 32
WIDTH = 32
SECTIONS = 4
DEPTH = 32
CROPS = 2


def levels(rng, dims, split, least, largest):
    def one(dim, shards_of):
        draws = jax.random.uniform(jax.random.fold_in(jax.random.fold_in(rng, 6), dim), (shards_of,), jnp.float32, least / len(split), largest / len(split))
        return jnp.repeat(jnp.exp(draws), dims[dim] // shards_of).reshape((-1,) + (1,) * (len(dims) - dim - 1))

    gain = one(*split[0])
    for cut in split[1:]:
        gain = gain * one(*cut)
    return gain


def scatter_about(own_key, shape, scale, reach, cuts=(), kind=jnp.bfloat16):
    gain = levels(own_key, shape, cuts, -0.22, 0.18) if cuts else 1.0
    values = jax.random.normal(own_key, shape, jnp.float32) * scale * gain
    return jnp.minimum(jnp.maximum(values, -reach), reach).astype(kind)


def setup_inputs(seed: int = 0) -> dict:
    splits = jax.random.split(jax.random.key(seed), 5)
    volume = scatter_about(splits[0], (CROPS, DEPTH, HEIGHT, WIDTH, CHANNELS), 1.0, 6.0, ((0, 2), (1, 16)))
    weights = scatter_about(splits[1], (SECTIONS, 27 * CHANNELS, CHANNELS), (27 * CHANNELS // 2) ** -0.5, 0.15625, ((0, 4),))
    biases = scatter_about(splits[2], (SECTIONS, CHANNELS), 0.5, 3.0, ((0, 4),))
    cotangent = scatter_about(splits[3], (CROPS, DEPTH, HEIGHT, WIDTH, CHANNELS), 1.0, 6.0, ((0, 2), (1, 16)))
    return {"volume": volume, "weights": weights, "biases": biases, "cotangent": cotangent}


def pad_volume(field):
    return jnp.pad(field, ((0, 0), (1, 1), (1, 1), (1, 1), (0, 0)))

def convolve(padded, weight_mat):
    chans = padded.shape[4]
    depth_n = padded.shape[1] - 2
    height_n = padded.shape[2] - 2
    width_n = padded.shape[3] - 2
    taps = weight_mat.reshape(27, chans, weight_mat.shape[1])
    totals = jnp.zeros((padded.shape[0] * depth_n * height_n * width_n, weight_mat.shape[1]), jnp.float32)
    for tap_index in range(27):
        plane_off = tap_index // 9
        row_off = tap_index // 3 % 3
        col_off = tap_index % 3
        segment = padded[:, plane_off:plane_off + depth_n, row_off:row_off + height_n, col_off:col_off + width_n, :].reshape(-1, chans)
        totals = totals + jnp.dot(segment, taps[tap_index], preferred_element_type=jnp.float32)
    return totals.reshape(padded.shape[0], depth_n, height_n, width_n, -1)

def kernel_grad(padded, delta_vol):
    chans = padded.shape[4]
    depth_n = padded.shape[1] - 2
    height_n = padded.shape[2] - 2
    width_n = padded.shape[3] - 2
    flat_delta = delta_vol.reshape(-1, delta_vol.shape[4])
    blocks = []
    for tap_index in range(27):
        plane_off = tap_index // 9
        row_off = tap_index // 3 % 3
        col_off = tap_index % 3
        segment = padded[:, plane_off:plane_off + depth_n, row_off:row_off + height_n, col_off:col_off + width_n, :].reshape(-1, chans)
        blocks.append(lax.dot_general(segment, flat_delta, (((0,), (0,)), ((), ())), preferred_element_type=jnp.float32))
    return jnp.concatenate(blocks, axis=0)

def flip_weight(weight_mat):
    chans = weight_mat.shape[1]
    taps = weight_mat.reshape(27, -1, chans)
    return jnp.transpose(taps[::-1], (0, 2, 1)).reshape(-1, chans)

def silu_slope(values):
    logistic = jax.nn.sigmoid(values)
    return logistic * (1.0 + values * (1.0 - logistic))

def reference(volume, weights, biases, cotangent):
    grad_scale = 1.0 / math.sqrt(CROPS * DEPTH * HEIGHT * WIDTH)
    current = volume
    saved_pads = []
    saved_pres = []
    results = []
    for layer in range(SECTIONS):
        padded = pad_volume(current)
        pre_full = convolve(padded, weights[layer]) + biases[layer].astype(jnp.float32)
        saved_pads.append(padded)
        saved_pres.append(pre_full.astype(jnp.bfloat16))
        current = (pre_full * jax.nn.sigmoid(pre_full)).astype(jnp.bfloat16)
        results.append(current)
    incoming = cotangent
    backs = [None] * SECTIONS
    kernel_grads = [None] * SECTIONS
    bias_terms = [None] * SECTIONS
    for layer in reversed(range(SECTIONS)):
        pre_val = saved_pres[layer].astype(jnp.float32)
        delta_vol = (incoming.astype(jnp.float32) * silu_slope(pre_val)).astype(jnp.bfloat16)
        back = convolve(pad_volume(delta_vol), flip_weight(weights[layer])).astype(jnp.bfloat16)
        kernel_grads[layer] = kernel_grad(saved_pads[layer], delta_vol) * grad_scale
        bias_terms[layer] = lax.optimization_barrier(jnp.sum(delta_vol.astype(jnp.float32), axis=(0, 1, 2, 3))) * grad_scale
        backs[layer] = back
        incoming = back
    return (jnp.stack(results), jnp.stack(backs), jnp.stack(kernel_grads), jnp.stack(bias_terms))
```

```python
import math

import jax
import jax.numpy as jnp
from jax import lax
from jax.experimental import pallas as pl
from jax.experimental.pallas import tpu as pltpu
from jax.sharding import PartitionSpec as P

BF = jnp.bfloat16
F32 = jnp.float32

SMEM = pl.BlockSpec(memory_space=pltpu.SMEM)
VMEM = pl.BlockSpec(memory_space=pltpu.VMEM)
ANY = pl.BlockSpec(memory_space=pl.ANY)


def sds(shape, dtype=BF):
    return jax.ShapeDtypeStruct(shape, dtype)


def call(body, name, out, n_any_or_specs, scratch, out_specs=None):
    return pl.pallas_call(
        body,
        name=name,
        grid=(1,),
        out_shape=out,
        in_specs=n_any_or_specs,
        out_specs=out_specs if out_specs is not None else jax.tree.map(lambda _: VMEM, out),
        scratch_shapes=scratch,
        compiler_params=pltpu.CompilerParams(vmem_limit_bytes=48 * 1024 * 1024),
    )


def column(w_ref, t):
    return jnp.concatenate(
        [jnp.concatenate([w_ref[t, 3 * k + c] for c in range(3)], axis=1) for k in range(9)], axis=0
    )


def conv_plane(x_ref, p, wide, nr):
    W, C = x_ref.shape[2], x_ref.shape[3]
    m = nr * W
    lhs = jnp.concatenate(
        [x_ref[p + a, b : b + nr].reshape(m, C) for a in range(3) for b in range(3)], axis=1
    )
    y = jnp.dot(lhs, wide, preferred_element_type=F32)
    x_pos = lax.broadcasted_iota(jnp.int32, (m, C), 0) % W
    left = jnp.where(x_pos == 0, 0.0, pltpu.roll(y[:, :C], 1, 0))
    right = jnp.where(x_pos == W - 1, 0.0, pltpu.roll(y[:, 2 * C :], m - 1, 0))
    return y[:, C : 2 * C] + left + right


def inside(nr, W, C, first_row, H, plane, D):
    row = first_row + lax.broadcasted_iota(jnp.int32, (nr * W, C), 0) // W
    return (row >= 0) & (row < H) & (plane >= 0) & (plane < D)


def slope(pre):
    q = jax.nn.sigmoid(pre)
    return q * (1.0 + pre * (1.0 - q))


def assemble(dst, lo, own, hi, d, last):
    zero = jnp.zeros(lo.shape, BF)
    dst[0:2] = jnp.where(d > 0, lo[...], zero)
    dst[2:4] = own[...]
    dst[4:6] = jnp.where(d < last, hi[...], zero)


def forward_pair(geo, first, n0, bias_rows):
    R, H, D, last = geo

    def body(idx, own, lo, hi, w, bias, *rest):
        return idx, own, lo, hi, w, bias, rest

    return body


def shards(volume, weights, biases, cotangent):
    n_sec = lax.axis_size("section")
    n_dep = lax.axis_size("depth")
    n_dp = lax.axis_size("dp")
    s = lax.axis_index("section")
    d = lax.axis_index("depth")
    c = lax.axis_index("dp")
    assert n_sec == 4 and n_dep == 16 and n_dp == 2
    PL, H, W, C = volume.shape[1:]
    assert PL == 2
    R = H // n_sec
    D = PL * n_dep
    last = n_dep - 1
    grad_scale = 1.0 / math.sqrt(n_dp * D * H * W)
    idx = jnp.stack([s, d, c]).astype(jnp.int32)
    TAP = 27 * C
    HALF = TAP // 2
    HB = HALF + 16

    def sec(v, k):
        return lax.ppermute(v, "section", [(i, (i + k) % n_sec) for i in range(n_sec)])

    def dep(v, k):
        return lax.ppermute(v, "depth", [(i, (i + k) % n_dep) for i in range(n_dep)])

    def swap(v):
        return lax.ppermute(v, "dp", [(0, 1), (1, 0)])

    def xdep(v, k):
        return lax.ppermute(v, "depth", [(i, i // 4 * 4 + (i + k) % 4) for i in range(n_dep)])

    def ydep(v, k):
        return lax.ppermute(v, "depth", [(i, (i + 4 * k) % n_dep) for i in range(n_dep)])

    own_w = weights[0]
    bias16 = jnp.broadcast_to(biases, (16, C))
    own_half = jnp.concatenate([lax.dynamic_slice_in_dim(own_w, c * HALF, HALF, 0), bias16], axis=0)
    got = [sec(own_half, k) for k in (1, 2, 3)]

    def window(v, ext):
        padded = jnp.pad(v, ((0, 0), (ext, ext), (0, 0), (0, 0)))
        return lax.dynamic_slice_in_dim(padded, s * R, R + 2 * ext, 1)

    h0 = window(volume[0], 8)
    h0_lo, h0_hi = dep(h0, 1), dep(h0, -1)
    cot = window(cotangent[0], 4)
    swapped = [swap(g) for g in got]

    def gather_weights(idx, own, b16, g1, g2, g3, s1, s2, s3, wall, ball, sem):
        s_, c_ = idx[0], idx[2]
        mine = pl.multiple_of(c_ * HALF, 16)
        other = pl.multiple_of((1 - c_) * HALF, 16)
        copies = [
            pltpu.make_async_copy(own, wall.at[s_], sem.at[0]),
            pltpu.make_async_copy(b16, ball.at[s_], sem.at[1]),
        ]
        for k, (g, o) in enumerate(((g1, s1), (g2, s2), (g3, s3)), 1):
            t = (s_ + 4 - k) % 4
            copies += [
                pltpu.make_async_copy(g.at[pl.ds(0, HALF)], wall.at[t, pl.ds(mine, HALF)], sem.at[3 * k - 1]),
                pltpu.make_async_copy(o.at[pl.ds(0, HALF)], wall.at[t, pl.ds(other, HALF)], sem.at[3 * k]),
                pltpu.make_async_copy(g.at[pl.ds(HALF, 16)], ball.at[t], sem.at[3 * k + 1]),
            ]
        for cp in copies:
            cp.start()
        for cp in copies:
            cp.wait()

    wall, ball = call(
        gather_weights,
        "gather_weights",
        (sds((4, TAP, C)), sds((4, 16, C))),
        [SMEM] + [ANY] * 8,
        [pltpu.SemaphoreType.DMA((11,))],
        (ANY, ANY),
    )(idx, own_w, bias16, *got, *swapped)
    wall = wall.reshape(4, 27, C, C)

    def w_block(i):
        return pl.BlockSpec((2, 27, C, C), lambda _: (i, 0, 0, 0))

    def k1(idx, own, lo, hi, w, bias, h0e, pre0, h1e, pre1, h2, x, h1):
        s_, d_ = idx[0], idx[1]
        assemble(x, lo, own, hi, d_, last)
        h0e[...] = x[1:5, 8 : 8 + R]
        wide = column(w, 0)
        b0 = bias[0, 0:1].astype(F32)

        def one(p, _):
            pre = conv_plane(x, p, wide, R + 14) + b0
            h = jnp.where(inside(R + 14, W, C, s_ * R - 7, H, 2 * d_ - 1 + p, D), pre * jax.nn.sigmoid(pre), 0.0)
            h = h.astype(BF).reshape(R + 14, W, C)
            h1[p] = h
            h1e[p] = h[7 : 7 + R]
            pre0[p] = pre[6 * W : (16 + 0) * W].astype(BF).reshape(R + 2, W, C)
            return 0

        lax.fori_loop(0, 4, one, 0)
        wide1 = column(w, 1)
        b1 = bias[1, 0:1].astype(F32)

        def two(p, _):
            pre = conv_plane(h1, p, wide1, R + 12) + b1
            h = jnp.where(inside(R + 12, W, C, s_ * R - 6, H, 2 * d_ + p, D), pre * jax.nn.sigmoid(pre), 0.0)
            h2[p] = h.astype(BF).reshape(R + 12, W, C)
            pre1[p] = pre[4 * W : 16 * W].astype(BF).reshape(R + 4, W, C)
            return 0

        lax.fori_loop(0, 2, two, 0)

    h0e, pre0, h1e, pre1, h2 = call(
        k1,
        "layers01",
        (
            sds((4, R, W, C)),
            sds((4, R + 2, W, C)),
            sds((4, R, W, C)),
            sds((2, R + 4, W, C)),
            sds((2, R + 12, W, C)),
        ),
        [SMEM, VMEM, VMEM, VMEM, w_block(0), VMEM],
        [pltpu.VMEM((6, R + 16, W, C), BF), pltpu.VMEM((4, R + 14, W, C), BF)],
    )(idx, h0, h0_lo, h0_hi, wall, ball)

    h2_lo, h2_hi = dep(h2, 1), dep(h2, -1)

    def turn(w, out):
        for j in range(27):
            out[0, j] = w[0, 26 - j].T

    wturn = pl.pallas_call(
        turn,
        name="turn_weights",
        grid=(4,),
        out_shape=sds((4, 27, C, C)),
        in_specs=[pl.BlockSpec((1, 27, C, C), lambda t: (t, 0, 0, 0))],
        out_specs=pl.BlockSpec((1, 27, C, C), lambda t: (t, 0, 0, 0)),
    )(wall)

    def k2(idx, own, lo, hi, w, bias, cot, h2e, pre2, h3e, h4, d3, x, h3):
        s_, d_ = idx[0], idx[1]
        assemble(x, lo, own, hi, d_, last)
        h2e[...] = x[1:5, 6 : 6 + R]
        wide = column(w, 0)
        b0 = bias[2, 0:1].astype(F32)

        def one(p, _):
            pre = conv_plane(x, p, wide, R + 10) + b0
            h = jnp.where(inside(R + 10, W, C, s_ * R - 5, H, 2 * d_ - 1 + p, D), pre * jax.nn.sigmoid(pre), 0.0)
            h = h.astype(BF).reshape(R + 10, W, C)
            h3[p] = h
            h3e[p] = h[5 : 5 + R]
            pre2[p] = pre[2 * W : 16 * W].astype(BF).reshape(R + 6, W, C)
            return 0

        lax.fori_loop(0, 4, one, 0)
        wide1 = column(w, 1)
        b1 = bias[3, 0:1].astype(F32)

        def two(p, _):
            pre = conv_plane(h3, p, wide1, R + 8) + b1
            h = (pre * jax.nn.sigmoid(pre)).astype(BF).reshape(R + 8, W, C)
            h4[p] = h[4 : 4 + R]
            g = cot[p].reshape((R + 8) * W, C).astype(F32)
            dl = g * slope(pre.astype(BF).astype(F32))
            dl = jnp.where(inside(R + 8, W, C, s_ * R - 4, H, 2 * d_ + p, D), dl, 0.0)
            d3[p] = dl.astype(BF).reshape(R + 8, W, C)
            return 0

        lax.fori_loop(0, 2, two, 0)

    h2e, pre2, h3e, h4, d3 = call(
        k2,
        "layers23",
        (
            sds((4, R, W, C)),
            sds((4, R + 6, W, C)),
            sds((4, R, W, C)),
            sds((2, R, W, C)),
            sds((2, R + 8, W, C)),
        ),
        [SMEM, VMEM, VMEM, VMEM, w_block(1), VMEM, VMEM],
        [pltpu.VMEM((6, R + 12, W, C), BF), pltpu.VMEM((4, R + 10, W, C), BF)],
    )(idx, h2, h2_lo, h2_hi, wall, ball, cot)

    d3_lo, d3_hi = dep(d3, 1), dep(d3, -1)

    def pick(values, k):
        t = (s + k) % 4
        return jnp.where(t == 0, values[0], jnp.where(t == 1, values[1], jnp.where(t == 2, values[2], values[3])))

    ins = [h0e, h1e, h2e, h3e]
    outs = [h1e[1:3], h2e[1:3], h3e[1:3], h4]
    in_own, out_own = pick(ins, 0), pick(outs, 0)
    in_got = [sec(pick(ins, k), k) for k in (1, 2, 3)]
    out_got = [sec(pick(outs, k), k) for k in (1, 2, 3)]

    def backward_pair(e0, final_delta):
        n1, n2 = R + 2 * e0 - 2, R + 2 * e0 - 4

        def body(idx, own, lo, hi, w, pre_a, *rest):
            if final_delta:
                pre_b, ga, da, gb, db, x, dbuf = rest
            else:
                ga, da, gb, x, dbuf = rest
            s_, d_ = idx[0], idx[1]
            assemble(x, lo, own, hi, d_, last)
            wide = column(w, 1)

            def one(p, _):
                g = conv_plane(x, p, wide, n1).astype(BF)
                dl = g.astype(F32) * slope(pre_a[p].reshape(n1 * W, C).astype(F32))
                dl = jnp.where(inside(n1, W, C, s_ * R - e0 + 1, H, 2 * d_ - 1 + p, D), dl, 0.0)
                dl = dl.astype(BF).reshape(n1, W, C)
                dbuf[p] = dl
                gr = g.reshape(n1, W, C)

                @pl.when((p > 0) & (p < 3))
                def _():
                    ga[p - 1] = gr[e0 - 1 : e0 - 1 + R]
                    da[p - 1] = dl[e0 - 1 : e0 - 1 + R]

                return 0

            lax.fori_loop(0, 4, one, 0)
            wide1 = column(w, 0)

            def two(p, _):
                g = conv_plane(dbuf, p, wide1, n2).astype(BF)
                gr = g.reshape(n2, W, C)
                gb[p] = gr[e0 - 2 : e0 - 2 + R]
                if final_delta:
                    dl = g.astype(F32) * slope(pre_b[p].reshape(n2 * W, C).astype(F32))
                    dl = jnp.where(inside(n2, W, C, s_ * R - e0 + 2, H, 2 * d_ + p, D), dl, 0.0)
                    db[p] = dl.astype(BF).reshape(n2, W, C)
                return 0

            lax.fori_loop(0, 2, two, 0)

        piece = sds((2, R, W, C))
        out = (piece, piece, piece) + ((sds((2, n2, W, C)),) if final_delta else ())
        return call(
            body,
            "back32" if final_delta else "back10",
            out,
            [SMEM, VMEM, VMEM, VMEM, w_block(1 if final_delta else 0), VMEM] + ([VMEM] if final_delta else []),
            [pltpu.VMEM((6, R + 2 * e0, W, C), BF), pltpu.VMEM((4, n1, W, C), BF)],
        )

    g3, d2, g2, d1 = backward_pair(4, True)(idx, d3, d3_lo, d3_hi, wturn, pre2, pre1)
    d1_lo, d1_hi = dep(d1, 1), dep(d1, -1)
    g1, d0, g0 = backward_pair(2, False)(idx, d1, d1_lo, d1_hi, wturn, pre0)

    deltas = [d0, d1[:, 2 : 2 + R], d2, d3[:, 4 : 4 + R]]
    grads = [g0, g1, g2, g3]
    d_own = pick(deltas, 0)
    d_got = [sec(pick(deltas, k), k) for k in (1, 2, 3)]
    g_own = pick(grads, 0)
    g_got = [sec(pick(grads, k), k) for k in (1, 2, 3)]

    ROWS = TAP + C

    def kw(idx, x0, x1, x2, x3, e0, e1, e2, e3, out, x, dl, wide):
        s_ = idx[0]
        x[:, 0] = jnp.zeros((4, W, C), BF)
        x[:, H + 1] = jnp.zeros((4, W, C), BF)
        for k, (xs, es) in enumerate(((x0, e0), (x1, e1), (x2, e2), (x3, e3))):
            row = ((s_ + 4 - k) % 4) * R
            x[:, pl.ds(row + 1, R)] = xs[...]
            dl[:, pl.ds(row, R)] = es[...]
        acc_b = jnp.zeros((1, C), F32)
        m = H * W
        pos = lax.broadcasted_iota(jnp.int32, (m, C), 0) % W
        for p in range(2):
            v = dl[p].reshape(m, C).astype(F32)
            acc_b = acc_b + jnp.sum(v, axis=0, keepdims=True)
            wide[p, :, 0:C] = jnp.where(pos == W - 1, 0.0, pltpu.roll(v, m - 1, 0)).astype(BF)
            wide[p, :, C : 2 * C] = dl[p].reshape(m, C)
            wide[p, :, 2 * C :] = jnp.where(pos == 0, 0.0, pltpu.roll(v, 1, 0)).astype(BF)

        def one(k, _):
            a, b = k // 3, k % 3
            acc = jnp.zeros((C, 3 * C), F32)
            for p in range(2):
                acc = acc + lax.dot_general(
                    x[p + a, pl.ds(b, H)].reshape(m, C),
                    wide[p],
                    (((0,), (0,)), ((), ())),
                    preferred_element_type=F32,
                )
            for j in range(3):
                out[pl.ds(pl.multiple_of((3 * k + j) * C, C), C)] = acc[:, j * C : (j + 1) * C]
            return 0

        lax.fori_loop(0, 9, one, 0)
        first = lax.broadcasted_iota(jnp.int32, (C, C), 0) == 0
        out[TAP:] = jnp.where(first, jnp.broadcast_to(acc_b, (C, C)), 0.0)

    total = call(
        kw,
        "kernel_grad",
        sds((ROWS, C), F32),
        [SMEM] + [VMEM] * 8,
        [
            pltpu.VMEM((4, H + 2, W, C), BF),
            pltpu.VMEM((2, H, W, C), BF),
            pltpu.VMEM((2, H * W, 3 * C), BF),
        ],
        VMEM,
    )(idx, in_own, *in_got, d_own, *d_got)

    RH, RQ = ROWS // 2, ROWS // 8
    xi, yi = d % 4, d // 4
    half = lax.dynamic_slice_in_dim(total, c * RH, RH, 0)
    away = lax.dynamic_slice_in_dim(total, (1 - c) * RH, RH, 0).astype(BF)
    half = half + swap(away).astype(F32)
    low = half.astype(BF)

    def quarter(v, i):
        return lax.dynamic_slice_in_dim(v, (i % 4) * RQ, RQ, 0)

    xs = [xdep(quarter(low, xi + k), k) for k in (1, 2, 3)]
    q = quarter(half, xi)
    for v in xs:
        q = q + v.astype(F32)
    q = q.astype(BF)
    ys = [ydep(q, k) for k in (1, 2, 3)]

    def ordered(idx, q0, q1, q2, q3, out, buf):
        y = idx[1] // 4
        for k, r in enumerate((q0, q1, q2, q3)):
            buf[k] = r[...].astype(F32)
        acc = buf[y % 4]
        for j in range(1, 4):
            acc = acc + buf[(y + 4 - j) % 4]
        out[...] = acc.astype(BF)

    q = call(ordered, "ordered_sum", sds((RQ, C)), [SMEM] + [VMEM] * 4, [pltpu.VMEM((4, RQ, C), F32)], VMEM)(idx, q, *ys)
    qs = [q] + [xdep(q, k) for k in (1, 2, 3)]

    def join(idx, q0, q1, q2, q3, out):
        x = idx[1] % 4
        for k, r in enumerate((q0, q1, q2, q3)):
            out[(x + 4 - k) % 4] = r[...]

    half = call(join, "join", sds((4, RQ, C)), [SMEM] + [VMEM] * 4, [], VMEM)(idx, *qs)
    other = swap(half)

    def finish(idx, mine, theirs, w_out, b_out, buf):
        buf[idx[2]] = mine[...].reshape(RH, C)
        buf[1 - idx[2]] = theirs[...].reshape(RH, C)
        w_out[0:RH] = buf[0].astype(F32) * grad_scale
        w_out[RH:] = buf[1, 0 : TAP - RH].astype(F32) * grad_scale
        b_out[...] = buf[1, TAP - RH : TAP - RH + 8].astype(F32) * grad_scale

    w_grad, b_grad = call(
        finish,
        "finish",
        (sds((TAP, C), F32), sds((8, C), F32)),
        [SMEM, VMEM, VMEM],
        [pltpu.VMEM((2, RH, C), BF)],
    )(idx, half, other)

    def place(idx, a0, a1, a2, a3, b0, b1, b2, b3, oa, ob, sem):
        copies = []
        for k, (va, vb) in enumerate(((a0, b0), (a1, b1), (a2, b2), (a3, b3))):
            row = ((idx[0] + 4 - k) % 4) * R
            copies.append(pltpu.make_async_copy(va, oa.at[:, pl.ds(row, R)], sem.at[2 * k]))
            copies.append(pltpu.make_async_copy(vb, ob.at[:, pl.ds(row, R)], sem.at[2 * k + 1]))
        for cp in copies:
            cp.start()
        for cp in copies:
            cp.wait()

    full = sds((2, H, W, C))
    out_h, out_g = call(
        place, "place", (full, full), [SMEM] + [ANY] * 8, [pltpu.SemaphoreType.DMA((8,))], (ANY, ANY)
    )(idx, out_own, *out_got, g_own, *g_got)
    return out_h[None, None], out_g[None, None], w_grad[None], b_grad[0:1]


def solution(mesh):
    in_specs = (
        P("dp", "depth", None, None, None),
        P("section", None, None),
        P("section", None),
        P("dp", "depth", None, None, None),
    )
    out_specs = (
        P("section", "dp", "depth", None, None, None),
        P("section", "dp", "depth", None, None, None),
        P("section", None, None),
        P("section", None),
    )
    return jax.shard_map(shards, mesh=mesh, in_specs=in_specs, out_specs=out_specs, check_vma=False)
```

```python
import math

import jax
import jax.numpy as jnp
from jax import lax
from jax.experimental import pallas as pl
from jax.experimental.pallas import tpu as pltpu
from jax.sharding import PartitionSpec as P


BF = jnp.bfloat16
F32 = jnp.float32

SMEM = pl.BlockSpec(memory_space=pltpu.SMEM)
VMEM = pl.BlockSpec(memory_space=pltpu.VMEM)
ANY = pl.BlockSpec(memory_space=pl.ANY)


def sds(shape, dtype=BF):
    return jax.ShapeDtypeStruct(shape, dtype)


def call(body, out, n_any_or_specs, scratch, out_specs=None, vmem=20):
    return pl.pallas_call(
        body,
        grid=(1,),
        out_shape=out,
        in_specs=n_any_or_specs,
        out_specs=out_specs if out_specs is not None else jax.tree.map(lambda _: VMEM, out),
        scratch_shapes=scratch,
        compiler_params=pltpu.CompilerParams(vmem_limit_bytes=vmem * 1024 * 1024),
    )


def column(w_ref, t, C=128):
    return jnp.concatenate(
        [
            jnp.concatenate([w_ref[t, (3 * k + c) * C : (3 * k + c + 1) * C] for c in range(3)], axis=1)
            for k in range(9)
        ],
        axis=0,
    )


def conv_plane(x_ref, p, wide, nr):
    W, C = x_ref.shape[2], x_ref.shape[3]
    m = nr * W
    lhs = jnp.concatenate(
        [x_ref[p + a, b : b + nr].reshape(m, C) for a in range(3) for b in range(3)], axis=1
    )
    y = jnp.dot(lhs, wide, preferred_element_type=F32)
    x_pos = lax.broadcasted_iota(jnp.int32, (m, C), 0) % W
    left = jnp.where(x_pos == 0, 0.0, pltpu.roll(y[:, :C], 1, 0))
    right = jnp.where(x_pos == W - 1, 0.0, pltpu.roll(y[:, 2 * C :], m - 1, 0))
    return y[:, C : 2 * C] + left + right


def inside(nr, W, C, first_row, H, plane, D):
    row = first_row + lax.broadcasted_iota(jnp.int32, (nr * W, C), 0) // W
    return (row >= 0) & (row < H) & (plane >= 0) & (plane < D)


def slope(pre):
    q = jax.nn.sigmoid(pre)
    return q * (1.0 + pre * (1.0 - q))


def assemble(dst, lo, own, hi, d, last):
    zero = jnp.zeros(lo.shape, BF)
    dst[0:2] = jnp.where(d > 0, lo[...], zero)
    dst[2:4] = own[...]
    dst[4:6] = jnp.where(d < last, hi[...], zero)


def halves(s, c, t, own, got, swp, dst, sem, half):
    mine = pl.multiple_of(c * half, 16)
    other = pl.multiple_of((1 - c) * half, 16)
    k = (s + 4 - t) % 4

    def pair(first, second):
        return (
            pltpu.make_async_copy(first, dst.at[pl.ds(mine, half)], sem.at[0]),
            pltpu.make_async_copy(second, dst.at[pl.ds(other, half)], sem.at[1]),
        )

    def start():
        @pl.when(k == 0)
        def _():
            for cp in pair(own.at[pl.ds(mine, half)], own.at[pl.ds(other, half)]):
                cp.start()

        for i in range(3):

            @pl.when(k == i + 1)
            def _():
                for cp in pair(got[i].at[pl.ds(0, half)], swp[i].at[pl.ds(0, half)]):
                    cp.start()

    def wait():
        for cp in pair(own.at[pl.ds(mine, half)], own.at[pl.ds(other, half)]):
            cp.wait()

    return start, wait


def bias_of(s, t, own_bias, got_bias):
    k = (s + 4 - t) % 4
    row = own_bias[...].astype(F32)
    for i in range(3):
        row = jnp.where(k == i + 1, got_bias[i][0:1].astype(F32), row)
    return row


def shards(volume, weights, biases, cotangent):
    n_sec = lax.axis_size("section")
    n_dep = lax.axis_size("depth")
    n_dp = lax.axis_size("dp")
    s = lax.axis_index("section")
    d = lax.axis_index("depth")
    c = lax.axis_index("dp")
    assert n_sec == 4 and n_dep == 16 and n_dp == 2
    PL, H, W, C = volume.shape[1:]
    assert PL == 2
    R = H // n_sec
    D = PL * n_dep
    last = n_dep - 1
    grad_scale = 1.0 / math.sqrt(n_dp * D * H * W)
    idx = jnp.stack([s, d, c]).astype(jnp.int32)
    TAP = 27 * C
    HALF = TAP // 2
    HB = HALF + 16

    def sec(v, k):
        return lax.ppermute(v, "section", [(i, (i + k) % n_sec) for i in range(n_sec)])

    def dep(v, k):
        return lax.ppermute(v, "depth", [(i, (i + k) % n_dep) for i in range(n_dep)])

    def swap(v):
        return lax.ppermute(v, "dp", [(0, 1), (1, 0)])

    def xdep(v, k):
        return lax.ppermute(v, "depth", [(i, i // 4 * 4 + (i + k) % 4) for i in range(n_dep)])

    def ydep(v, k):
        return lax.ppermute(v, "depth", [(i, (i + 4 * k) % n_dep) for i in range(n_dep)])

    def window(v, ext):
        padded = jnp.pad(v, ((0, 0), (ext, ext), (0, 0), (0, 0)))
        return lax.dynamic_slice_in_dim(padded, s * R, R + 2 * ext, 1)

    h0 = window(volume[0], 8)
    h0_lo, h0_hi = dep(h0, 1), dep(h0, -1)

    own_w = weights[0]

    def prepare(idx, w, b, out):
        out[0:HALF] = w[idx[2]]
        out[HALF:] = jnp.broadcast_to(b[...], (16, C))

    own_half = call(prepare, sds((HB, C)), [SMEM, VMEM, VMEM], [], VMEM)(idx, own_w.reshape(2, HALF, C), biases)
    got = [sec(own_half, k) for k in (1, 3, 2)]
    got = [got[0], got[2], got[1]]
    swapped = [swap(g) for g in got]
    all_w = (own_w, *got, *swapped)
    W_SPECS = [ANY] * 7
    got_b = tuple(g[HALF:] for g in got)
    all_b = (biases, *got_b)

    cot = window(cotangent[0], 4)

    def turn(idx, own, g1, g2, g3, s1, s2, s3, out, buf, sem):
        steps = [
            halves(idx[0], idx[2], t, own, (g1, g2, g3), (s1, s2, s3), buf.at[t], sem.at[t], HALF) for t in range(4)
        ]
        for start, _ in steps:
            start()
        for t in (3, 2, 1, 0):
            steps[t][1]()

            def one(j, _):
                out[t, pl.ds(pl.multiple_of(j * C, C), C)] = buf[t, pl.ds(pl.multiple_of((26 - j) * C, C), C)].T
                return 0

            lax.fori_loop(0, 27, one, 0, unroll=3)

    def k1(idx, own, lo, hi, ow, g1, g2, g3, s1, s2, s3, ob, b1_, b2_, b3_, h0e, pre0, h1e, pre1, h2, x, h1, w, sem):
        s_, d_ = idx[0], idx[1]
        steps = [
            halves(s_, idx[2], t, ow, (g1, g2, g3), (s1, s2, s3), w.at[t], sem.at[t], HALF) for t in range(2)
        ]
        for start, _ in steps:
            start()
        assemble(x, lo, own, hi, d_, last)
        h0e[...] = x[1:5, 8 : 8 + R]
        steps[0][1]()
        wide = column(w, 0)
        b0 = bias_of(s_, 0, ob, (b1_, b2_, b3_))

        def one(p, _):
            pre = conv_plane(x, p, wide, R + 14) + b0
            h = jnp.where(inside(R + 14, W, C, s_ * R - 7, H, 2 * d_ - 1 + p, D), pre * jax.nn.sigmoid(pre), 0.0)
            h = h.astype(BF).reshape(R + 14, W, C)
            h1[p] = h
            h1e[p] = h[7 : 7 + R]
            pre0[p] = pre[6 * W : (16 + 0) * W].astype(BF).reshape(R + 2, W, C)
            return 0

        lax.fori_loop(0, 4, one, 0)
        steps[1][1]()
        wide1 = column(w, 1)
        b1 = bias_of(s_, 1, ob, (b1_, b2_, b3_))

        def two(p, _):
            pre = conv_plane(h1, p, wide1, R + 12) + b1
            h = jnp.where(inside(R + 12, W, C, s_ * R - 6, H, 2 * d_ + p, D), pre * jax.nn.sigmoid(pre), 0.0)
            h2[p] = h.astype(BF).reshape(R + 12, W, C)
            pre1[p] = pre[4 * W : 16 * W].astype(BF).reshape(R + 4, W, C)
            return 0

        lax.fori_loop(0, 2, two, 0)

    h0e, pre0, h1e, pre1, h2 = call(
        k1,
        (
            sds((4, R, W, C)),
            sds((4, R + 2, W, C)),
            sds((4, R, W, C)),
            sds((2, R + 4, W, C)),
            sds((2, R + 12, W, C)),
        ),
        [SMEM, VMEM, VMEM, VMEM] + W_SPECS + [VMEM] * 4,
        [
            pltpu.VMEM((6, R + 16, W, C), BF),
            pltpu.VMEM((4, R + 14, W, C), BF),
            pltpu.VMEM((2, TAP, C), BF),
            pltpu.SemaphoreType.DMA((2, 2)),
        ],
    )(idx, h0, h0_lo, h0_hi, *all_w, *all_b)

    h2_lo, h2_hi = dep(h2, 1), dep(h2, -1)

    wturn = call(
        turn, sds((4, TAP, C)), [SMEM] + W_SPECS, [pltpu.VMEM((4, TAP, C), BF), pltpu.SemaphoreType.DMA((4, 2))], VMEM
    )(idx, *all_w)
    h2_lo, h2_hi, wturn = lax.optimization_barrier((h2_lo, h2_hi, wturn))

    def k2(idx, own, lo, hi, ow, g1, g2, g3, s1, s2, s3, ob, b1_, b2_, b3_, cot, h2e, pre2, h3e, h4, d3, x, h3, w, sem):
        s_, d_ = idx[0], idx[1]
        steps = [
            halves(s_, idx[2], t + 2, ow, (g1, g2, g3), (s1, s2, s3), w.at[t], sem.at[t], HALF) for t in range(2)
        ]
        for start, _ in steps:
            start()
        assemble(x, lo, own, hi, d_, last)
        h2e[...] = x[1:5, 6 : 6 + R]
        steps[0][1]()
        wide = column(w, 0)
        b0 = bias_of(s_, 2, ob, (b1_, b2_, b3_))

        def one(p, _):
            pre = conv_plane(x, p, wide, R + 10) + b0
            h = jnp.where(inside(R + 10, W, C, s_ * R - 5, H, 2 * d_ - 1 + p, D), pre * jax.nn.sigmoid(pre), 0.0)
            h = h.astype(BF).reshape(R + 10, W, C)
            h3[p] = h
            h3e[p] = h[5 : 5 + R]
            pre2[p] = pre[2 * W : 16 * W].astype(BF).reshape(R + 6, W, C)
            return 0

        lax.fori_loop(0, 4, one, 0)
        steps[1][1]()
        wide1 = column(w, 1)
        b1 = bias_of(s_, 3, ob, (b1_, b2_, b3_))

        def two(p, _):
            pre = conv_plane(h3, p, wide1, R + 8) + b1
            h = (pre * jax.nn.sigmoid(pre)).astype(BF).reshape(R + 8, W, C)
            h4[p] = h[4 : 4 + R]
            g = cot[p].reshape((R + 8) * W, C).astype(F32)
            dl = g * slope(pre.astype(BF).astype(F32))
            dl = jnp.where(inside(R + 8, W, C, s_ * R - 4, H, 2 * d_ + p, D), dl, 0.0)
            d3[p] = dl.astype(BF).reshape(R + 8, W, C)
            return 0

        lax.fori_loop(0, 2, two, 0)

    h2e, pre2, h3e, h4, d3 = call(
        k2,
        (
            sds((4, R, W, C)),
            sds((4, R + 6, W, C)),
            sds((4, R, W, C)),
            sds((2, R, W, C)),
            sds((2, R + 8, W, C)),
        ),
        [SMEM, VMEM, VMEM, VMEM] + W_SPECS + [VMEM] * 5,
        [
            pltpu.VMEM((6, R + 12, W, C), BF),
            pltpu.VMEM((4, R + 10, W, C), BF),
            pltpu.VMEM((2, TAP, C), BF),
            pltpu.SemaphoreType.DMA((2, 2)),
        ],
    )(idx, h2, h2_lo, h2_hi, *all_w, *all_b, cot)

    d3_lo, d3_hi = dep(d3, 1), dep(d3, -1)

    def pack(idx, x0, x1, x2, x3, x4, own, a1, a2, a3):
        xs = (x0, x1, x2, x3)
        for k, out in enumerate((own, a1, a2, a3)):
            for t in range(4):

                @pl.when((idx[0] + k) % 4 == t)
                def _():
                    out[0:4] = xs[t][...]
                    out[4:6] = x4[...] if t == 3 else xs[t + 1][1:3]

    six = sds((6, R, W, C))
    h_own, *h_send = call(pack, (six,) * 4, [SMEM] + [VMEM] * 5, [])(idx, h0e, h1e, h2e, h3e, h4)
    h_got = [sec(h_send[k - 1], k) for k in (1, 2, 3)]

    def backward_pair(e0, final_delta):
        n1, n2 = R + 2 * e0 - 2, R + 2 * e0 - 4

        def body(idx, own, lo, hi, w, pre_a, *rest):
            if final_delta:
                pre_b, ga, da, gb, db, x, dbuf = rest
            else:
                d1_, d2_, d3_, g2_, g3_, *sends, ga, da, gb, x, dbuf = rest
            s_, d_ = idx[0], idx[1]
            assemble(x, lo, own, hi, d_, last)
            wide = column(w, 1)

            def one(p, _):
                g = conv_plane(x, p, wide, n1).astype(BF)
                dl = g.astype(F32) * slope(pre_a[p].reshape(n1 * W, C).astype(F32))
                dl = jnp.where(inside(n1, W, C, s_ * R - e0 + 1, H, 2 * d_ - 1 + p, D), dl, 0.0)
                dl = dl.astype(BF).reshape(n1, W, C)
                dbuf[p] = dl
                gr = g.reshape(n1, W, C)

                @pl.when((p > 0) & (p < 3))
                def _():
                    ga[p - 1] = gr[e0 - 1 : e0 - 1 + R]
                    da[p - 1] = dl[e0 - 1 : e0 - 1 + R]

                return 0

            lax.fori_loop(0, 4, one, 0)
            wide1 = column(w, 0)

            def two(p, _):
                g = conv_plane(dbuf, p, wide1, n2).astype(BF)
                gr = g.reshape(n2, W, C)
                gb[p] = gr[e0 - 2 : e0 - 2 + R]
                if final_delta:
                    dl = g.astype(F32) * slope(pre_b[p].reshape(n2 * W, C).astype(F32))
                    dl = jnp.where(inside(n2, W, C, s_ * R - e0 + 2, H, 2 * d_ + p, D), dl, 0.0)
                    db[p] = dl.astype(BF).reshape(n2, W, C)
                return 0

            lax.fori_loop(0, 2, two, 0)
            if not final_delta:
                ds = (da[...], d1_[:, 2 : 2 + R], d2_[...], d3_[:, 4 : 4 + R])
                gs = (gb[...], ga[...], g2_[...], g3_[...])
                for k in range(4):
                    for t in range(4):

                        @pl.when((s_ + k) % 4 == t)
                        def _():
                            sends[k][...] = ds[t]
                            sends[4 + k][...] = gs[t]

        piece = sds((2, R, W, C))
        out = (piece, piece, piece, sds((2, n2, W, C))) if final_delta else (piece,) * 8
        held = [] if final_delta else [pltpu.VMEM(piece.shape, BF)] * 3
        return call(
            body,
            out,
            [SMEM, VMEM, VMEM, VMEM, pl.BlockSpec((2, TAP, C), lambda _: (1 if final_delta else 0, 0, 0)), VMEM]
            + [VMEM] * (1 if final_delta else 5),
            held + [pltpu.VMEM((6, R + 2 * e0, W, C), BF), pltpu.VMEM((4, n1, W, C), BF)],
        )

    g3, d2, g2, d1 = backward_pair(4, True)(idx, d3, d3_lo, d3_hi, wturn, pre2, pre1)
    d1_lo, d1_hi = dep(d1, 1), dep(d1, -1)
    sends = backward_pair(2, False)(idx, d1, d1_lo, d1_hi, wturn, pre0, d1, d2, d3, g2, g3)
    d_got = [sec(sends[k], k) for k in (1, 2, 3)]
    g_got = [sec(sends[4 + k], k) for k in (1, 2, 3)]

    ROWS = TAP + C

    def kw(idx, x0, x1, x2, x3, e0, e1, e2, e3, keep, away, x, dl, wide, out):
        s_ = idx[0]
        x[:, 0] = jnp.zeros((4, W, C), BF)
        x[:, H + 1] = jnp.zeros((4, W, C), BF)
        for k, (xs, es) in enumerate(((x0, e0), (x1, e1), (x2, e2), (x3, e3))):
            row = ((s_ + 4 - k) % 4) * R
            x[:, pl.ds(row + 1, R)] = xs[0:4]
            dl[:, pl.ds(row, R)] = es[...]
        acc_b = jnp.zeros((1, C), F32)
        m = H * W
        pos = lax.broadcasted_iota(jnp.int32, (m, C), 0) % W
        for p in range(2):
            v = dl[p].reshape(m, C).astype(F32)
            acc_b = acc_b + jnp.sum(v, axis=0, keepdims=True)
            wide[p, :, 0:C] = jnp.where(pos == W - 1, 0.0, pltpu.roll(v, m - 1, 0)).astype(BF)
            wide[p, :, C : 2 * C] = dl[p].reshape(m, C)
            wide[p, :, 2 * C :] = jnp.where(pos == 0, 0.0, pltpu.roll(v, 1, 0)).astype(BF)

        def one(k, _):
            a, b = k // 3, k % 3
            acc = jnp.zeros((C, 3 * C), F32)
            for p in range(2):
                acc = acc + lax.dot_general(
                    x[p + a, pl.ds(b, H)].reshape(m, C),
                    wide[p],
                    (((0,), (0,)), ((), ())),
                    preferred_element_type=F32,
                )
            for j in range(3):
                out[3 * k + j] = acc[:, j * C : (j + 1) * C]
            return 0

        lax.fori_loop(0, 9, one, 0)
        first = lax.broadcasted_iota(jnp.int32, (C, C), 0) == 0
        out[27] = jnp.where(first, jnp.broadcast_to(acc_b, (C, C)), 0.0)
        keep[...] = out[pl.ds(idx[2] * 14, 14)].reshape(RH, C)
        away[...] = out[pl.ds((1 - idx[2]) * 14, 14)].reshape(RH, C).astype(BF)

    RH, RQ = ROWS // 2, ROWS // 8
    keep, away = call(
        kw,
        (sds((RH, C), F32), sds((RH, C))),
        [SMEM] + [VMEM] * 8,
        [
            pltpu.VMEM((4, H + 2, W, C), BF),
            pltpu.VMEM((2, H, W, C), BF),
            pltpu.VMEM((2, H * W, 3 * C), BF),
            pltpu.VMEM((28, C, C), F32),
        ],
    )(idx, h_own, *h_got, sends[0], *d_got)

    recv = swap(away)

    def split(idx, keep, recv, mine, q1, q2, q3, buf):
        x = idx[1] % 4
        buf[...] = keep[...].reshape(4, RQ, C) + recv[...].reshape(4, RQ, C).astype(F32)
        mine[...] = buf[x]
        for k, q in enumerate((q1, q2, q3), 1):
            q[...] = buf[(x + k) % 4].astype(BF)

    quart = sds((RQ, C))
    q, *qs = call(
        split, (sds((RQ, C), F32), quart, quart, quart), [SMEM, VMEM, VMEM], [pltpu.VMEM((4, RQ, C), F32)]
    )(idx, keep, recv)
    xs = [xdep(qs[k - 1], k) for k in (1, 2, 3)]
    for v in xs:
        q = q + v.astype(F32)
    q = q.astype(BF)
    ys = [ydep(q, k) for k in (1, 2, 3)]

    def ordered(idx, q0, q1, q2, q3, out, buf):
        y = idx[1] // 4
        for k, r in enumerate((q0, q1, q2, q3)):
            buf[k] = r[...].astype(F32)
        acc = buf[y % 4]
        for j in range(1, 4):
            acc = acc + buf[(y + 4 - j) % 4]
        out[...] = acc.astype(BF)

    q = call(ordered, sds((RQ, C)), [SMEM] + [VMEM] * 4, [pltpu.VMEM((4, RQ, C), F32)], VMEM)(idx, q, *ys)
    qs = [q] + [xdep(q, k) for k in (1, 2, 3)]

    def join(idx, q0, q1, q2, q3, out):
        x = idx[1] % 4
        for k, r in enumerate((q0, q1, q2, q3)):
            out[(x + 4 - k) % 4] = r[...]

    half = call(join, sds((4, RQ, C)), [SMEM] + [VMEM] * 4, [], VMEM)(idx, *qs)
    other = swap(half)

    def finish(idx, mine, theirs, w_out, b_out, buf):
        buf[idx[2]] = mine[...].reshape(RH, C)
        buf[1 - idx[2]] = theirs[...].reshape(RH, C)
        w_out[0:RH] = buf[0].astype(F32) * grad_scale
        w_out[RH:] = buf[1, 0 : TAP - RH].astype(F32) * grad_scale
        b_out[...] = buf[1, TAP - RH : TAP - RH + 8].astype(F32) * grad_scale

    w_grad, b_grad = call(
        finish, (sds((TAP, C), F32), sds((8, C), F32)), [SMEM, VMEM, VMEM], [pltpu.VMEM((2, RH, C), BF)]
    )(idx, half, other)

    def place(idx, a0, a1, a2, a3, b0, b1, b2, b3, oa, ob, sem):
        copies = []
        for k, (va, vb) in enumerate(((a0, b0), (a1, b1), (a2, b2), (a3, b3))):
            row = ((idx[0] + 4 - k) % 4) * R
            copies.append(pltpu.make_async_copy(va.at[4:6], oa.at[:, pl.ds(row, R)], sem.at[2 * k]))
            copies.append(pltpu.make_async_copy(vb, ob.at[:, pl.ds(row, R)], sem.at[2 * k + 1]))
        for cp in copies:
            cp.start()
        for cp in copies:
            cp.wait()

    full = sds((2, H, W, C))
    out_h, out_g = call(
        place, (full, full), [SMEM] + [ANY] * 8, [pltpu.SemaphoreType.DMA((8,))], (ANY, ANY)
    )(idx, h_own, *h_got, sends[4], *g_got)
    return out_h[None, None], out_g[None, None], w_grad[None], b_grad[0:1]


def solution(mesh):
    in_specs = (
        P("dp", "depth", None, None, None),
        P("section", None, None),
        P("section", None),
        P("dp", "depth", None, None, None),
    )
    out_specs = (
        P("section", "dp", "depth", None, None, None),
        P("section", "dp", "depth", None, None, None),
        P("section", None, None),
        P("section", None),
    )

    return jax.shard_map(shards, mesh=mesh, in_specs=in_specs, out_specs=out_specs, check_vma=False)
```

```python
import math

import jax
import jax.numpy as jnp
from jax import lax
from jax.experimental import pallas as pl
from jax.experimental.pallas import tpu as pltpu
from jax.sharding import PartitionSpec as P


BF = jnp.bfloat16
F32 = jnp.float32

SMEM = pl.BlockSpec(memory_space=pltpu.SMEM)
VMEM = pl.BlockSpec(memory_space=pltpu.VMEM)
ANY = pl.BlockSpec(memory_space=pl.ANY)
HBM = pl.BlockSpec(memory_space=pltpu.HBM)


def in_hbm(x):
    return pltpu.with_memory_space_constraint(x, pltpu.HBM)


def sds(shape, dtype=BF):
    return jax.ShapeDtypeStruct(shape, dtype)


def call(body, out, n_any_or_specs, scratch, out_specs=None, vmem=20):
    return pl.pallas_call(
        body,
        grid=(1,),
        out_shape=out,
        in_specs=n_any_or_specs,
        out_specs=out_specs if out_specs is not None else jax.tree.map(lambda _: VMEM, out),
        scratch_shapes=scratch,
        compiler_params=pltpu.CompilerParams(vmem_limit_bytes=vmem * 1024 * 1024),
    )


def column(w_ref, t, C=128):
    return jnp.concatenate(
        [
            jnp.concatenate([w_ref[t, (3 * k + c) * C : (3 * k + c + 1) * C] for c in range(3)], axis=1)
            for k in range(9)
        ],
        axis=0,
    )


def conv_plane(x_ref, p, wide, nr):
    W, C = x_ref.shape[2], x_ref.shape[3]
    m = nr * W
    lhs = jnp.concatenate(
        [x_ref[p + a, b : b + nr].reshape(m, C) for a in range(3) for b in range(3)], axis=1
    )
    y = jnp.dot(lhs, wide, preferred_element_type=F32)
    x_pos = lax.broadcasted_iota(jnp.int32, (m, C), 0) % W
    left = jnp.where(x_pos == 0, 0.0, pltpu.roll(y[:, :C], 1, 0))
    right = jnp.where(x_pos == W - 1, 0.0, pltpu.roll(y[:, 2 * C :], m - 1, 0))
    return y[:, C : 2 * C] + left + right


def inside(nr, W, C, first_row, H, plane, D):
    row = first_row + lax.broadcasted_iota(jnp.int32, (nr * W, C), 0) // W
    return (row >= 0) & (row < H) & (plane >= 0) & (plane < D)


def slope(pre):
    q = jax.nn.sigmoid(pre)
    return q * (1.0 + pre * (1.0 - q))


def assemble(dst, lo, own, hi, d, last):
    zero = jnp.zeros(lo.shape, BF)
    dst[0:2] = jnp.where(d > 0, lo[...], zero)
    dst[2:4] = own[...]
    dst[4:6] = jnp.where(d < last, hi[...], zero)


def halves(s, c, t, own, got, swp, dst, sem, half):
    mine = pl.multiple_of(c * half, 16)
    other = pl.multiple_of((1 - c) * half, 16)
    k = (s + 4 - t) % 4

    def pair(first, second):
        return (
            pltpu.make_async_copy(first, dst.at[pl.ds(mine, half)], sem.at[0]),
            pltpu.make_async_copy(second, dst.at[pl.ds(other, half)], sem.at[1]),
        )

    def start():
        @pl.when(k == 0)
        def _():
            for cp in pair(own.at[pl.ds(mine, half)], own.at[pl.ds(other, half)]):
                cp.start()

        for i in range(3):

            @pl.when(k == i + 1)
            def _():
                for cp in pair(got[i].at[pl.ds(0, half)], swp[i].at[pl.ds(0, half)]):
                    cp.start()

    def wait():
        for cp in pair(own.at[pl.ds(mine, half)], own.at[pl.ds(other, half)]):
            cp.wait()

    return start, wait


def bias_of(s, t, own_bias, got_bias):
    k = (s + 4 - t) % 4
    row = own_bias[0:1].astype(F32)
    for i in range(3):
        row = jnp.where(k == i + 1, got_bias[i][0:1].astype(F32), row)
    return row


def shards(volume, weights, biases, cotangent):
    n_sec = lax.axis_size("section")
    n_dep = lax.axis_size("depth")
    n_dp = lax.axis_size("dp")
    s = lax.axis_index("section")
    d = lax.axis_index("depth")
    c = lax.axis_index("dp")
    assert n_sec == 4 and n_dep == 16 and n_dp == 2
    PL, H, W, C = volume.shape[1:]
    assert PL == 2
    R = H // n_sec
    D = PL * n_dep
    last = n_dep - 1
    grad_scale = 1.0 / math.sqrt(n_dp * D * H * W)
    idx = jnp.stack([s, d, c]).astype(jnp.int32)
    TAP = 27 * C
    HALF = TAP // 2
    HB = HALF + 16

    def sec(v, k):
        return lax.ppermute(v, "section", [(i, (i + k) % n_sec) for i in range(n_sec)])

    def dep(v, k):
        return lax.ppermute(v, "depth", [(i, (i + k) % n_dep) for i in range(n_dep)])

    def swap(v):
        return lax.ppermute(v, "dp", [(0, 1), (1, 0)])

    def xdep(v, k):
        return lax.ppermute(v, "depth", [(i, i // 4 * 4 + (i + k) % 4) for i in range(n_dep)])

    def ydep(v, k):
        return lax.ppermute(v, "depth", [(i, (i + 4 * k) % n_dep) for i in range(n_dep)])

    own_w = weights[0]

    def prepare(vol, w, b, h0, half, pad, row, sem):
        s_, c_ = lax.axis_index("section"), lax.axis_index("dp")
        pull_w = pltpu.make_async_copy(w.at[c_], half.at[pl.ds(0, HALF)], sem.at[0])
        pull_v = pltpu.make_async_copy(vol, pad.at[:, pl.ds(8, H)], sem.at[1])
        pull_b = pltpu.make_async_copy(b, row, sem.at[2])
        pull_w.start()
        pull_v.start()
        pull_b.start()
        pad[:, 0:8] = jnp.zeros((PL, 8, W, C), BF)
        pad[:, H + 8 :] = jnp.zeros((PL, 8, W, C), BF)
        pull_b.wait()
        half[HALF:] = jnp.broadcast_to(row[...], (16, C))
        pull_v.wait()
        h0[...] = pad[:, pl.ds(s_ * R, R + 16)]
        pull_w.wait()

    h0, own_half = call(
        prepare,
        (sds((PL, R + 16, W, C)), sds((HB, C))),
        [HBM, HBM, HBM],
        [pltpu.VMEM((PL, H + 16, W, C), BF), pltpu.VMEM((1, C), BF), pltpu.SemaphoreType.DMA((3,))],
    )(in_hbm(volume[0]), in_hbm(own_w.reshape(2, HALF, C)), in_hbm(biases))
    h0_lo, h0_hi = dep(h0, 1), dep(h0, -1)

    near = [sec(own_half, k) for k in (1, 3)]
    got = [near[0], sec(own_half, 2), near[1]]
    swapped = [swap(g) for g in got]
    all_w = (own_w, *got, *swapped)
    W_SPECS = [HBM] + [ANY] * 6
    all_b = (own_half, *got)
    tail_rows = pl.BlockSpec((16, C), lambda _: (HALF // 16, 0))
    B_SPECS = [tail_rows] * 4

    def turn(idx, own, g1, g2, g3, s1, s2, s3, out, buf, sem):
        steps = [
            halves(idx[0], idx[2], t, own, (g1, g2, g3), (s1, s2, s3), buf.at[t], sem.at[t], HALF) for t in range(4)
        ]
        for start, _ in steps:
            start()
        for t in (3, 2, 1, 0):
            steps[t][1]()

            def one(j, _):
                out[t, pl.ds(pl.multiple_of(j * C, C), C)] = buf[t, pl.ds(pl.multiple_of((26 - j) * C, C), C)].T
                return 0

            lax.fori_loop(0, 27, one, 0, unroll=3)

    def k1(idx, own, lo, hi, ow, g1, g2, g3, s1, s2, s3, ob, b1_, b2_, b3_, h0e, pre0, h1e, pre1, h2, x, h1, w, sem):
        s_, d_ = idx[0], idx[1]
        steps = [
            halves(s_, idx[2], t, ow, (g1, g2, g3), (s1, s2, s3), w.at[t], sem.at[t], HALF) for t in range(2)
        ]
        for start, _ in steps:
            start()
        assemble(x, lo, own, hi, d_, last)
        h0e[...] = x[1:5, 8 : 8 + R]
        steps[0][1]()
        b0 = bias_of(s_, 0, ob, (b1_, b2_, b3_))

        def one(p, _):
            pre = conv_plane(x, p, column(w, 0), R + 14) + b0
            h = jnp.where(inside(R + 14, W, C, s_ * R - 7, H, 2 * d_ - 1 + p, D), pre * jax.nn.sigmoid(pre), 0.0)
            h = h.astype(BF).reshape(R + 14, W, C)
            h1[p] = h
            h1e[p] = h[7 : 7 + R]
            pre0[p] = pre[6 * W : (16 + 0) * W].astype(BF).reshape(R + 2, W, C)
            return 0

        lax.fori_loop(0, 4, one, 0)
        steps[1][1]()
        b1 = bias_of(s_, 1, ob, (b1_, b2_, b3_))

        def two(p, _):
            pre = conv_plane(h1, p, column(w, 1), R + 12) + b1
            h = jnp.where(inside(R + 12, W, C, s_ * R - 6, H, 2 * d_ + p, D), pre * jax.nn.sigmoid(pre), 0.0)
            h2[p] = h.astype(BF).reshape(R + 12, W, C)
            pre1[p] = pre[4 * W : 16 * W].astype(BF).reshape(R + 4, W, C)
            return 0

        lax.fori_loop(0, 2, two, 0)

    h0e, pre0, h1e, pre1, h2 = call(
        k1,
        (
            sds((4, R, W, C)),
            sds((4, R + 2, W, C)),
            sds((4, R, W, C)),
            sds((2, R + 4, W, C)),
            sds((2, R + 12, W, C)),
        ),
        [SMEM, VMEM, VMEM, VMEM] + W_SPECS + B_SPECS,
        [
            pltpu.VMEM((6, R + 16, W, C), BF),
            pltpu.VMEM((4, R + 14, W, C), BF),
            pltpu.VMEM((2, TAP, C), BF),
            pltpu.SemaphoreType.DMA((2, 2)),
        ],
    )(idx, h0, h0_lo, h0_hi, *all_w, *all_b)

    h2_lo, h2_hi = dep(h2, 1), dep(h2, -1)

    wturn = call(
        turn, sds((4, TAP, C)), [SMEM] + W_SPECS, [pltpu.VMEM((4, TAP, C), BF), pltpu.SemaphoreType.DMA((4, 2))], VMEM
    )(idx, *all_w)
    h2_lo, h2_hi, wturn = lax.optimization_barrier((h2_lo, h2_hi, wturn))

    def k2(idx, own, lo, hi, ow, g1, g2, g3, s1, s2, s3, ob, b1_, b2_, b3_, cot, h2e, pre2, h3e, h4, d3, x, h3, w, gpad, sem):
        s_, d_ = idx[0], idx[1]
        steps = [
            halves(s_, idx[2], t + 2, ow, (g1, g2, g3), (s1, s2, s3), w.at[t], sem.at[t], HALF) for t in range(2)
        ]
        for start, _ in steps:
            start()
        assemble(x, lo, own, hi, d_, last)
        h2e[...] = x[1:5, 6 : 6 + R]
        gpad[:, 4 : 4 + H] = cot[...]
        steps[0][1]()
        b0 = bias_of(s_, 2, ob, (b1_, b2_, b3_))

        def one(p, _):
            pre = conv_plane(x, p, column(w, 0), R + 10) + b0
            h = jnp.where(inside(R + 10, W, C, s_ * R - 5, H, 2 * d_ - 1 + p, D), pre * jax.nn.sigmoid(pre), 0.0)
            h = h.astype(BF).reshape(R + 10, W, C)
            h3[p] = h
            h3e[p] = h[5 : 5 + R]
            pre2[p] = pre[2 * W : 16 * W].astype(BF).reshape(R + 6, W, C)
            return 0

        lax.fori_loop(0, 4, one, 0)
        steps[1][1]()
        b1 = bias_of(s_, 3, ob, (b1_, b2_, b3_))

        def two(p, _):
            pre = conv_plane(h3, p, column(w, 1), R + 8) + b1
            h = (pre * jax.nn.sigmoid(pre)).astype(BF).reshape(R + 8, W, C)
            h4[p] = h[4 : 4 + R]
            g = gpad[p, pl.ds(s_ * R, R + 8)].reshape((R + 8) * W, C).astype(F32)
            dl = g * slope(pre.astype(BF).astype(F32))
            dl = jnp.where(inside(R + 8, W, C, s_ * R - 4, H, 2 * d_ + p, D), dl, 0.0)
            d3[p] = dl.astype(BF).reshape(R + 8, W, C)
            return 0

        lax.fori_loop(0, 2, two, 0)

    h2e, pre2, h3e, h4, d3 = call(
        k2,
        (
            sds((4, R, W, C)),
            sds((4, R + 6, W, C)),
            sds((4, R, W, C)),
            sds((2, R, W, C)),
            sds((2, R + 8, W, C)),
        ),
        [SMEM, VMEM, VMEM, VMEM] + W_SPECS + B_SPECS + [VMEM],
        [
            pltpu.VMEM((6, R + 12, W, C), BF),
            pltpu.VMEM((4, R + 10, W, C), BF),
            pltpu.VMEM((2, TAP, C), BF),
            pltpu.VMEM((PL, H + 8, W, C), BF),
            pltpu.SemaphoreType.DMA((2, 2)),
        ],
    )(idx, h2, h2_lo, h2_hi, *all_w, *all_b, cotangent[0])

    d3_lo, d3_hi = dep(d3, 1), dep(d3, -1)

    def pack(idx, x0, x1, x2, x3, x4, own, a1, a2, a3):
        xs = (x0, x1, x2, x3)
        for k, out in enumerate((own, a1, a2, a3)):
            for t in range(4):

                @pl.when((idx[0] + k) % 4 == t)
                def _():
                    out[0:4] = xs[t][...]
                    out[4:6] = x4[...] if t == 3 else xs[t + 1][1:3]

    six = sds((6, R, W, C))
    h_own, *h_send = call(pack, (six,) * 4, [SMEM] + [VMEM] * 5, [])(idx, h0e, h1e, h2e, h3e, h4)
    h_got = [sec(h_send[k - 1], k) for k in (1, 2, 3)]

    def wturn_of(t):
        return pl.BlockSpec((1, TAP, C), lambda _: (t, 0, 0))

    piece = sds((2, R, W, C))

    def delta_of(g, pre, p, n, first_row, plane):
        dl = g.astype(F32) * slope(pre[p].reshape(n * W, C).astype(F32))
        dl = jnp.where(inside(n, W, C, first_row, H, plane, D), dl, 0.0)
        return dl.astype(BF).reshape(n, W, C)

    def send_all(s_, outs, values):
        for k in range(4):
            for t in range(4):

                @pl.when((s_ + k) % 4 == t)
                def _():
                    outs[k][...] = values[t]()

    def k3(idx, own, lo, hi, wa, wb, pre_a, pre_b, ga, da, gb, db, x, dbuf):
        s_, d_ = idx[0], idx[1]
        assemble(x, lo, own, hi, d_, last)

        def one(p, _):
            g = conv_plane(x, p, column(wa, 0), R + 6).astype(BF)
            dl = delta_of(g, pre_a, p, R + 6, s_ * R - 3, 2 * d_ - 1 + p)
            dbuf[p] = dl

            @pl.when((p > 0) & (p < 3))
            def _():
                ga[p - 1] = g.reshape(R + 6, W, C)[3 : 3 + R]
                da[p - 1] = dl[3 : 3 + R]

            return 0

        lax.fori_loop(0, 4, one, 0)

        def two(p, _):
            g = conv_plane(dbuf, p, column(wb, 0), R + 4).astype(BF)
            gb[p] = g.reshape(R + 4, W, C)[2 : 2 + R]
            db[p] = delta_of(g, pre_b, p, R + 4, s_ * R - 2, 2 * d_ + p)
            return 0

        lax.fori_loop(0, 2, two, 0)

    g3, d2, g2, d1 = call(
        k3,
        (piece, piece, piece, sds((2, R + 4, W, C))),
        [SMEM, VMEM, VMEM, VMEM, wturn_of(3), wturn_of(2), VMEM, VMEM],
        [pltpu.VMEM((6, R + 8, W, C), BF), pltpu.VMEM((4, R + 6, W, C), BF)],
    )(idx, d3, d3_lo, d3_hi, wturn, wturn, pre2, pre1)
    d1_lo, d1_hi = dep(d1, 1), dep(d1, -1)

    def k4a(idx, own, lo, hi, wa, pre_a, e1, e2, e3, g1, dbuf, *rest):
        *sends, x = rest
        s_, d_ = idx[0], idx[1]
        assemble(x, lo, own, hi, d_, last)

        def one(p, _):
            g = conv_plane(x, p, column(wa, 0), R + 2).astype(BF)
            dbuf[p] = delta_of(g, pre_a, p, R + 2, s_ * R - 1, 2 * d_ - 1 + p)

            @pl.when((p > 0) & (p < 3))
            def _():
                g1[p - 1] = g.reshape(R + 2, W, C)[1 : 1 + R]

            return 0

        lax.fori_loop(0, 4, one, 0)
        send_all(
            s_,
            sends,
            (
                lambda: dbuf[1:3, 1 : 1 + R],
                lambda: e1[:, 2 : 2 + R],
                lambda: e2[...],
                lambda: e3[:, 4 : 4 + R],
            ),
        )

    g1, d0, *d_send = call(
        k4a,
        (piece, sds((4, R + 2, W, C))) + (piece,) * 4,
        [SMEM, VMEM, VMEM, VMEM, wturn_of(1), VMEM, VMEM, VMEM, VMEM],
        [pltpu.VMEM((6, R + 4, W, C), BF)],
    )(idx, d1, d1_lo, d1_hi, wturn, pre0, d1, d2, d3)
    d_got = [sec(d_send[k], k) for k in (1, 3, 2)]
    d_got = [d_got[0], d_got[2], d_got[1]]

    def k4b(idx, dbuf, wb, g1, g2, g3, *rest):
        *sends, g0 = rest

        def two(p, _):
            g0[p] = conv_plane(dbuf, p, column(wb, 0), R).astype(BF).reshape(R, W, C)
            return 0

        lax.fori_loop(0, 2, two, 0)
        send_all(idx[0], sends, (lambda: g0[...], lambda: g1[...], lambda: g2[...], lambda: g3[...]))

    g_send = call(
        k4b, (piece,) * 4, [SMEM, VMEM, wturn_of(0), VMEM, VMEM, VMEM], [pltpu.VMEM(piece.shape, BF)]
    )(idx, d0, wturn, g1, g2, g3)
    g_got = []
    for k in (1, 2, 3):
        g_got.append(sec(g_send[k], k))

    def kx(idx, x0, x1, x2, x3, x):
        x[:, 0] = jnp.zeros((4, W, C), BF)
        x[:, H + 1] = jnp.zeros((4, W, C), BF)
        for k, xs in enumerate((x0, x1, x2, x3)):
            x[:, pl.ds(((idx[0] + 4 - k) % 4) * R + 1, R)] = xs[0:4]

    x_all = call(kx, sds((4, H + 2, W, C)), [SMEM] + [VMEM] * 4, [], VMEM)(idx, h_own, *h_got)

    ROWS = TAP + C

    def kw(idx, x, e0, e1, e2, e3, keep, away, dl, wide, out):
        s_ = idx[0]
        for k, es in enumerate((e0, e1, e2, e3)):
            dl[:, pl.ds(((s_ + 4 - k) % 4) * R, R)] = es[...]
        m = 4 * W
        pos = lax.broadcasted_iota(jnp.int32, (m, C), 0) % W

        def spread(i, acc):
            for p in range(2):
                v16 = dl[p, pl.ds(i * 4, 4)].reshape(m, C)
                v = v16.astype(F32)
                at = pl.ds(pl.multiple_of(i * m, m), m)
                wide[p, at, 0:C] = jnp.where(pos == W - 1, 0.0, pltpu.roll(v, m - 1, 0)).astype(BF)
                wide[p, at, C : 2 * C] = v16
                wide[p, at, 2 * C :] = jnp.where(pos == 0, 0.0, pltpu.roll(v, 1, 0)).astype(BF)
                acc = acc + jnp.sum(v.reshape(m // 8, 8, C), axis=0)
            return acc

        acc_b = jnp.sum(lax.fori_loop(0, H // 4, spread, jnp.zeros((8, C), F32)), axis=0, keepdims=True)

        def one(a, _):
            acc = jnp.zeros((3 * C, 3 * C), F32)
            for p in range(2):
                lhs = jnp.concatenate([x[p + a, b : b + H].reshape(H * W, C) for b in range(3)], axis=1)
                acc = acc + lax.dot_general(
                    lhs, wide[p], (((0,), (0,)), ((), ())), preferred_element_type=F32
                )
            for b in range(3):
                for j in range(3):
                    out[9 * a + 3 * b + j] = acc[b * C : (b + 1) * C, j * C : (j + 1) * C]
            return 0

        lax.fori_loop(0, 3, one, 0)
        first = lax.broadcasted_iota(jnp.int32, (C, C), 0) == 0
        out[27] = jnp.where(first, jnp.broadcast_to(acc_b, (C, C)), 0.0)
        keep[...] = out[pl.ds(idx[2] * 14, 14)].reshape(RH, C)
        away[...] = out[pl.ds((1 - idx[2]) * 14, 14)].reshape(RH, C).astype(BF)

    RH, RQ = ROWS // 2, ROWS // 8
    keep, away = call(
        kw,
        (sds((RH, C), F32), sds((RH, C))),
        [SMEM] + [VMEM] * 5,
        [
            pltpu.VMEM((2, H, W, C), BF),
            pltpu.VMEM((2, H * W, 3 * C), BF),
            pltpu.VMEM((28, C, C), F32),
        ],
    )(idx, x_all, d_send[0], *d_got)

    recv = swap(away)

    def split(idx, keep, recv, mine, q1, q2, q3, buf):
        x = idx[1] % 4
        buf[...] = keep[...].reshape(4, RQ, C) + recv[...].reshape(4, RQ, C).astype(F32)
        mine[...] = buf[x]
        for k, q in enumerate((q1, q2, q3), 1):
            q[...] = buf[(x + k) % 4].astype(BF)

    quart = sds((RQ, C))
    q, *qs = call(
        split, (sds((RQ, C), F32), quart, quart, quart), [SMEM, VMEM, VMEM], [pltpu.VMEM((4, RQ, C), F32)]
    )(idx, keep, recv)
    xs = [xdep(qs[k - 1], k) for k in (1, 2, 3)]
    for v in xs:
        q = q + v.astype(F32)
    q = q.astype(BF)
    ys = [ydep(q, k) for k in (1, 2, 3)]

    def ordered(idx, q0, q1, q2, q3, out, buf):
        y = idx[1] // 4
        for k, r in enumerate((q0, q1, q2, q3)):
            buf[k] = r[...].astype(F32)
        acc = buf[y % 4]
        for j in range(1, 4):
            acc = acc + buf[(y + 4 - j) % 4]
        out[...] = acc.astype(BF)

    q = call(ordered, sds((RQ, C)), [SMEM] + [VMEM] * 4, [pltpu.VMEM((4, RQ, C), F32)], VMEM)(idx, q, *ys)
    qs = [q] + [xdep(q, k) for k in (1, 2, 3)]

    def join(idx, q0, q1, q2, q3, out):
        x = idx[1] % 4
        for k, r in enumerate((q0, q1, q2, q3)):
            out[(x + 4 - k) % 4] = r[...]

    half = call(join, sds((4, RQ, C)), [SMEM] + [VMEM] * 4, [], VMEM)(idx, *qs)
    other = swap(half)

    def place(idx, a0, a1, a2, a3, b0, b1, b2, b3, mine, oa, ob, w_out, buf, sem):
        copies = []
        for k, (va, vb) in enumerate(((a0, b0), (a1, b1), (a2, b2), (a3, b3))):
            row = ((idx[0] + 4 - k) % 4) * R
            copies.append(pltpu.make_async_copy(va.at[4:6], oa.at[:, pl.ds(row, R)], sem.at[2 * k]))
            copies.append(pltpu.make_async_copy(vb, ob.at[:, pl.ds(row, R)], sem.at[2 * k + 1]))
        for cp in copies:
            cp.start()
        buf[...] = mine[...].reshape(RH, C).astype(F32) * grad_scale
        for c_, n in ((0, RH), (1, TAP - RH)):

            @pl.when(idx[2] == c_)
            def _():
                cp = pltpu.make_async_copy(
                    buf.at[pl.ds(0, n)], w_out.at[pl.ds(c_ * RH, n)], sem.at[8]
                )
                cp.start()
                cp.wait()

        for cp in copies:
            cp.wait()

    full = sds((2, H, W, C))
    out_h, out_g, w_part = call(
        place,
        (full, full, sds((TAP, C), F32)),
        [SMEM] + [ANY] * 8 + [VMEM],
        [pltpu.VMEM((RH, C), F32), pltpu.SemaphoreType.DMA((9,))],
        (ANY, ANY, ANY),
    )(idx, h_own, *h_got, g_send[0], *g_got, half)

    def finish(idx, mine, theirs, w_in, w_out, b_out, buf, sem):
        parts = 4
        row = TAP - RH
        c_ = idx[2]
        step = RH // parts
        for i in range(parts):
            buf[i * step : (i + 1) * step] = theirs[...].reshape(RH, C)[i * step : (i + 1) * step].astype(F32) * grad_scale
            n = min(step, row - i * step)

            @pl.when(c_ == 1)
            def _():
                pltpu.make_async_copy(
                    buf.at[pl.ds(i * step, step)], w_out.at[pl.ds(i * step, step)], sem.at[i]
                ).start()

            @pl.when(c_ == 0)
            def _():
                pltpu.make_async_copy(
                    buf.at[pl.ds(i * step, n)], w_out.at[pl.ds(RH + i * step, n)], sem.at[i]
                ).start()

        own_b = mine[3, RQ - C : RQ - C + 8].astype(F32) * grad_scale
        b_out[...] = jnp.where(c_ == 1, own_b, buf[row : row + 8])[0:1]
        for i in range(parts):
            n = min(step, row - i * step)

            @pl.when(c_ == 1)
            def _():
                pltpu.make_async_copy(
                    buf.at[pl.ds(i * step, step)], w_out.at[pl.ds(i * step, step)], sem.at[i]
                ).wait()

            @pl.when(c_ == 0)
            def _():
                pltpu.make_async_copy(
                    buf.at[pl.ds(i * step, n)], w_out.at[pl.ds(RH + i * step, n)], sem.at[i]
                ).wait()

    w_grad, b_grad = pl.pallas_call(
        finish,
        name="finish",
        grid=(1,),
        out_shape=(sds((TAP, C), F32), sds((1, C), F32)),
        in_specs=[SMEM, VMEM, VMEM, ANY],
        out_specs=(ANY, VMEM),
        scratch_shapes=[pltpu.VMEM((RH, C), F32), pltpu.SemaphoreType.DMA((4,))],
        input_output_aliases={3: 0},
        compiler_params=pltpu.CompilerParams(vmem_limit_bytes=20 * 1024 * 1024),
    )(idx, half, other, w_part)
    return out_h[None, None], out_g[None, None], w_grad[None], b_grad


def solution(mesh):
    in_specs = (
        P("dp", "depth", None, None, None),
        P("section", None, None),
        P("section", None),
        P("dp", "depth", None, None, None),
    )
    out_specs = (
        P("section", "dp", "depth", None, None, None),
        P("section", "dp", "depth", None, None, None),
        P("section", None, None),
        P("section", None),
    )

    return jax.shard_map(shards, mesh=mesh, in_specs=in_specs, out_specs=out_specs, check_vma=False)
```

```python
import math

import jax
import jax.numpy as jnp
from jax import lax
from jax.experimental import pallas as pl
from jax.experimental.pallas import tpu as pltpu
from jax.sharding import PartitionSpec as P


BF = jnp.bfloat16
F32 = jnp.float32

SMEM = pl.BlockSpec(memory_space=pltpu.SMEM)
VMEM = pl.BlockSpec(memory_space=pltpu.VMEM)
ANY = pl.BlockSpec(memory_space=pl.ANY)
HBM = pl.BlockSpec(memory_space=pltpu.HBM)


def in_hbm(x):
    return pltpu.with_memory_space_constraint(x, pltpu.HBM)


def sds(shape, dtype=BF):
    return jax.ShapeDtypeStruct(shape, dtype)


def call(body, out, n_any_or_specs, scratch, out_specs=None, vmem=20):
    return pl.pallas_call(
        body,
        grid=(1,),
        out_shape=out,
        in_specs=n_any_or_specs,
        out_specs=out_specs if out_specs is not None else jax.tree.map(lambda _: VMEM, out),
        scratch_shapes=scratch,
        compiler_params=pltpu.CompilerParams(vmem_limit_bytes=vmem * 1024 * 1024),
    )


def column(w_ref, t, C=128):
    return jnp.concatenate(
        [
            jnp.concatenate([w_ref[t, (3 * k + c) * C : (3 * k + c + 1) * C] for c in range(3)], axis=1)
            for k in range(9)
        ],
        axis=0,
    )


def conv_plane(x_ref, p, wide, nr):
    W, C = x_ref.shape[2], x_ref.shape[3]
    m = nr * W
    lhs = jnp.concatenate(
        [x_ref[p + a, b : b + nr].reshape(m, C) for a in range(3) for b in range(3)], axis=1
    )
    y = jnp.dot(lhs, wide, preferred_element_type=F32)
    x_pos = lax.broadcasted_iota(jnp.int32, (m, C), 0) % W
    left = jnp.where(x_pos == 0, 0.0, pltpu.roll(y[:, :C], 1, 0))
    right = jnp.where(x_pos == W - 1, 0.0, pltpu.roll(y[:, 2 * C :], m - 1, 0))
    return y[:, C : 2 * C] + left + right


def inside(nr, W, C, first_row, H, plane, D):
    row = first_row + lax.broadcasted_iota(jnp.int32, (nr * W, C), 0) // W
    return (row >= 0) & (row < H) & (plane >= 0) & (plane < D)


def slope(pre):
    q = jax.nn.sigmoid(pre)
    return q * (1.0 + pre * (1.0 - q))


def assemble(dst, far, own, near, d, last):
    odd = d % 2
    zero = jnp.zeros(far.shape, BF)
    dst[pl.ds(4 * odd, 2)] = jnp.where((d > 0) & (d < last), far[...], zero)
    dst[2:4] = own[...]
    dst[pl.ds(4 - 4 * odd, 2)] = near[...]


def layer_copies(s, c, t, own, got, swp, dst, sem, rows):
    k = (s + 4 - t) % 4

    def four(parts):
        out = []
        for i, part in enumerate(parts):
            at = pl.multiple_of((2 * c + i if i < 2 else 2 * (1 - c) + i - 2) * rows, 16)
            out.append((part, at, i))
        return [
            pltpu.make_async_copy(own.at[pl.ds(at, rows)] if part is None else part.at[pl.ds(0, rows)], dst.at[pl.ds(at, rows)], sem.at[i])
            for part, at, i in out
        ]

    def start():
        @pl.when(k == 0)
        def _():
            for cp in four((None,) * 4):
                cp.start()

        for i in range(3):

            @pl.when(k == i + 1)
            def _():
                for cp in four((*got[2 * i : 2 * i + 2], *swp[2 * i : 2 * i + 2])):
                    cp.start()

    def wait():
        for cp in four((None,) * 4):
            cp.wait()

    return start, wait


def bias_of(s, t, own_bias, got_bias):
    k = (s + 4 - t) % 4
    row = own_bias[0:1].astype(F32)
    for i in range(3):
        row = jnp.where(k == i + 1, got_bias[i][0:1].astype(F32), row)
    return row


def shards(volume, weights, biases, cotangent):
    n_sec = lax.axis_size("section")
    n_dep = lax.axis_size("depth")
    n_dp = lax.axis_size("dp")
    s = lax.axis_index("section")
    d = lax.axis_index("depth")
    c = lax.axis_index("dp")
    assert n_sec == 4 and n_dep == 16 and n_dp == 2
    PL, H, W, C = volume.shape[1:]
    assert PL == 2
    R = H // n_sec
    D = PL * n_dep
    last = n_dep - 1
    grad_scale = 1.0 / math.sqrt(n_dp * D * H * W)
    idx = jnp.stack([s, d, c]).astype(jnp.int32)
    TAP = 27 * C
    HALF = TAP // 2
    QR = HALF // 2
    QB = QR + 16

    def sec(v, k):
        return lax.ppermute(v, "section", [(i, i ^ k) for i in range(n_sec)])

    def both(v):
        result = []
        for first in (1, 0):
            pairs = [(i, i + 1) for i in range(first, n_dep - 1, 2)]
            result.append(lax.ppermute(v, "depth", pairs + [(b, a) for a, b in pairs]))
        return result

    def swap(v):
        return lax.ppermute(v, "dp", [(0, 1), (1, 0)])

    def xdep(v, k):
        return lax.ppermute(v, "depth", [(i, i ^ k) for i in range(n_dep)])

    def ydep(v, k):
        return lax.ppermute(v, "depth", [(i, i ^ (4 * k)) for i in range(n_dep)])

    own_w = weights[0]

    def prepare(vol, w, b, h0, part_a, part_b, own_b, pad, row, sem):
        s_, c_ = lax.axis_index("section"), lax.axis_index("dp")
        pulls = [
            pltpu.make_async_copy(w.at[2 * c_], part_a.at[pl.ds(0, QR)], sem.at[0]),
            pltpu.make_async_copy(w.at[2 * c_ + 1], part_b.at[pl.ds(0, QR)], sem.at[1]),
            pltpu.make_async_copy(b, row, sem.at[2]),
            pltpu.make_async_copy(vol, pad.at[:, pl.ds(8, H)], sem.at[3]),
        ]
        for cp in pulls:
            cp.start()
        pad[:, 0:8] = jnp.zeros((PL, 8, W, C), BF)
        pad[:, H + 8 :] = jnp.zeros((PL, 8, W, C), BF)
        for cp in pulls:
            cp.wait()
        bias = jnp.broadcast_to(row[...], (16, C))
        part_a[QR:] = bias
        part_b[QR:] = bias
        own_b[...] = bias
        h0[...] = pad[:, pl.ds(s_ * R, R + 16)]

    h0, part_a, part_b, own_b = call(
        prepare,
        (sds((PL, R + 16, W, C)), sds((QB, C)), sds((QB, C)), sds((16, C))),
        [HBM, HBM, HBM],
        [pltpu.VMEM((PL, H + 16, W, C), BF), pltpu.VMEM((1, C), BF), pltpu.SemaphoreType.DMA((4,))],
    )(in_hbm(volume[0]), in_hbm(own_w.reshape(4, QR, C)), in_hbm(biases))
    h0_lo, h0_hi = both(h0)

    def ring(v, k):
        return lax.ppermute(v, "section", [(i, (i + k) % n_sec) for i in range(n_sec)])

    a1, b3 = ring(part_a, 1), ring(part_b, 3)
    b1, a3 = ring(part_b, 1), ring(part_a, 3)
    a2, b2 = ring(a1, 1), ring(b3, 3)
    got = (a1, b1, a2, b2, a3, b3)
    swapped = [swap(g) for g in got]
    all_w = (own_w, *got, *swapped)
    W_SPECS = [HBM] + [ANY] * 12
    all_b = (own_b, a1, a2, a3)
    tail_rows = pl.BlockSpec((16, C), lambda _: (QR // 16, 0))
    B_SPECS = [VMEM] + [tail_rows] * 3

    def turn(idx, own, *rest):
        got_, swp_, (out, buf, sem) = rest[:6], rest[6:12], rest[12:]
        steps = [
            layer_copies(idx[0], idx[2], t, own, got_, swp_, buf.at[t], sem.at[t], QR) for t in range(4)
        ]
        for start, _ in steps:
            start()
        for t in (3, 2, 1, 0):
            steps[t][1]()

            def one(j, _):
                out[t, pl.ds(pl.multiple_of(j * C, C), C)] = buf[t, pl.ds(pl.multiple_of((26 - j) * C, C), C)].T
                return 0

            lax.fori_loop(0, 27, one, 0, unroll=3)

    def k1(idx, own, lo, hi, ow, *rest):
        got_, swp_, rest = rest[:6], rest[6:12], rest[12:]
        ob, b1_, b2_, b3_, h0e, pre0, h1e, pre1, h2, x, h1, w, sem = rest
        s_, d_ = idx[0], idx[1]
        steps = [
            layer_copies(s_, idx[2], t, ow, got_, swp_, w.at[t], sem.at[t], QR) for t in range(2)
        ]
        for start, _ in steps:
            start()
        assemble(x, lo, own, hi, d_, last)
        h0e[...] = x[1:5, 8 : 8 + R]
        steps[0][1]()
        b0 = bias_of(s_, 0, ob, (b1_, b2_, b3_))

        def one(p, _):
            pre = conv_plane(x, p, column(w, 0), R + 14) + b0
            h = jnp.where(inside(R + 14, W, C, s_ * R - 7, H, 2 * d_ - 1 + p, D), pre * jax.nn.sigmoid(pre), 0.0)
            h = h.astype(BF).reshape(R + 14, W, C)
            h1[p] = h
            h1e[p] = h[7 : 7 + R]
            pre0[p] = pre[6 * W : (16 + 0) * W].astype(BF).reshape(R + 2, W, C)
            return 0

        lax.fori_loop(0, 4, one, 0)
        steps[1][1]()
        b1 = bias_of(s_, 1, ob, (b1_, b2_, b3_))

        def two(p, _):
            pre = conv_plane(h1, p, column(w, 1), R + 12) + b1
            h = jnp.where(inside(R + 12, W, C, s_ * R - 6, H, 2 * d_ + p, D), pre * jax.nn.sigmoid(pre), 0.0)
            h2[p] = h.astype(BF).reshape(R + 12, W, C)
            pre1[p] = pre[4 * W : 16 * W].astype(BF).reshape(R + 4, W, C)
            return 0

        lax.fori_loop(0, 2, two, 0)

    h0e, pre0, h1e, pre1, h2 = call(
        k1,
        (
            sds((4, R, W, C)),
            sds((4, R + 2, W, C)),
            sds((4, R, W, C)),
            sds((2, R + 4, W, C)),
            sds((2, R + 12, W, C)),
        ),
        [SMEM, VMEM, VMEM, VMEM] + W_SPECS + B_SPECS,
        [
            pltpu.VMEM((6, R + 16, W, C), BF),
            pltpu.VMEM((4, R + 14, W, C), BF),
            pltpu.VMEM((2, TAP, C), BF),
            pltpu.SemaphoreType.DMA((2, 4)),
        ],
    )(idx, h0, h0_lo, h0_hi, *all_w, *all_b)

    h2_lo, h2_hi = both(h2)

    wturn = call(
        turn, sds((4, TAP, C)), [SMEM] + W_SPECS, [pltpu.VMEM((4, TAP, C), BF), pltpu.SemaphoreType.DMA((4, 4))], VMEM
    )(idx, *all_w)
    h2_lo, h2_hi, wturn = lax.optimization_barrier((h2_lo, h2_hi, wturn))

    def k2(idx, own, lo, hi, ow, *rest):
        got_, swp_, rest = rest[:6], rest[6:12], rest[12:]
        ob, b1_, b2_, b3_, cot, h2e, pre2, h3e, h4, d3, x, h3, w, gpad, sem = rest
        s_, d_ = idx[0], idx[1]
        steps = [
            layer_copies(s_, idx[2], t + 2, ow, got_, swp_, w.at[t], sem.at[t], QR) for t in range(2)
        ]
        for start, _ in steps:
            start()
        assemble(x, lo, own, hi, d_, last)
        h2e[...] = x[1:5, 6 : 6 + R]
        gpad[:, 4 : 4 + H] = cot[...]
        steps[0][1]()
        b0 = bias_of(s_, 2, ob, (b1_, b2_, b3_))

        def one(p, _):
            pre = conv_plane(x, p, column(w, 0), R + 10) + b0
            h = jnp.where(inside(R + 10, W, C, s_ * R - 5, H, 2 * d_ - 1 + p, D), pre * jax.nn.sigmoid(pre), 0.0)
            h = h.astype(BF).reshape(R + 10, W, C)
            h3[p] = h
            h3e[p] = h[5 : 5 + R]
            pre2[p] = pre[2 * W : 16 * W].astype(BF).reshape(R + 6, W, C)
            return 0

        lax.fori_loop(0, 4, one, 0)
        steps[1][1]()
        b1 = bias_of(s_, 3, ob, (b1_, b2_, b3_))

        def two(p, _):
            pre = conv_plane(h3, p, column(w, 1), R + 8) + b1
            h = (pre * jax.nn.sigmoid(pre)).astype(BF).reshape(R + 8, W, C)
            h4[p] = h[4 : 4 + R]
            g = gpad[p, pl.ds(s_ * R, R + 8)].reshape((R + 8) * W, C).astype(F32)
            dl = g * slope(pre.astype(BF).astype(F32))
            dl = jnp.where(inside(R + 8, W, C, s_ * R - 4, H, 2 * d_ + p, D), dl, 0.0)
            d3[p] = dl.astype(BF).reshape(R + 8, W, C)
            return 0

        lax.fori_loop(0, 2, two, 0)

    h2e, pre2, h3e, h4, d3 = call(
        k2,
        (
            sds((4, R, W, C)),
            sds((4, R + 6, W, C)),
            sds((4, R, W, C)),
            sds((2, R, W, C)),
            sds((2, R + 8, W, C)),
        ),
        [SMEM, VMEM, VMEM, VMEM] + W_SPECS + B_SPECS + [VMEM],
        [
            pltpu.VMEM((6, R + 12, W, C), BF),
            pltpu.VMEM((4, R + 10, W, C), BF),
            pltpu.VMEM((2, TAP, C), BF),
            pltpu.VMEM((PL, H + 8, W, C), BF),
            pltpu.SemaphoreType.DMA((2, 4)),
        ],
    )(idx, h2, h2_lo, h2_hi, *all_w, *all_b, cotangent[0])

    d3_lo, d3_hi = both(d3)

    def pack(idx, x0, x1, x2, x3, x4, own, a1, a2, a3):
        xs = (x0, x1, x2, x3)
        for k, out in enumerate((own, a1, a2, a3)):
            for t in range(4):

                @pl.when((idx[0] ^ k) == t)
                def _():
                    out[0:4] = xs[t][...]
                    out[4:6] = x4[...] if t == 3 else xs[t + 1][1:3]

    six = sds((6, R, W, C))
    h_own, *h_send = call(pack, (six,) * 4, [SMEM] + [VMEM] * 5, [])(idx, h0e, h1e, h2e, h3e, h4)
    h_got = [sec(h_send[k - 1], k) for k in (1, 2, 3)]

    def wturn_of(t):
        return pl.BlockSpec((1, TAP, C), lambda _: (t, 0, 0))

    piece = sds((2, R, W, C))

    def delta_of(g, pre, p, n, first_row, plane):
        dl = g.astype(F32) * slope(pre[p].reshape(n * W, C).astype(F32))
        dl = jnp.where(inside(n, W, C, first_row, H, plane, D), dl, 0.0)
        return dl.astype(BF).reshape(n, W, C)

    def send_all(s_, outs, values):
        for k in range(4):
            for t in range(4):

                @pl.when((s_ ^ k) == t)
                def _():
                    outs[k][...] = values[t]()

    def k3(idx, own, lo, hi, wa, wb, pre_a, pre_b, ga, da, gb, db, x, dbuf):
        s_, d_ = idx[0], idx[1]
        assemble(x, lo, own, hi, d_, last)

        def one(p, _):
            g = conv_plane(x, p, column(wa, 0), R + 6).astype(BF)
            dl = delta_of(g, pre_a, p, R + 6, s_ * R - 3, 2 * d_ - 1 + p)
            dbuf[p] = dl

            @pl.when((p > 0) & (p < 3))
            def _():
                ga[p - 1] = g.reshape(R + 6, W, C)[3 : 3 + R]
                da[p - 1] = dl[3 : 3 + R]

            return 0

        lax.fori_loop(0, 4, one, 0)

        def two(p, _):
            g = conv_plane(dbuf, p, column(wb, 0), R + 4).astype(BF)
            gb[p] = g.reshape(R + 4, W, C)[2 : 2 + R]
            db[p] = delta_of(g, pre_b, p, R + 4, s_ * R - 2, 2 * d_ + p)
            return 0

        lax.fori_loop(0, 2, two, 0)

    g3, d2, g2, d1 = call(
        k3,
        (piece, piece, piece, sds((2, R + 4, W, C))),
        [SMEM, VMEM, VMEM, VMEM, wturn_of(3), wturn_of(2), VMEM, VMEM],
        [pltpu.VMEM((6, R + 8, W, C), BF), pltpu.VMEM((4, R + 6, W, C), BF)],
    )(idx, d3, d3_lo, d3_hi, wturn, wturn, pre2, pre1)
    d1_lo, d1_hi = both(d1)

    def k4a(idx, own, lo, hi, wa, pre_a, e1, e2, e3, g1, dbuf, *rest):
        *sends, x = rest
        s_, d_ = idx[0], idx[1]
        assemble(x, lo, own, hi, d_, last)

        def one(p, _):
            g = conv_plane(x, p, column(wa, 0), R + 2).astype(BF)
            dbuf[p] = delta_of(g, pre_a, p, R + 2, s_ * R - 1, 2 * d_ - 1 + p)

            @pl.when((p > 0) & (p < 3))
            def _():
                g1[p - 1] = g.reshape(R + 2, W, C)[1 : 1 + R]

            return 0

        lax.fori_loop(0, 4, one, 0)
        send_all(
            s_,
            sends,
            (
                lambda: dbuf[1:3, 1 : 1 + R],
                lambda: e1[:, 2 : 2 + R],
                lambda: e2[...],
                lambda: e3[:, 4 : 4 + R],
            ),
        )

    g1, d0, *d_send = call(
        k4a,
        (piece, sds((4, R + 2, W, C))) + (piece,) * 4,
        [SMEM, VMEM, VMEM, VMEM, wturn_of(1), VMEM, VMEM, VMEM, VMEM],
        [pltpu.VMEM((6, R + 4, W, C), BF)],
    )(idx, d1, d1_lo, d1_hi, wturn, pre0, d1, d2, d3)
    d_got = [sec(d_send[k], k) for k in (1, 3, 2)]
    d_got = [d_got[0], d_got[2], d_got[1]]

    def k4b(idx, dbuf, wb, g1, g2, g3, *rest):
        *sends, g0 = rest

        def two(p, _):
            g0[p] = conv_plane(dbuf, p, column(wb, 0), R).astype(BF).reshape(R, W, C)
            return 0

        lax.fori_loop(0, 2, two, 0)
        send_all(idx[0], sends, (lambda: g0[...], lambda: g1[...], lambda: g2[...], lambda: g3[...]))

    g_send = call(
        k4b, (piece,) * 4, [SMEM, VMEM, wturn_of(0), VMEM, VMEM, VMEM], [pltpu.VMEM(piece.shape, BF)]
    )(idx, d0, wturn, g1, g2, g3)
    g_got = []
    for k in (1, 2, 3):
        g_got.append(sec(g_send[k], k))

    def kx(idx, x0, x1, x2, x3, x):
        x[:, 0] = jnp.zeros((4, W, C), BF)
        x[:, H + 1] = jnp.zeros((4, W, C), BF)
        for k, xs in enumerate((x0, x1, x2, x3)):
            x[:, pl.ds((idx[0] ^ k) * R + 1, R)] = xs[0:4]

    x_all = call(kx, sds((4, H + 2, W, C)), [SMEM] + [VMEM] * 4, [], VMEM)(idx, h_own, *h_got)

    ROWS = TAP + C

    def kw(idx, x, e0, e1, e2, e3, keep, away, dl, wide, out):
        s_ = idx[0]
        for k, es in enumerate((e0, e1, e2, e3)):
            dl[:, pl.ds((s_ ^ k) * R, R)] = es[...]
        m = 4 * W
        pos = lax.broadcasted_iota(jnp.int32, (m, C), 0) % W

        def spread(i, acc):
            for p in range(2):
                v16 = dl[p, pl.ds(i * 4, 4)].reshape(m, C)
                v = v16.astype(F32)
                at = pl.ds(pl.multiple_of(i * m, m), m)
                wide[p, at, 0:C] = jnp.where(pos == W - 1, 0.0, pltpu.roll(v, m - 1, 0)).astype(BF)
                wide[p, at, C : 2 * C] = v16
                wide[p, at, 2 * C :] = jnp.where(pos == 0, 0.0, pltpu.roll(v, 1, 0)).astype(BF)
                acc = acc + jnp.sum(v.reshape(m // 8, 8, C), axis=0)
            return acc

        acc_b = jnp.sum(lax.fori_loop(0, H // 4, spread, jnp.zeros((8, C), F32)), axis=0, keepdims=True)

        def one(a, _):
            acc = jnp.zeros((3 * C, 3 * C), F32)
            for p in range(2):
                lhs = jnp.concatenate([x[p + a, b : b + H].reshape(H * W, C) for b in range(3)], axis=1)
                acc = acc + lax.dot_general(
                    lhs, wide[p], (((0,), (0,)), ((), ())), preferred_element_type=F32
                )
            for b in range(3):
                for j in range(3):
                    out[9 * a + 3 * b + j] = acc[b * C : (b + 1) * C, j * C : (j + 1) * C]
            return 0

        lax.fori_loop(0, 3, one, 0)
        first = lax.broadcasted_iota(jnp.int32, (C, C), 0) == 0
        out[27] = jnp.where(first, jnp.broadcast_to(acc_b, (C, C)), 0.0)
        keep[...] = out[pl.ds(idx[2] * 14, 14)].reshape(RH, C)
        away[...] = out[pl.ds((1 - idx[2]) * 14, 14)].reshape(RH, C).astype(BF)

    RH, RQ = ROWS // 2, ROWS // 8
    keep, away = call(
        kw,
        (sds((RH, C), F32), sds((RH, C))),
        [SMEM] + [VMEM] * 5,
        [
            pltpu.VMEM((2, H, W, C), BF),
            pltpu.VMEM((2, H * W, 3 * C), BF),
            pltpu.VMEM((28, C, C), F32),
        ],
    )(idx, x_all, d_send[0], *d_got)

    recv = swap(away)

    def split(idx, keep, recv, mine, q1, q2, q3, buf):
        x = idx[1] % 4
        buf[...] = keep[...].reshape(4, RQ, C) + recv[...].reshape(4, RQ, C).astype(F32)
        mine[...] = buf[x]
        for k, q in enumerate((q1, q2, q3), 1):
            q[...] = buf[x ^ k].astype(BF)

    quart = sds((RQ, C))
    q, *qs = call(
        split, (sds((RQ, C), F32), quart, quart, quart), [SMEM, VMEM, VMEM], [pltpu.VMEM((4, RQ, C), F32)]
    )(idx, keep, recv)
    xs = [xdep(qs[k - 1], k) for k in (1, 2, 3)]
    for v in xs:
        q = q + v.astype(F32)
    q = q.astype(BF)
    ys = [ydep(q, k) for k in (1, 2, 3)]

    def ordered(idx, q0, q1, q2, q3, out, buf):
        y = idx[1] // 4
        for k, r in enumerate((q0, q1, q2, q3)):
            buf[k] = r[...].astype(F32)
        acc = buf[y]
        for j in range(1, 4):
            acc = acc + buf[y ^ j]
        out[...] = acc.astype(BF)

    q = call(ordered, sds((RQ, C)), [SMEM] + [VMEM] * 4, [pltpu.VMEM((4, RQ, C), F32)], VMEM)(idx, q, *ys)
    qs = [q] + [xdep(q, k) for k in (1, 2, 3)]

    def join(idx, q0, q1, q2, q3, out):
        x = idx[1] % 4
        for k, r in enumerate((q0, q1, q2, q3)):
            out[x ^ k] = r[...]

    half = call(join, sds((4, RQ, C)), [SMEM] + [VMEM] * 4, [], VMEM)(idx, *qs)
    other = swap(half)

    def place(idx, a0, a1, a2, a3, b0, b1, b2, b3, mine, oa, ob, w_out, buf, sem):
        copies = []
        for k, (va, vb) in enumerate(((a0, b0), (a1, b1), (a2, b2), (a3, b3))):
            row = (idx[0] ^ k) * R
            copies.append(pltpu.make_async_copy(va.at[4:6], oa.at[:, pl.ds(row, R)], sem.at[2 * k]))
            copies.append(pltpu.make_async_copy(vb, ob.at[:, pl.ds(row, R)], sem.at[2 * k + 1]))
        for cp in copies:
            cp.start()
        buf[...] = mine[...].reshape(RH, C).astype(F32) * grad_scale
        for c_, n in ((0, RH), (1, TAP - RH)):

            @pl.when(idx[2] == c_)
            def _():
                cp = pltpu.make_async_copy(
                    buf.at[pl.ds(0, n)], w_out.at[pl.ds(c_ * RH, n)], sem.at[8]
                )
                cp.start()
                cp.wait()

        for cp in copies:
            cp.wait()

    full = sds((2, H, W, C))
    out_h, out_g, w_part = call(
        place,
        (full, full, sds((TAP, C), F32)),
        [SMEM] + [ANY] * 8 + [VMEM],
        [pltpu.VMEM((RH, C), F32), pltpu.SemaphoreType.DMA((9,))],
        (ANY, ANY, ANY),
    )(idx, h_own, *h_got, g_send[0], *g_got, half)

    def finish(idx, mine, theirs, w_in, w_out, b_out, buf, sem):
        parts = 4
        row = TAP - RH
        c_ = idx[2]
        step = RH // parts
        for i in range(parts):
            buf[i * step : (i + 1) * step] = theirs[...].reshape(RH, C)[i * step : (i + 1) * step].astype(F32) * grad_scale
            n = min(step, row - i * step)

            @pl.when(c_ == 1)
            def _():
                pltpu.make_async_copy(
                    buf.at[pl.ds(i * step, step)], w_out.at[pl.ds(i * step, step)], sem.at[i]
                ).start()

            @pl.when(c_ == 0)
            def _():
                pltpu.make_async_copy(
                    buf.at[pl.ds(i * step, n)], w_out.at[pl.ds(RH + i * step, n)], sem.at[i]
                ).start()

        own_b = mine[3, RQ - C : RQ - C + 8].astype(F32) * grad_scale
        b_out[...] = jnp.where(c_ == 1, own_b, buf[row : row + 8])[0:1]
        for i in range(parts):
            n = min(step, row - i * step)

            @pl.when(c_ == 1)
            def _():
                pltpu.make_async_copy(
                    buf.at[pl.ds(i * step, step)], w_out.at[pl.ds(i * step, step)], sem.at[i]
                ).wait()

            @pl.when(c_ == 0)
            def _():
                pltpu.make_async_copy(
                    buf.at[pl.ds(i * step, n)], w_out.at[pl.ds(RH + i * step, n)], sem.at[i]
                ).wait()

    w_grad, b_grad = pl.pallas_call(
        finish,
        name="finish",
        grid=(1,),
        out_shape=(sds((TAP, C), F32), sds((1, C), F32)),
        in_specs=[SMEM, VMEM, VMEM, ANY],
        out_specs=(ANY, VMEM),
        scratch_shapes=[pltpu.VMEM((RH, C), F32), pltpu.SemaphoreType.DMA((4,))],
        input_output_aliases={3: 0},
        compiler_params=pltpu.CompilerParams(vmem_limit_bytes=20 * 1024 * 1024),
    )(idx, half, other, w_part)
    return out_h[None, None], out_g[None, None], w_grad[None], b_grad


def solution(mesh):
    in_specs = (
        P("dp", "depth", None, None, None),
        P("section", None, None),
        P("section", None),
        P("dp", "depth", None, None, None),
    )
    out_specs = (
        P("section", "dp", "depth", None, None, None),
        P("section", "dp", "depth", None, None, None),
        P("section", None, None),
        P("section", None),
    )

    return jax.shard_map(shards, mesh=mesh, in_specs=in_specs, out_specs=out_specs, check_vma=False)
```

```python
import math

import jax
import jax.numpy as jnp
from jax import lax
from jax.experimental import pallas as pl
from jax.experimental.pallas import tpu as pltpu
from jax.sharding import PartitionSpec as P


BF = jnp.bfloat16
F32 = jnp.float32

SMEM = pl.BlockSpec(memory_space=pltpu.SMEM)
VMEM = pl.BlockSpec(memory_space=pltpu.VMEM)
ANY = pl.BlockSpec(memory_space=pl.ANY)
HBM = pl.BlockSpec(memory_space=pltpu.HBM)


def in_hbm(x):
    return pltpu.with_memory_space_constraint(x, pltpu.HBM)


def sds(shape, dtype=BF):
    return jax.ShapeDtypeStruct(shape, dtype)


def call(body, out, n_any_or_specs, scratch, out_specs=None, vmem=20):
    return pl.pallas_call(
        body,
        grid=(1,),
        out_shape=out,
        in_specs=n_any_or_specs,
        out_specs=out_specs if out_specs is not None else jax.tree.map(lambda _: VMEM, out),
        scratch_shapes=scratch,
        compiler_params=pltpu.CompilerParams(vmem_limit_bytes=vmem * 1024 * 1024),
    )


def column(w_ref, t, C=128):
    return jnp.concatenate(
        [
            jnp.concatenate([w_ref[t, (3 * k + c) * C : (3 * k + c + 1) * C] for c in range(3)], axis=1)
            for k in range(9)
        ],
        axis=0,
    )


def conv_plane(x_ref, p, wide, nr):
    W, C = x_ref.shape[2], x_ref.shape[3]
    m = nr * W
    lhs = jnp.concatenate(
        [x_ref[p + a, b : b + nr].reshape(m, C) for a in range(3) for b in range(3)], axis=1
    )
    y = jnp.dot(lhs, wide, preferred_element_type=F32)
    x_pos = lax.broadcasted_iota(jnp.int32, (m, C), 0) % W
    left = jnp.where(x_pos == 0, 0.0, pltpu.roll(y[:, :C], 1, 0))
    right = jnp.where(x_pos == W - 1, 0.0, pltpu.roll(y[:, 2 * C :], m - 1, 0))
    return y[:, C : 2 * C] + left + right


def inside(nr, W, C, first_row, H, plane, D):
    row = first_row + lax.broadcasted_iota(jnp.int32, (nr * W, C), 0) // W
    return (row >= 0) & (row < H) & (plane >= 0) & (plane < D)


def slope(pre):
    q = jax.nn.sigmoid(pre)
    return q * (1.0 + pre * (1.0 - q))


def assemble(dst, far, own, near, d, last):
    odd = d % 2
    zero = jnp.zeros(far.shape, BF)
    dst[pl.ds(4 * odd, 2)] = jnp.where((d > 0) & (d < last), far[...], zero)
    dst[2:4] = own[...]
    dst[pl.ds(4 - 4 * odd, 2)] = near[...]


def load_layer(s, c, t, own, got, swp, dst, rows):
    k = (s + 4 - t) % 4

    @pl.when(k == 0)
    def _():
        dst[...] = own[...]

    for i in range(3):

        @pl.when(k == i + 1)
        def _():
            for j in range(2):
                dst[pl.ds(pl.multiple_of((2 * c + j) * rows, 16), rows)] = got[2 * i + j][0:rows]
                dst[pl.ds(pl.multiple_of((2 - 2 * c + j) * rows, 16), rows)] = swp[2 * i + j][0:rows]


def bias_of(s, t, own_bias, got_bias):
    k = (s + 4 - t) % 4
    row = own_bias[0:1].astype(F32)
    for i in range(3):
        row = jnp.where(k == i + 1, got_bias[i][0:1].astype(F32), row)
    return row


def shards(volume, weights, biases, cotangent):
    n_sec = lax.axis_size("section")
    n_dep = lax.axis_size("depth")
    n_dp = lax.axis_size("dp")
    s = lax.axis_index("section")
    d = lax.axis_index("depth")
    c = lax.axis_index("dp")
    assert n_sec == 4 and n_dep == 16 and n_dp == 2
    PL, H, W, C = volume.shape[1:]
    assert PL == 2
    R = H // n_sec
    D = PL * n_dep
    last = n_dep - 1
    grad_scale = 1.0 / math.sqrt(n_dp * D * H * W)
    idx = jnp.stack([s, d, c]).astype(jnp.int32)
    TAP = 27 * C
    HALF = TAP // 2
    QR = HALF // 2
    QB = QR + 16

    def sec(v, k):
        return lax.ppermute(v, "section", [(i, i ^ k) for i in range(n_sec)])

    def both(v):
        result = []
        for first in (1, 0):
            pairs = [(i, i + 1) for i in range(first, n_dep - 1, 2)]
            result.append(lax.ppermute(v, "depth", pairs + [(b, a) for a, b in pairs]))
        return result

    def swap(v):
        return lax.ppermute(v, "dp", [(0, 1), (1, 0)])

    def xdep(v, k):
        return lax.ppermute(v, "depth", [(i, i ^ k) for i in range(n_dep)])

    def ydep(v, k):
        return lax.ppermute(v, "depth", [(i, i ^ (4 * k)) for i in range(n_dep)])

    own_w = weights[0]

    def prepare(vol, w, b, h0, part_a, part_b, own_b, pad, row, sem):
        s_, c_ = lax.axis_index("section"), lax.axis_index("dp")
        pulls = [
            pltpu.make_async_copy(w.at[2 * c_], part_a.at[pl.ds(0, QR)], sem.at[0]),
            pltpu.make_async_copy(w.at[2 * c_ + 1], part_b.at[pl.ds(0, QR)], sem.at[1]),
            pltpu.make_async_copy(b, row, sem.at[2]),
            pltpu.make_async_copy(vol, pad.at[:, pl.ds(8, H)], sem.at[3]),
        ]
        for cp in pulls:
            cp.start()
        pad[:, 0:8] = jnp.zeros((PL, 8, W, C), BF)
        pad[:, H + 8 :] = jnp.zeros((PL, 8, W, C), BF)
        for cp in pulls:
            cp.wait()
        bias = jnp.broadcast_to(row[...], (16, C))
        part_a[QR:] = bias
        part_b[QR:] = bias
        own_b[...] = bias
        h0[...] = pad[:, pl.ds(s_ * R, R + 16)]

    h0, part_a, part_b, own_b = call(
        prepare,
        (sds((PL, R + 16, W, C)), sds((QB, C)), sds((QB, C)), sds((16, C))),
        [HBM, HBM, HBM],
        [pltpu.VMEM((PL, H + 16, W, C), BF), pltpu.VMEM((1, C), BF), pltpu.SemaphoreType.DMA((4,))],
    )(in_hbm(volume[0]), in_hbm(own_w.reshape(4, QR, C)), in_hbm(biases))
    h0_lo, h0_hi = both(h0)

    def ring(v, k):
        return lax.ppermute(v, "section", [(i, (i + k) % n_sec) for i in range(n_sec)])

    a1, b3 = ring(part_a, 1), ring(part_b, 3)
    b1, a3 = ring(part_b, 1), ring(part_a, 3)
    a2, b2 = ring(a1, 1), ring(b3, 3)
    got = (a1, b1, a2, b2, a3, b3)
    swapped = [swap(g) for g in got]
    all_w = (own_w, *got, *swapped)
    W_SPECS = [VMEM] * 13
    all_b = (own_b, a1, a2, a3)
    tail_rows = pl.BlockSpec((16, C), lambda _: (QR // 16, 0))
    B_SPECS = [VMEM] + [tail_rows] * 3

    def turn(idx, own, *rest):
        got_, swp_, (out, buf) = rest[:6], rest[6:12], rest[12:]
        for t in (3, 2, 1, 0):
            load_layer(idx[0], idx[2], t, own, got_, swp_, buf.at[t], QR)

            def one(j, _):
                out[t, pl.ds(pl.multiple_of(j * C, C), C)] = buf[t, pl.ds(pl.multiple_of((26 - j) * C, C), C)].T
                return 0

            lax.fori_loop(0, 27, one, 0, unroll=3)

    def k1(idx, own, lo, hi, ow, *rest):
        got_, swp_, rest = rest[:6], rest[6:12], rest[12:]
        ob, b1_, b2_, b3_, h0e, pre0, h1e, pre1, h2, x, h1, w = rest
        s_, d_ = idx[0], idx[1]
        for t in range(2):
            load_layer(s_, idx[2], t, ow, got_, swp_, w.at[t], QR)
        assemble(x, lo, own, hi, d_, last)
        h0e[...] = x[1:5, 8 : 8 + R]
        b0 = bias_of(s_, 0, ob, (b1_, b2_, b3_))

        def one(p, _):
            pre = conv_plane(x, p, column(w, 0), R + 14) + b0
            h = jnp.where(inside(R + 14, W, C, s_ * R - 7, H, 2 * d_ - 1 + p, D), pre * jax.nn.sigmoid(pre), 0.0)
            h = h.astype(BF).reshape(R + 14, W, C)
            h1[p] = h
            h1e[p] = h[7 : 7 + R]
            pre0[p] = pre[6 * W : (16 + 0) * W].astype(BF).reshape(R + 2, W, C)
            return 0

        lax.fori_loop(0, 4, one, 0)
        b1 = bias_of(s_, 1, ob, (b1_, b2_, b3_))

        def two(p, _):
            pre = conv_plane(h1, p, column(w, 1), R + 12) + b1
            h = jnp.where(inside(R + 12, W, C, s_ * R - 6, H, 2 * d_ + p, D), pre * jax.nn.sigmoid(pre), 0.0)
            h2[p] = h.astype(BF).reshape(R + 12, W, C)
            pre1[p] = pre[4 * W : 16 * W].astype(BF).reshape(R + 4, W, C)
            return 0

        lax.fori_loop(0, 2, two, 0)

    h0e, pre0, h1e, pre1, h2 = call(
        k1,
        (
            sds((4, R, W, C)),
            sds((4, R + 2, W, C)),
            sds((4, R, W, C)),
            sds((2, R + 4, W, C)),
            sds((2, R + 12, W, C)),
        ),
        [SMEM, VMEM, VMEM, VMEM] + W_SPECS + B_SPECS,
        [
            pltpu.VMEM((6, R + 16, W, C), BF),
            pltpu.VMEM((4, R + 14, W, C), BF),
            pltpu.VMEM((2, TAP, C), BF),
        ],
    )(idx, h0, h0_lo, h0_hi, *all_w, *all_b)

    h2_lo, h2_hi = both(h2)

    wturn = call(turn, sds((4, TAP, C)), [SMEM] + W_SPECS, [pltpu.VMEM((4, TAP, C), BF)], VMEM)(idx, *all_w)
    h2_lo, h2_hi, wturn = lax.optimization_barrier((h2_lo, h2_hi, wturn))

    def k2(idx, own, lo, hi, ow, *rest):
        got_, swp_, rest = rest[:6], rest[6:12], rest[12:]
        ob, b1_, b2_, b3_, cot, h2e, pre2, h3e, h4, d3, x, h3, w, gpad = rest
        s_, d_ = idx[0], idx[1]
        for t in range(2):
            load_layer(s_, idx[2], t + 2, ow, got_, swp_, w.at[t], QR)
        assemble(x, lo, own, hi, d_, last)
        h2e[...] = x[1:5, 6 : 6 + R]
        gpad[:, 4 : 4 + H] = cot[...]
        b0 = bias_of(s_, 2, ob, (b1_, b2_, b3_))

        def one(p, _):
            pre = conv_plane(x, p, column(w, 0), R + 10) + b0
            h = jnp.where(inside(R + 10, W, C, s_ * R - 5, H, 2 * d_ - 1 + p, D), pre * jax.nn.sigmoid(pre), 0.0)
            h = h.astype(BF).reshape(R + 10, W, C)
            h3[p] = h
            h3e[p] = h[5 : 5 + R]
            pre2[p] = pre[2 * W : 16 * W].astype(BF).reshape(R + 6, W, C)
            return 0

        lax.fori_loop(0, 4, one, 0)
        b1 = bias_of(s_, 3, ob, (b1_, b2_, b3_))

        def two(p, _):
            pre = conv_plane(h3, p, column(w, 1), R + 8) + b1
            h = (pre * jax.nn.sigmoid(pre)).astype(BF).reshape(R + 8, W, C)
            h4[p] = h[4 : 4 + R]
            g = gpad[p, pl.ds(s_ * R, R + 8)].reshape((R + 8) * W, C).astype(F32)
            dl = g * slope(pre.astype(BF).astype(F32))
            dl = jnp.where(inside(R + 8, W, C, s_ * R - 4, H, 2 * d_ + p, D), dl, 0.0)
            d3[p] = dl.astype(BF).reshape(R + 8, W, C)
            return 0

        lax.fori_loop(0, 2, two, 0)

    h2e, pre2, h3e, h4, d3 = call(
        k2,
        (
            sds((4, R, W, C)),
            sds((4, R + 6, W, C)),
            sds((4, R, W, C)),
            sds((2, R, W, C)),
            sds((2, R + 8, W, C)),
        ),
        [SMEM, VMEM, VMEM, VMEM] + W_SPECS + B_SPECS + [VMEM],
        [
            pltpu.VMEM((6, R + 12, W, C), BF),
            pltpu.VMEM((4, R + 10, W, C), BF),
            pltpu.VMEM((2, TAP, C), BF),
            pltpu.VMEM((PL, H + 8, W, C), BF),
        ],
    )(idx, h2, h2_lo, h2_hi, *all_w, *all_b, cotangent[0])

    d3_lo, d3_hi = both(d3)

    def pack(idx, x0, x1, x2, x3, x4, own, a1, a2, a3):
        xs = (x0, x1, x2, x3)
        for k, out in enumerate((own, a1, a2, a3)):
            for t in range(4):

                @pl.when((idx[0] ^ k) == t)
                def _():
                    out[0:4] = xs[t][...]
                    out[4:6] = x4[...] if t == 3 else xs[t + 1][1:3]

    six = sds((6, R, W, C))
    h_own, *h_send = call(pack, (six,) * 4, [SMEM] + [VMEM] * 5, [])(idx, h0e, h1e, h2e, h3e, h4)
    h_got = [sec(h_send[k - 1], k) for k in (1, 2, 3)]

    def wturn_of(t):
        return pl.BlockSpec((1, TAP, C), lambda _: (t, 0, 0))

    piece = sds((2, R, W, C))

    def delta_of(g, pre, p, n, first_row, plane):
        dl = g.astype(F32) * slope(pre[p].reshape(n * W, C).astype(F32))
        dl = jnp.where(inside(n, W, C, first_row, H, plane, D), dl, 0.0)
        return dl.astype(BF).reshape(n, W, C)

    def send_all(s_, outs, values):
        for k in range(4):
            for t in range(4):

                @pl.when((s_ ^ k) == t)
                def _():
                    outs[k][...] = values[t]()

    def k3(idx, own, lo, hi, wa, wb, pre_a, pre_b, ga, da, gb, db, x, dbuf):
        s_, d_ = idx[0], idx[1]
        assemble(x, lo, own, hi, d_, last)

        def one(p, _):
            g = conv_plane(x, p, column(wa, 0), R + 6).astype(BF)
            dl = delta_of(g, pre_a, p, R + 6, s_ * R - 3, 2 * d_ - 1 + p)
            dbuf[p] = dl

            @pl.when((p > 0) & (p < 3))
            def _():
                ga[p - 1] = g.reshape(R + 6, W, C)[3 : 3 + R]
                da[p - 1] = dl[3 : 3 + R]

            return 0

        lax.fori_loop(0, 4, one, 0)

        def two(p, _):
            g = conv_plane(dbuf, p, column(wb, 0), R + 4).astype(BF)
            gb[p] = g.reshape(R + 4, W, C)[2 : 2 + R]
            db[p] = delta_of(g, pre_b, p, R + 4, s_ * R - 2, 2 * d_ + p)
            return 0

        lax.fori_loop(0, 2, two, 0)

    g3, d2, g2, d1 = call(
        k3,
        (piece, piece, piece, sds((2, R + 4, W, C))),
        [SMEM, VMEM, VMEM, VMEM, wturn_of(3), wturn_of(2), VMEM, VMEM],
        [pltpu.VMEM((6, R + 8, W, C), BF), pltpu.VMEM((4, R + 6, W, C), BF)],
    )(idx, d3, d3_lo, d3_hi, wturn, wturn, pre2, pre1)
    d1_lo, d1_hi = both(d1)

    def k4a(idx, own, lo, hi, wa, pre_a, e1, e2, e3, g1, dbuf, *rest):
        *sends, x = rest
        s_, d_ = idx[0], idx[1]
        assemble(x, lo, own, hi, d_, last)

        def one(p, _):
            g = conv_plane(x, p, column(wa, 0), R + 2).astype(BF)
            dbuf[p] = delta_of(g, pre_a, p, R + 2, s_ * R - 1, 2 * d_ - 1 + p)

            @pl.when((p > 0) & (p < 3))
            def _():
                g1[p - 1] = g.reshape(R + 2, W, C)[1 : 1 + R]

            return 0

        lax.fori_loop(0, 4, one, 0)
        send_all(
            s_,
            sends,
            (
                lambda: dbuf[1:3, 1 : 1 + R],
                lambda: e1[:, 2 : 2 + R],
                lambda: e2[...],
                lambda: e3[:, 4 : 4 + R],
            ),
        )

    g1, d0, *d_send = call(
        k4a,
        (piece, sds((4, R + 2, W, C))) + (piece,) * 4,
        [SMEM, VMEM, VMEM, VMEM, wturn_of(1), VMEM, VMEM, VMEM, VMEM],
        [pltpu.VMEM((6, R + 4, W, C), BF)],
    )(idx, d1, d1_lo, d1_hi, wturn, pre0, d1, d2, d3)
    d_got = [sec(d_send[k], k) for k in (1, 3, 2)]
    d_got = [d_got[0], d_got[2], d_got[1]]

    def k4b(idx, dbuf, wb, g1, g2, g3, *rest):
        *sends, g0 = rest

        def two(p, _):
            g0[p] = conv_plane(dbuf, p, column(wb, 0), R).astype(BF).reshape(R, W, C)
            return 0

        lax.fori_loop(0, 2, two, 0)
        send_all(idx[0], sends, (lambda: g0[...], lambda: g1[...], lambda: g2[...], lambda: g3[...]))

    g_send = call(
        k4b, (piece,) * 4, [SMEM, VMEM, wturn_of(0), VMEM, VMEM, VMEM], [pltpu.VMEM(piece.shape, BF)]
    )(idx, d0, wturn, g1, g2, g3)
    g_got = []
    for k in (1, 2, 3):
        g_got.append(sec(g_send[k], k))

    def kx(idx, x0, x1, x2, x3, x):
        x[:, 0] = jnp.zeros((4, W, C), BF)
        x[:, H + 1] = jnp.zeros((4, W, C), BF)
        for k, xs in enumerate((x0, x1, x2, x3)):
            x[:, pl.ds((idx[0] ^ k) * R + 1, R)] = xs[0:4]

    x_all = call(kx, sds((4, H + 2, W, C)), [SMEM] + [VMEM] * 4, [], VMEM)(idx, h_own, *h_got)

    ROWS = TAP + C

    def kw(idx, x, e0, e1, e2, e3, keep, away, dl, wide, out):
        s_ = idx[0]
        for k, es in enumerate((e0, e1, e2, e3)):
            dl[:, pl.ds((s_ ^ k) * R, R)] = es[...]
        m = 4 * W
        pos = lax.broadcasted_iota(jnp.int32, (m, C), 0) % W

        def spread(i, acc):
            for p in range(2):
                v16 = dl[p, pl.ds(i * 4, 4)].reshape(m, C)
                v = v16.astype(F32)
                at = pl.ds(pl.multiple_of(i * m, m), m)
                wide[p, at, 0:C] = jnp.where(pos == W - 1, 0.0, pltpu.roll(v, m - 1, 0)).astype(BF)
                wide[p, at, C : 2 * C] = v16
                wide[p, at, 2 * C :] = jnp.where(pos == 0, 0.0, pltpu.roll(v, 1, 0)).astype(BF)
                acc = acc + jnp.sum(v.reshape(m // 8, 8, C), axis=0)
            return acc

        acc_b = jnp.sum(lax.fori_loop(0, H // 4, spread, jnp.zeros((8, C), F32)), axis=0, keepdims=True)

        def one(a, _):
            acc = jnp.zeros((3 * C, 3 * C), F32)
            for p in range(2):
                lhs = jnp.concatenate([x[p + a, b : b + H].reshape(H * W, C) for b in range(3)], axis=1)
                acc = acc + lax.dot_general(
                    lhs, wide[p], (((0,), (0,)), ((), ())), preferred_element_type=F32
                )
            for b in range(3):
                for j in range(3):
                    out[9 * a + 3 * b + j] = acc[b * C : (b + 1) * C, j * C : (j + 1) * C]
            return 0

        lax.fori_loop(0, 3, one, 0)
        first = lax.broadcasted_iota(jnp.int32, (C, C), 0) == 0
        out[27] = jnp.where(first, jnp.broadcast_to(acc_b, (C, C)), 0.0)
        keep[...] = out[pl.ds(idx[2] * 14, 14)].reshape(RH, C)
        away[...] = out[pl.ds((1 - idx[2]) * 14, 14)].reshape(RH, C).astype(BF)

    RH, RQ = ROWS // 2, ROWS // 8
    keep, away = call(
        kw,
        (sds((RH, C), F32), sds((RH, C))),
        [SMEM] + [VMEM] * 5,
        [
            pltpu.VMEM((2, H, W, C), BF),
            pltpu.VMEM((2, H * W, 3 * C), BF),
            pltpu.VMEM((28, C, C), F32),
        ],
    )(idx, x_all, d_send[0], *d_got)

    recv = swap(away)

    def split(idx, keep, recv, mine, q1, q2, q3, buf):
        x = idx[1] % 4
        buf[...] = keep[...].reshape(4, RQ, C) + recv[...].reshape(4, RQ, C).astype(F32)
        mine[...] = buf[x]
        for k, q in enumerate((q1, q2, q3), 1):
            q[...] = buf[x ^ k].astype(BF)

    quart = sds((RQ, C))
    q, *qs = call(
        split, (sds((RQ, C), F32), quart, quart, quart), [SMEM, VMEM, VMEM], [pltpu.VMEM((4, RQ, C), F32)]
    )(idx, keep, recv)
    xs = [xdep(qs[k - 1], k) for k in (1, 2, 3)]
    for v in xs:
        q = q + v.astype(F32)
    q = q.astype(BF)
    ys = [ydep(q, k) for k in (1, 2, 3)]

    def ordered(idx, q0, q1, q2, q3, out, buf):
        y = idx[1] // 4
        for k, r in enumerate((q0, q1, q2, q3)):
            buf[k] = r[...].astype(F32)
        acc = buf[y]
        for j in range(1, 4):
            acc = acc + buf[y ^ j]
        out[...] = acc.astype(BF)

    q = call(ordered, sds((RQ, C)), [SMEM] + [VMEM] * 4, [pltpu.VMEM((4, RQ, C), F32)], VMEM)(idx, q, *ys)
    qs = [q] + [xdep(q, k) for k in (1, 2, 3)]

    def join(idx, q0, q1, q2, q3, out):
        x = idx[1] % 4
        for k, r in enumerate((q0, q1, q2, q3)):
            out[x ^ k] = r[...]

    half = call(join, sds((4, RQ, C)), [SMEM] + [VMEM] * 4, [], VMEM)(idx, *qs)
    other = swap(half)

    def place(idx, a0, a1, a2, a3, b0, b1, b2, b3, mine, oa, ob, w_out, buf, sem):
        copies = []
        for k, (va, vb) in enumerate(((a0, b0), (a1, b1), (a2, b2), (a3, b3))):
            row = (idx[0] ^ k) * R
            copies.append(pltpu.make_async_copy(va.at[4:6], oa.at[:, pl.ds(row, R)], sem.at[2 * k]))
            copies.append(pltpu.make_async_copy(vb, ob.at[:, pl.ds(row, R)], sem.at[2 * k + 1]))
        for cp in copies:
            cp.start()
        buf[...] = mine[...].reshape(RH, C).astype(F32) * grad_scale
        for c_, n in ((0, RH), (1, TAP - RH)):

            @pl.when(idx[2] == c_)
            def _():
                cp = pltpu.make_async_copy(
                    buf.at[pl.ds(0, n)], w_out.at[pl.ds(c_ * RH, n)], sem.at[8]
                )
                cp.start()
                cp.wait()

        for cp in copies:
            cp.wait()

    full = sds((2, H, W, C))
    out_h, out_g, w_part = call(
        place,
        (full, full, sds((TAP, C), F32)),
        [SMEM] + [ANY] * 8 + [VMEM],
        [pltpu.VMEM((RH, C), F32), pltpu.SemaphoreType.DMA((9,))],
        (ANY, ANY, ANY),
    )(idx, h_own, *h_got, g_send[0], *g_got, half)

    def finish(idx, mine, theirs, w_in, w_out, b_out, buf, sem):
        parts = 4
        row = TAP - RH
        c_ = idx[2]
        step = RH // parts
        for i in range(parts):
            buf[i * step : (i + 1) * step] = theirs[...].reshape(RH, C)[i * step : (i + 1) * step].astype(F32) * grad_scale
            n = min(step, row - i * step)

            @pl.when(c_ == 1)
            def _():
                pltpu.make_async_copy(
                    buf.at[pl.ds(i * step, step)], w_out.at[pl.ds(i * step, step)], sem.at[i]
                ).start()

            @pl.when(c_ == 0)
            def _():
                pltpu.make_async_copy(
                    buf.at[pl.ds(i * step, n)], w_out.at[pl.ds(RH + i * step, n)], sem.at[i]
                ).start()

        own_b = mine[3, RQ - C : RQ - C + 8].astype(F32) * grad_scale
        b_out[...] = jnp.where(c_ == 1, own_b, buf[row : row + 8])[0:1]
        for i in range(parts):
            n = min(step, row - i * step)

            @pl.when(c_ == 1)
            def _():
                pltpu.make_async_copy(
                    buf.at[pl.ds(i * step, step)], w_out.at[pl.ds(i * step, step)], sem.at[i]
                ).wait()

            @pl.when(c_ == 0)
            def _():
                pltpu.make_async_copy(
                    buf.at[pl.ds(i * step, n)], w_out.at[pl.ds(RH + i * step, n)], sem.at[i]
                ).wait()

    w_grad, b_grad = pl.pallas_call(
        finish,
        name="finish",
        grid=(1,),
        out_shape=(sds((TAP, C), F32), sds((1, C), F32)),
        in_specs=[SMEM, VMEM, VMEM, ANY],
        out_specs=(ANY, VMEM),
        scratch_shapes=[pltpu.VMEM((RH, C), F32), pltpu.SemaphoreType.DMA((4,))],
        input_output_aliases={3: 0},
        compiler_params=pltpu.CompilerParams(vmem_limit_bytes=20 * 1024 * 1024),
    )(idx, half, other, w_part)
    return out_h[None, None], out_g[None, None], w_grad[None], b_grad


def solution(mesh):
    in_specs = (
        P("dp", "depth", None, None, None),
        P("section", None, None),
        P("section", None),
        P("dp", "depth", None, None, None),
    )
    out_specs = (
        P("section", "dp", "depth", None, None, None),
        P("section", "dp", "depth", None, None, None),
        P("section", None, None),
        P("section", None),
    )

    return jax.shard_map(shards, mesh=mesh, in_specs=in_specs, out_specs=out_specs, check_vma=False)
```

```python
import math

import jax
import jax.numpy as jnp
from jax import lax
from jax.experimental import pallas as pl
from jax.experimental.pallas import tpu as pltpu
from jax.sharding import PartitionSpec as P


BF = jnp.bfloat16
F32 = jnp.float32

SMEM = pl.BlockSpec(memory_space=pltpu.SMEM)
VMEM = pl.BlockSpec(memory_space=pltpu.VMEM)
ANY = pl.BlockSpec(memory_space=pl.ANY)
HBM = pl.BlockSpec(memory_space=pltpu.HBM)


def in_hbm(x):
    return pltpu.with_memory_space_constraint(x, pltpu.HBM)


def sds(shape, dtype=BF):
    return jax.ShapeDtypeStruct(shape, dtype)


def call(body, out, n_any_or_specs, scratch, out_specs=None, vmem=20):
    return pl.pallas_call(
        body,
        grid=(1,),
        out_shape=out,
        in_specs=n_any_or_specs,
        out_specs=out_specs if out_specs is not None else jax.tree.map(lambda _: VMEM, out),
        scratch_shapes=scratch,
        compiler_params=pltpu.CompilerParams(vmem_limit_bytes=vmem * 1024 * 1024),
    )


def column(w_ref, t, C=128):
    return jnp.concatenate(
        [
            jnp.concatenate([w_ref[t, (3 * k + c) * C : (3 * k + c + 1) * C] for c in range(3)], axis=1)
            for k in range(9)
        ],
        axis=0,
    )


def conv_plane(x_ref, p, wide, nr):
    W, C = x_ref.shape[2], x_ref.shape[3]
    m = nr * W
    lhs = jnp.concatenate(
        [x_ref[p + a, b : b + nr].reshape(m, C) for a in range(3) for b in range(3)], axis=1
    )
    y = jnp.dot(lhs, wide, preferred_element_type=F32)
    x_pos = lax.broadcasted_iota(jnp.int32, (m, C), 0) % W
    left = jnp.where(x_pos == 0, 0.0, pltpu.roll(y[:, :C], 1, 0))
    right = jnp.where(x_pos == W - 1, 0.0, pltpu.roll(y[:, 2 * C :], m - 1, 0))
    return y[:, C : 2 * C] + left + right


def inside(nr, W, C, first_row, H, plane, D):
    row = first_row + lax.broadcasted_iota(jnp.int32, (nr * W, C), 0) // W
    return (row >= 0) & (row < H) & (plane >= 0) & (plane < D)


def slope(pre):
    q = jax.nn.sigmoid(pre)
    return q * (1.0 + pre * (1.0 - q))


def assemble(dst, far, own, near, d, last):
    odd = d % 2
    zero = jnp.zeros(far.shape, BF)
    dst[pl.ds(4 * odd, 2)] = jnp.where((d > 0) & (d < last), far[...], zero)
    dst[2:4] = own[...]
    dst[pl.ds(4 - 4 * odd, 2)] = near[...]


def load_layer(s, c, t, own, got, swp, dst, rows):
    k = (s + 4 - t) % 4

    @pl.when(k == 0)
    def _():
        dst[...] = own[...]

    for i in range(3):

        @pl.when(k == i + 1)
        def _():
            for j in range(2):
                dst[pl.ds(pl.multiple_of((2 * c + j) * rows, 16), rows)] = got[2 * i + j][0:rows]
                dst[pl.ds(pl.multiple_of((2 - 2 * c + j) * rows, 16), rows)] = swp[2 * i + j][0:rows]


def bias_of(s, t, own_bias, got_bias):
    k = (s + 4 - t) % 4
    row = own_bias[0:1].astype(F32)
    for i in range(3):
        row = jnp.where(k == i + 1, got_bias[i][0:1].astype(F32), row)
    return row


def shards(volume, weights, biases, cotangent):
    n_sec = lax.axis_size("section")
    n_dep = lax.axis_size("depth")
    n_dp = lax.axis_size("dp")
    s = lax.axis_index("section")
    d = lax.axis_index("depth")
    c = lax.axis_index("dp")
    assert n_sec == 4 and n_dep == 16 and n_dp == 2
    PL, H, W, C = volume.shape[1:]
    assert PL == 2
    R = H // n_sec
    D = PL * n_dep
    last = n_dep - 1
    grad_scale = 1.0 / math.sqrt(n_dp * D * H * W)
    idx = jnp.stack([s, d, c]).astype(jnp.int32)
    TAP = 27 * C
    HALF = TAP // 2
    QR = HALF // 2
    QB = QR + 16

    def sec(v, k):
        return lax.ppermute(v, "section", [(i, i ^ k) for i in range(n_sec)])

    def three(send, values):
        got = {}
        for k in (2, 1, 3):
            got[k] = send(values[k], k)
        return [got[k] for k in (1, 2, 3)]

    def both(v):
        result = []
        for first in (1, 0):
            pairs = [(i, i + 1) for i in range(first, n_dep - 1, 2)]
            result.append(lax.ppermute(v, "depth", pairs + [(b, a) for a, b in pairs]))
        return result

    def swap(v):
        return lax.ppermute(v, "dp", [(0, 1), (1, 0)])

    def xdep(v, k):
        return lax.ppermute(v, "depth", [(i, i ^ k) for i in range(n_dep)])

    def ydep(v, k):
        return lax.ppermute(v, "depth", [(i, i ^ (4 * k)) for i in range(n_dep)])

    own_w = weights[0]

    def prepare(w, b, part_a, part_b, own_b, row, sem):
        c_ = lax.axis_index("dp")
        pulls = [
            pltpu.make_async_copy(w.at[2 * c_], part_a.at[pl.ds(0, QR)], sem.at[0]),
            pltpu.make_async_copy(w.at[2 * c_ + 1], part_b.at[pl.ds(0, QR)], sem.at[1]),
            pltpu.make_async_copy(b, row, sem.at[2]),
        ]
        for cp in pulls:
            cp.start()
        for cp in pulls:
            cp.wait()
        bias = jnp.broadcast_to(row[...], (16, C))
        part_a[QR:] = bias
        part_b[QR:] = bias
        own_b[...] = bias

    part_a, part_b, own_b = call(
        prepare,
        (sds((QB, C)), sds((QB, C)), sds((16, C))),
        [HBM, HBM],
        [pltpu.VMEM((1, C), BF), pltpu.SemaphoreType.DMA((3,))],
    )(in_hbm(own_w.reshape(4, QR, C)), in_hbm(biases))

    def rows_of(vol, h0, pad, sem):
        pull = pltpu.make_async_copy(vol, pad.at[:, pl.ds(8, H)], sem)
        pull.start()
        pad[:, 0:8] = jnp.zeros((PL, 8, W, C), BF)
        pad[:, H + 8 :] = jnp.zeros((PL, 8, W, C), BF)
        pull.wait()
        h0[...] = pad[:, pl.ds(lax.axis_index("section") * R, R + 16)]

    h0 = call(
        rows_of, sds((PL, R + 16, W, C)), [HBM], [pltpu.VMEM((PL, H + 16, W, C), BF), pltpu.SemaphoreType.DMA], VMEM
    )(in_hbm(volume[0]))
    h0_lo, h0_hi = both(h0)

    def ring(v, k):
        return lax.ppermute(v, "section", [(i, (i + k) % n_sec) for i in range(n_sec)])

    a1, b3 = ring(part_a, 1), ring(part_b, 3)
    b1, a3 = ring(part_b, 1), ring(part_a, 3)
    a2, b2 = ring(a1, 1), ring(b3, 3)
    got = (a1, b1, a2, b2, a3, b3)
    swapped = [swap(g) for g in got]
    all_w = (own_w, *got, *swapped)
    W_SPECS = [VMEM] * 13
    all_b = (own_b, a1, a2, a3)
    tail_rows = pl.BlockSpec((16, C), lambda _: (QR // 16, 0))
    B_SPECS = [VMEM] + [tail_rows] * 3

    def turn(idx, own, *rest):
        got_, swp_, (out, buf) = rest[:6], rest[6:12], rest[12:]
        for t in (3, 2, 1, 0):
            load_layer(idx[0], idx[2], t, own, got_, swp_, buf.at[t], QR)

            def one(j, _):
                out[t, pl.ds(pl.multiple_of(j * C, C), C)] = buf[t, pl.ds(pl.multiple_of((26 - j) * C, C), C)].T
                return 0

            lax.fori_loop(0, 27, one, 0, unroll=3)

    def k1(idx, own, lo, hi, ow, *rest):
        got_, swp_, rest = rest[:6], rest[6:12], rest[12:]
        ob, b1_, b2_, b3_, h0e, pre0, h1e, pre1, h2, x, h1, w = rest
        s_, d_ = idx[0], idx[1]
        for t in range(2):
            load_layer(s_, idx[2], t, ow, got_, swp_, w.at[t], QR)
        assemble(x, lo, own, hi, d_, last)
        h0e[...] = x[1:5, 8 : 8 + R]
        b0 = bias_of(s_, 0, ob, (b1_, b2_, b3_))

        def one(p, _):
            pre = conv_plane(x, p, column(w, 0), R + 14) + b0
            h = jnp.where(inside(R + 14, W, C, s_ * R - 7, H, 2 * d_ - 1 + p, D), pre * jax.nn.sigmoid(pre), 0.0)
            h = h.astype(BF).reshape(R + 14, W, C)
            h1[p] = h
            h1e[p] = h[7 : 7 + R]
            pre0[p] = pre[6 * W : (16 + 0) * W].astype(BF).reshape(R + 2, W, C)
            return 0

        lax.fori_loop(0, 4, one, 0)
        b1 = bias_of(s_, 1, ob, (b1_, b2_, b3_))

        def two(p, _):
            pre = conv_plane(h1, p, column(w, 1), R + 12) + b1
            h = jnp.where(inside(R + 12, W, C, s_ * R - 6, H, 2 * d_ + p, D), pre * jax.nn.sigmoid(pre), 0.0)
            h2[p] = h.astype(BF).reshape(R + 12, W, C)
            pre1[p] = pre[4 * W : 16 * W].astype(BF).reshape(R + 4, W, C)
            return 0

        lax.fori_loop(0, 2, two, 0)

    h0e, pre0, h1e, pre1, h2 = call(
        k1,
        (
            sds((4, R, W, C)),
            sds((4, R + 2, W, C)),
            sds((4, R, W, C)),
            sds((2, R + 4, W, C)),
            sds((2, R + 12, W, C)),
        ),
        [SMEM, VMEM, VMEM, VMEM] + W_SPECS + B_SPECS,
        [
            pltpu.VMEM((6, R + 16, W, C), BF),
            pltpu.VMEM((4, R + 14, W, C), BF),
            pltpu.VMEM((2, TAP, C), BF),
        ],
    )(idx, h0, h0_lo, h0_hi, *all_w, *all_b)

    h2_lo, h2_hi = both(h2)

    wturn = call(turn, sds((4, TAP, C)), [SMEM] + W_SPECS, [pltpu.VMEM((4, TAP, C), BF)], VMEM)(idx, *all_w)
    h2_lo, h2_hi, wturn = lax.optimization_barrier((h2_lo, h2_hi, wturn))

    def k2(idx, own, lo, hi, ow, *rest):
        got_, swp_, rest = rest[:6], rest[6:12], rest[12:]
        ob, b1_, b2_, b3_, cot, h2e, pre2, h3e, h4, d3, x, h3, w, gpad = rest
        s_, d_ = idx[0], idx[1]
        for t in range(2):
            load_layer(s_, idx[2], t + 2, ow, got_, swp_, w.at[t], QR)
        assemble(x, lo, own, hi, d_, last)
        h2e[...] = x[1:5, 6 : 6 + R]
        gpad[:, 4 : 4 + H] = cot[...]
        b0 = bias_of(s_, 2, ob, (b1_, b2_, b3_))

        def one(p, _):
            pre = conv_plane(x, p, column(w, 0), R + 10) + b0
            h = jnp.where(inside(R + 10, W, C, s_ * R - 5, H, 2 * d_ - 1 + p, D), pre * jax.nn.sigmoid(pre), 0.0)
            h = h.astype(BF).reshape(R + 10, W, C)
            h3[p] = h
            h3e[p] = h[5 : 5 + R]
            pre2[p] = pre[2 * W : 16 * W].astype(BF).reshape(R + 6, W, C)
            return 0

        lax.fori_loop(0, 4, one, 0)
        b1 = bias_of(s_, 3, ob, (b1_, b2_, b3_))

        def two(p, _):
            pre = conv_plane(h3, p, column(w, 1), R + 8) + b1
            h = (pre * jax.nn.sigmoid(pre)).astype(BF).reshape(R + 8, W, C)
            h4[p] = h[4 : 4 + R]
            g = gpad[p, pl.ds(s_ * R, R + 8)].reshape((R + 8) * W, C).astype(F32)
            dl = g * slope(pre.astype(BF).astype(F32))
            dl = jnp.where(inside(R + 8, W, C, s_ * R - 4, H, 2 * d_ + p, D), dl, 0.0)
            d3[p] = dl.astype(BF).reshape(R + 8, W, C)
            return 0

        lax.fori_loop(0, 2, two, 0)

    h2e, pre2, h3e, h4, d3 = call(
        k2,
        (
            sds((4, R, W, C)),
            sds((4, R + 6, W, C)),
            sds((4, R, W, C)),
            sds((2, R, W, C)),
            sds((2, R + 8, W, C)),
        ),
        [SMEM, VMEM, VMEM, VMEM] + W_SPECS + B_SPECS + [VMEM],
        [
            pltpu.VMEM((6, R + 12, W, C), BF),
            pltpu.VMEM((4, R + 10, W, C), BF),
            pltpu.VMEM((2, TAP, C), BF),
            pltpu.VMEM((PL, H + 8, W, C), BF),
        ],
    )(idx, h2, h2_lo, h2_hi, *all_w, *all_b, cotangent[0])

    d3_lo, d3_hi = both(d3)

    def pack(idx, x0, x1, x2, x3, x4, own, a1, a2, a3):
        xs = (x0, x1, x2, x3)
        for k, out in enumerate((own, a1, a2, a3)):
            for t in range(4):

                @pl.when((idx[0] ^ k) == t)
                def _():
                    out[0:4] = xs[t][...]
                    out[4:6] = x4[...] if t == 3 else xs[t + 1][1:3]

    six = sds((6, R, W, C))
    h_own, *h_send = call(pack, (six,) * 4, [SMEM] + [VMEM] * 5, [])(idx, h0e, h1e, h2e, h3e, h4)
    h_got = [sec(h_send[k - 1], k) for k in (1, 2, 3)]

    def wturn_of(t):
        return pl.BlockSpec((1, TAP, C), lambda _: (t, 0, 0))

    piece = sds((2, R, W, C))

    def delta_of(g, pre, p, n, first_row, plane):
        dl = g.astype(F32) * slope(pre[p].reshape(n * W, C).astype(F32))
        dl = jnp.where(inside(n, W, C, first_row, H, plane, D), dl, 0.0)
        return dl.astype(BF).reshape(n, W, C)

    def send_all(s_, outs, values):
        for k in range(4):
            for t in range(4):

                @pl.when((s_ ^ k) == t)
                def _():
                    outs[k][...] = values[t]()

    def k3(idx, own, lo, hi, wa, wb, pre_a, pre_b, ga, da, gb, db, x, dbuf):
        s_, d_ = idx[0], idx[1]
        assemble(x, lo, own, hi, d_, last)

        def one(p, _):
            g = conv_plane(x, p, column(wa, 0), R + 6).astype(BF)
            dl = delta_of(g, pre_a, p, R + 6, s_ * R - 3, 2 * d_ - 1 + p)
            dbuf[p] = dl

            @pl.when((p > 0) & (p < 3))
            def _():
                ga[p - 1] = g.reshape(R + 6, W, C)[3 : 3 + R]
                da[p - 1] = dl[3 : 3 + R]

            return 0

        lax.fori_loop(0, 4, one, 0)

        def two(p, _):
            g = conv_plane(dbuf, p, column(wb, 0), R + 4).astype(BF)
            gb[p] = g.reshape(R + 4, W, C)[2 : 2 + R]
            db[p] = delta_of(g, pre_b, p, R + 4, s_ * R - 2, 2 * d_ + p)
            return 0

        lax.fori_loop(0, 2, two, 0)

    g3, d2, g2, d1 = call(
        k3,
        (piece, piece, piece, sds((2, R + 4, W, C))),
        [SMEM, VMEM, VMEM, VMEM, wturn_of(3), wturn_of(2), VMEM, VMEM],
        [pltpu.VMEM((6, R + 8, W, C), BF), pltpu.VMEM((4, R + 6, W, C), BF)],
    )(idx, d3, d3_lo, d3_hi, wturn, wturn, pre2, pre1)
    d1_lo, d1_hi = both(d1)

    def k4a(idx, own, lo, hi, wa, pre_a, e1, e2, e3, g1, dbuf, *rest):
        *sends, x = rest
        s_, d_ = idx[0], idx[1]
        assemble(x, lo, own, hi, d_, last)

        def one(p, _):
            g = conv_plane(x, p, column(wa, 0), R + 2).astype(BF)
            dbuf[p] = delta_of(g, pre_a, p, R + 2, s_ * R - 1, 2 * d_ - 1 + p)

            @pl.when((p > 0) & (p < 3))
            def _():
                g1[p - 1] = g.reshape(R + 2, W, C)[1 : 1 + R]

            return 0

        lax.fori_loop(0, 4, one, 0)
        send_all(
            s_,
            sends,
            (
                lambda: dbuf[1:3, 1 : 1 + R],
                lambda: e1[:, 2 : 2 + R],
                lambda: e2[...],
                lambda: e3[:, 4 : 4 + R],
            ),
        )

    g1, d0, *d_send = call(
        k4a,
        (piece, sds((4, R + 2, W, C))) + (piece,) * 4,
        [SMEM, VMEM, VMEM, VMEM, wturn_of(1), VMEM, VMEM, VMEM, VMEM],
        [pltpu.VMEM((6, R + 4, W, C), BF)],
    )(idx, d1, d1_lo, d1_hi, wturn, pre0, d1, d2, d3)
    d_got = three(sec, d_send)

    def k4b(idx, dbuf, wb, g1, g2, g3, *rest):
        *sends, g0 = rest

        def two(p, _):
            g0[p] = conv_plane(dbuf, p, column(wb, 0), R).astype(BF).reshape(R, W, C)
            return 0

        lax.fori_loop(0, 2, two, 0)
        send_all(idx[0], sends, (lambda: g0[...], lambda: g1[...], lambda: g2[...], lambda: g3[...]))

    g_send = call(
        k4b, (piece,) * 4, [SMEM, VMEM, wturn_of(0), VMEM, VMEM, VMEM], [pltpu.VMEM(piece.shape, BF)]
    )(idx, d0, wturn, g1, g2, g3)
    g_got = []
    for k in (1, 2, 3):
        g_got.append(sec(g_send[k], k))

    def kx(idx, x0, x1, x2, x3, x):
        x[:, 0] = jnp.zeros((4, W, C), BF)
        x[:, H + 1] = jnp.zeros((4, W, C), BF)
        for k, xs in enumerate((x0, x1, x2, x3)):
            x[:, pl.ds((idx[0] ^ k) * R + 1, R)] = xs[0:4]

    x_all = call(kx, sds((4, H + 2, W, C)), [SMEM] + [VMEM] * 4, [], VMEM)(idx, h_own, *h_got)

    ROWS = TAP + C

    def kw(idx, x, e0, e1, e2, e3, keep, away, dl, wide, out):
        s_ = idx[0]
        for k, es in enumerate((e0, e1, e2, e3)):
            dl[:, pl.ds((s_ ^ k) * R, R)] = es[...]
        m = 4 * W
        pos = lax.broadcasted_iota(jnp.int32, (m, C), 0) % W

        def spread(i, acc):
            for p in range(2):
                v16 = dl[p, pl.ds(i * 4, 4)].reshape(m, C)
                v = v16.astype(F32)
                at = pl.ds(pl.multiple_of(i * m, m), m)
                wide[p, at, 0:C] = jnp.where(pos == W - 1, 0.0, pltpu.roll(v, m - 1, 0)).astype(BF)
                wide[p, at, C : 2 * C] = v16
                wide[p, at, 2 * C :] = jnp.where(pos == 0, 0.0, pltpu.roll(v, 1, 0)).astype(BF)
                acc = acc + jnp.sum(v.reshape(m // 8, 8, C), axis=0)
            return acc

        acc_b = jnp.sum(lax.fori_loop(0, H // 4, spread, jnp.zeros((8, C), F32)), axis=0, keepdims=True)

        def one(a, _):
            acc = jnp.zeros((3 * C, 3 * C), F32)
            for p in range(2):
                lhs = jnp.concatenate([x[p + a, b : b + H].reshape(H * W, C) for b in range(3)], axis=1)
                acc = acc + lax.dot_general(
                    lhs, wide[p], (((0,), (0,)), ((), ())), preferred_element_type=F32
                )
            for b in range(3):
                for j in range(3):
                    out[9 * a + 3 * b + j] = acc[b * C : (b + 1) * C, j * C : (j + 1) * C]
            return 0

        lax.fori_loop(0, 3, one, 0)
        first = lax.broadcasted_iota(jnp.int32, (C, C), 0) == 0
        out[27] = jnp.where(first, jnp.broadcast_to(acc_b, (C, C)), 0.0)
        keep[...] = out[pl.ds(idx[2] * 14, 14)].reshape(RH, C)
        away[...] = out[pl.ds((1 - idx[2]) * 14, 14)].reshape(RH, C).astype(BF)

    RH, RQ = ROWS // 2, ROWS // 8
    keep, away = call(
        kw,
        (sds((RH, C), F32), sds((RH, C))),
        [SMEM] + [VMEM] * 5,
        [
            pltpu.VMEM((2, H, W, C), BF),
            pltpu.VMEM((2, H * W, 3 * C), BF),
            pltpu.VMEM((28, C, C), F32),
        ],
    )(idx, x_all, d_send[0], *d_got)

    recv = swap(away)

    def split(idx, keep, recv, mine, q1, q2, q3, buf):
        x = idx[1] % 4
        buf[...] = keep[...].reshape(4, RQ, C) + recv[...].reshape(4, RQ, C).astype(F32)
        mine[...] = buf[x]
        for k, q in enumerate((q1, q2, q3), 1):
            q[...] = buf[x ^ k].astype(BF)

    quart = sds((RQ, C))
    q, *qs = call(
        split, (sds((RQ, C), F32), quart, quart, quart), [SMEM, VMEM, VMEM], [pltpu.VMEM((4, RQ, C), F32)]
    )(idx, keep, recv)
    xs = three(xdep, [None, *qs])
    for v in xs:
        q = q + v.astype(F32)
    q = q.astype(BF)
    ys = three(ydep, [q] * 4)

    def ordered(idx, q0, q1, q2, q3, out, buf):
        y = idx[1] // 4
        for k, r in enumerate((q0, q1, q2, q3)):
            buf[k] = r[...].astype(F32)
        acc = buf[y]
        for j in range(1, 4):
            acc = acc + buf[y ^ j]
        out[...] = acc.astype(BF)

    q = call(ordered, sds((RQ, C)), [SMEM] + [VMEM] * 4, [pltpu.VMEM((4, RQ, C), F32)], VMEM)(idx, q, *ys)
    qs = [q] + three(xdep, [q] * 4)

    others = [swap(v) for v in qs]

    def fill(buf, x, pieces):
        for k, q in enumerate(pieces):
            buf[pl.ds(pl.multiple_of((x ^ k) * RQ, 8), RQ)] = q[...].astype(F32) * grad_scale

    def place(idx, a0, a1, a2, a3, b0, b1, b2, b3, q0, q1, q2, q3, oa, ob, w_out, b_own, buf, sem):
        copies = []
        for k, (va, vb) in enumerate(((a0, b0), (a1, b1), (a2, b2), (a3, b3))):
            row = (idx[0] ^ k) * R
            copies.append(pltpu.make_async_copy(va.at[4:6], oa.at[:, pl.ds(row, R)], sem.at[2 * k]))
            copies.append(pltpu.make_async_copy(vb, ob.at[:, pl.ds(row, R)], sem.at[2 * k + 1]))
        for cp in copies:
            cp.start()
        fill(buf, idx[1] % 4, (q0, q1, q2, q3))
        b_own[...] = buf[TAP - RH : TAP - RH + 8]
        for c_, n in ((0, RH), (1, TAP - RH)):

            @pl.when(idx[2] == c_)
            def _():
                cp = pltpu.make_async_copy(
                    buf.at[pl.ds(0, n)], w_out.at[pl.ds(c_ * RH, n)], sem.at[8]
                )
                cp.start()
                cp.wait()

        for cp in copies:
            cp.wait()

    full = sds((2, H, W, C))
    out_h, out_g, w_part, b_own = call(
        place,
        (full, full, sds((TAP, C), F32), sds((8, C), F32)),
        [SMEM] + [ANY] * 8 + [VMEM] * 4,
        [pltpu.VMEM((RH, C), F32), pltpu.SemaphoreType.DMA((9,))],
        (ANY, ANY, ANY, VMEM),
    )(idx, h_own, *h_got, g_send[0], *g_got, *qs)

    def finish(idx, q0, q1, q2, q3, b_own, w_in, w_out, b_out, buf, sem):
        parts = 4
        row = TAP - RH
        c_ = idx[2]
        step = RH // parts
        fill(buf, idx[1] % 4, (q0, q1, q2, q3))
        for i in range(parts):
            n = min(step, row - i * step)

            @pl.when(c_ == 1)
            def _():
                pltpu.make_async_copy(
                    buf.at[pl.ds(i * step, step)], w_out.at[pl.ds(i * step, step)], sem.at[i]
                ).start()

            @pl.when(c_ == 0)
            def _():
                pltpu.make_async_copy(
                    buf.at[pl.ds(i * step, n)], w_out.at[pl.ds(RH + i * step, n)], sem.at[i]
                ).start()

        b_out[...] = jnp.where(c_ == 1, b_own[...], buf[row : row + 8])[0:1]
        for i in range(parts):
            n = min(step, row - i * step)

            @pl.when(c_ == 1)
            def _():
                pltpu.make_async_copy(
                    buf.at[pl.ds(i * step, step)], w_out.at[pl.ds(i * step, step)], sem.at[i]
                ).wait()

            @pl.when(c_ == 0)
            def _():
                pltpu.make_async_copy(
                    buf.at[pl.ds(i * step, n)], w_out.at[pl.ds(RH + i * step, n)], sem.at[i]
                ).wait()

    w_grad, b_grad = pl.pallas_call(
        finish,
        name="finish",
        grid=(1,),
        out_shape=(sds((TAP, C), F32), sds((1, C), F32)),
        in_specs=[SMEM] + [VMEM] * 5 + [ANY],
        out_specs=(ANY, VMEM),
        scratch_shapes=[pltpu.VMEM((RH, C), F32), pltpu.SemaphoreType.DMA((4,))],
        input_output_aliases={6: 0},
        compiler_params=pltpu.CompilerParams(vmem_limit_bytes=20 * 1024 * 1024),
    )(idx, *others, b_own, w_part)
    return out_h[None, None], out_g[None, None], w_grad[None], b_grad


def solution(mesh):
    in_specs = (
        P("dp", "depth", None, None, None),
        P("section", None, None),
        P("section", None),
        P("dp", "depth", None, None, None),
    )
    out_specs = (
        P("section", "dp", "depth", None, None, None),
        P("section", "dp", "depth", None, None, None),
        P("section", None, None),
        P("section", None),
    )

    return jax.shard_map(shards, mesh=mesh, in_specs=in_specs, out_specs=out_specs, check_vma=False)
```

```python
import math

import jax
import jax.numpy as jnp
from jax import lax
from jax.experimental import pallas as pl
from jax.experimental.pallas import tpu as pltpu
from jax.sharding import PartitionSpec as P


BF = jnp.bfloat16
F32 = jnp.float32

VMEM = pl.BlockSpec(memory_space=pltpu.VMEM)
ANY = pl.BlockSpec(memory_space=pl.ANY)
HBM = pl.BlockSpec(memory_space=pltpu.HBM)


def in_hbm(x):
    return pltpu.with_memory_space_constraint(x, pltpu.HBM)


def sds(shape, dtype=BF):
    return jax.ShapeDtypeStruct(shape, dtype)


def placed(body):
    def inner(*refs):
        return body(tuple(lax.axis_index(name) for name in ("section", "depth", "dp")), *refs)

    return inner


def call(body, out, in_specs, scratch, out_specs=None):
    return pl.pallas_call(
        body,
        grid=(1,),
        out_shape=out,
        in_specs=in_specs,
        out_specs=out_specs if out_specs is not None else jax.tree.map(lambda _: VMEM, out),
        scratch_shapes=scratch,
        compiler_params=pltpu.CompilerParams(vmem_limit_bytes=20 * 1024 * 1024),
    )


def column(w_ref, C=128):
    return jnp.concatenate(
        [
            jnp.concatenate([w_ref[(3 * k + c) * C : (3 * k + c + 1) * C] for c in range(3)], axis=1)
            for k in range(9)
        ],
        axis=0,
    )


def conv_plane(x_ref, p, wide, nr):
    W, C = x_ref.shape[2], x_ref.shape[3]
    m = nr * W
    lhs = jnp.concatenate(
        [x_ref[p + a, b : b + nr].reshape(m, C) for a in range(3) for b in range(3)], axis=1
    )
    y = jnp.dot(lhs, wide, preferred_element_type=F32)
    x_pos = lax.broadcasted_iota(jnp.int32, (m, C), 0) % W
    left = jnp.where(x_pos == 0, 0.0, pltpu.roll(y[:, :C], 1, 0))
    right = jnp.where(x_pos == W - 1, 0.0, pltpu.roll(y[:, 2 * C :], m - 1, 0))
    return y[:, C : 2 * C] + left + right


def inside(nr, W, C, first_row, H, plane, D):
    row = first_row + lax.broadcasted_iota(jnp.int32, (nr * W, C), 0) // W
    return (row >= 0) & (row < H) & (plane >= 0) & (plane < D)


def slope(pre):
    q = jax.nn.sigmoid(pre)
    return q * (1.0 + pre * (1.0 - q))


def assemble(dst, far, own, near, d, last):
    odd = d % 2
    zero = jnp.zeros(far.shape, BF)
    dst[pl.ds(4 * odd, 2)] = jnp.where((d > 0) & (d < last), far[...], zero)
    dst[2:4] = own[...]
    dst[pl.ds(4 - 4 * odd, 2)] = near[...]


def load_layer(s, c, t, own, got, swp, dst, rows):
    k = (s + 4 - t) % 4

    @pl.when(k == 0)
    def _():
        dst[...] = own[...]

    for i in range(3):

        @pl.when(k == i + 1)
        def _():
            for j in range(2):
                dst[pl.ds(pl.multiple_of((2 * c + j) * rows, 16), rows)] = got[2 * i + j][0:rows]
                dst[pl.ds(pl.multiple_of((2 - 2 * c + j) * rows, 16), rows)] = swp[2 * i + j][0:rows]


def bias_of(s, t, own_bias, got, rows):
    k = (s + 4 - t) % 4
    row = own_bias[0:1].astype(F32)
    for i in range(3):
        row = jnp.where(k == i + 1, got[2 * i][rows : rows + 1].astype(F32), row)
    return row


def shards(volume, weights, biases, cotangent):
    n_sec = lax.axis_size("section")
    n_dep = lax.axis_size("depth")
    n_dp = lax.axis_size("dp")
    assert n_sec == 4 and n_dep == 16 and n_dp == 2
    PL, H, W, C = volume.shape[1:]
    assert PL == 2
    R = H // n_sec
    D = PL * n_dep
    last = n_dep - 1
    grad_scale = 1.0 / math.sqrt(n_dp * D * H * W)
    TAP = 27 * C
    HALF = TAP // 2
    QR = HALF // 2
    QB = QR + 16

    def sec(v, k):
        return lax.ppermute(v, "section", [(i, i ^ k) for i in range(n_sec)])

    def three(send, values):
        got = {}
        for k in (2, 1, 3):
            got[k] = send(values[k], k)
        return [got[k] for k in (1, 2, 3)]

    def both(v):
        result = []
        for first in (1, 0):
            pairs = [(i, i + 1) for i in range(first, n_dep - 1, 2)]
            result.append(lax.ppermute(v, "depth", pairs + [(b, a) for a, b in pairs]))
        return result

    def swap(v):
        return lax.ppermute(v, "dp", [(0, 1), (1, 0)])

    def xdep(v, k):
        return lax.ppermute(v, "depth", [(i, i ^ k) for i in range(n_dep)])

    def ydep(v, k):
        return lax.ppermute(v, "depth", [(i, i ^ (4 * k)) for i in range(n_dep)])

    own_w = weights[0]

    def prepare(w, b, part_a, part_b, own_b, row, sem):
        c_ = lax.axis_index("dp")
        pulls = [
            pltpu.make_async_copy(w.at[2 * c_], part_a.at[pl.ds(0, QR)], sem.at[0]),
            pltpu.make_async_copy(w.at[2 * c_ + 1], part_b.at[pl.ds(0, QR)], sem.at[1]),
            pltpu.make_async_copy(b, row, sem.at[2]),
        ]
        for cp in pulls:
            cp.start()
        for cp in pulls:
            cp.wait()
        bias = jnp.broadcast_to(row[...], (16, C))
        part_a[QR:] = bias
        part_b[QR:] = bias
        own_b[...] = bias

    part_a, part_b, own_b = call(
        prepare,
        (sds((QB, C)), sds((QB, C)), sds((16, C))),
        [HBM, HBM],
        [pltpu.VMEM((1, C), BF), pltpu.SemaphoreType.DMA((3,))],
    )(in_hbm(own_w.reshape(4, QR, C)), in_hbm(biases))

    def rows_of(vol, h0, pad, sem):
        pull = pltpu.make_async_copy(vol, pad.at[:, pl.ds(8, H)], sem)
        pull.start()
        pad[:, 0:8] = jnp.zeros((PL, 8, W, C), BF)
        pad[:, H + 8 :] = jnp.zeros((PL, 8, W, C), BF)
        pull.wait()
        h0[...] = pad[:, pl.ds(lax.axis_index("section") * R, R + 16)]

    h0 = call(
        rows_of, sds((PL, R + 16, W, C)), [HBM], [pltpu.VMEM((PL, H + 16, W, C), BF), pltpu.SemaphoreType.DMA], VMEM
    )(in_hbm(volume[0]))
    h0_lo, h0_hi = both(h0)

    def ring(v, k):
        return lax.ppermute(v, "section", [(i, (i + k) % n_sec) for i in range(n_sec)])

    a1, b3 = ring(part_a, 1), ring(part_b, 3)
    b1, a3 = ring(part_b, 1), ring(part_a, 3)
    a2, b2 = ring(a1, 1), ring(b3, 3)
    got = (a1, b1, a2, b2, a3, b3)
    swapped = [swap(g) for g in got]
    all_w = (own_w, *got, *swapped)
    W_SPECS = [VMEM] * 13

    @placed
    def turn(idx, own, *rest):
        got_, swp_, (*outs, buf) = rest[:6], rest[6:12], rest[12:]
        for t in (3, 2, 1, 0):
            load_layer(idx[0], idx[2], t, own, got_, swp_, buf.at[t], QR)

            def one(j, _):
                outs[t][pl.ds(pl.multiple_of(j * C, C), C)] = buf[t, pl.ds(pl.multiple_of((26 - j) * C, C), C)].T
                return 0

            lax.fori_loop(0, 27, one, 0, unroll=3)

    @placed
    def k1(idx, own, lo, hi, ow, *rest):
        got_, swp_, rest = rest[:6], rest[6:12], rest[12:]
        ob, h0e, pre0, h1e, pre1, h2, x, h1, w = rest
        s_, d_ = idx[0], idx[1]
        for t in range(2):
            load_layer(s_, idx[2], t, ow, got_, swp_, w.at[t], QR)
        assemble(x, lo, own, hi, d_, last)
        h0e[...] = x[1:5, 8 : 8 + R]
        b0 = bias_of(s_, 0, ob, got_, QR)

        def one(p, _):
            pre = conv_plane(x, p, column(w.at[0]), R + 14) + b0
            h = jnp.where(inside(R + 14, W, C, s_ * R - 7, H, 2 * d_ - 1 + p, D), pre * jax.nn.sigmoid(pre), 0.0)
            h = h.astype(BF).reshape(R + 14, W, C)
            h1[p] = h
            h1e[p] = h[7 : 7 + R]
            pre0[p] = pre[6 * W : (16 + 0) * W].astype(BF).reshape(R + 2, W, C)
            return 0

        lax.fori_loop(0, 4, one, 0)
        b1 = bias_of(s_, 1, ob, got_, QR)

        def two(p, _):
            pre = conv_plane(h1, p, column(w.at[1]), R + 12) + b1
            h = jnp.where(inside(R + 12, W, C, s_ * R - 6, H, 2 * d_ + p, D), pre * jax.nn.sigmoid(pre), 0.0)
            h2[p] = h.astype(BF).reshape(R + 12, W, C)
            pre1[p] = pre[4 * W : 16 * W].astype(BF).reshape(R + 4, W, C)
            return 0

        lax.fori_loop(0, 2, two, 0)

    h0e, pre0, h1e, pre1, h2 = call(
        k1,
        (
            sds((4, R, W, C)),
            sds((4, R + 2, W, C)),
            sds((4, R, W, C)),
            sds((2, R + 4, W, C)),
            sds((2, R + 12, W, C)),
        ),
        [VMEM, VMEM, VMEM] + W_SPECS + [VMEM],
        [
            pltpu.VMEM((6, R + 16, W, C), BF),
            pltpu.VMEM((4, R + 14, W, C), BF),
            pltpu.VMEM((2, TAP, C), BF),
        ],
    )(h0, h0_lo, h0_hi, *all_w, own_b)

    h2_lo, h2_hi = both(h2)

    wturn = call(turn, (sds((TAP, C)),) * 4, W_SPECS, [pltpu.VMEM((4, TAP, C), BF)])(*all_w)
    h2_lo, h2_hi, *wturn = lax.optimization_barrier((h2_lo, h2_hi, *wturn))

    @placed
    def k2(idx, own, lo, hi, ow, *rest):
        got_, swp_, rest = rest[:6], rest[6:12], rest[12:]
        ob, cot, h2e, pre2, h3e, h4, d3, x, h3, w, gpad = rest
        s_, d_ = idx[0], idx[1]
        for t in range(2):
            load_layer(s_, idx[2], t + 2, ow, got_, swp_, w.at[t], QR)
        assemble(x, lo, own, hi, d_, last)
        h2e[...] = x[1:5, 6 : 6 + R]
        gpad[:, 4 : 4 + H] = cot[...]
        b0 = bias_of(s_, 2, ob, got_, QR)

        def one(p, _):
            pre = conv_plane(x, p, column(w.at[0]), R + 10) + b0
            h = jnp.where(inside(R + 10, W, C, s_ * R - 5, H, 2 * d_ - 1 + p, D), pre * jax.nn.sigmoid(pre), 0.0)
            h = h.astype(BF).reshape(R + 10, W, C)
            h3[p] = h
            h3e[p] = h[5 : 5 + R]
            pre2[p] = pre[2 * W : 16 * W].astype(BF).reshape(R + 6, W, C)
            return 0

        lax.fori_loop(0, 4, one, 0)
        b1 = bias_of(s_, 3, ob, got_, QR)

        def two(p, _):
            pre = conv_plane(h3, p, column(w.at[1]), R + 8) + b1
            h = (pre * jax.nn.sigmoid(pre)).astype(BF).reshape(R + 8, W, C)
            h4[p] = h[4 : 4 + R]
            g = gpad[p, pl.ds(s_ * R, R + 8)].reshape((R + 8) * W, C).astype(F32)
            dl = g * slope(pre.astype(BF).astype(F32))
            dl = jnp.where(inside(R + 8, W, C, s_ * R - 4, H, 2 * d_ + p, D), dl, 0.0)
            d3[p] = dl.astype(BF).reshape(R + 8, W, C)
            return 0

        lax.fori_loop(0, 2, two, 0)

    h2e, pre2, h3e, h4, d3 = call(
        k2,
        (
            sds((4, R, W, C)),
            sds((4, R + 6, W, C)),
            sds((4, R, W, C)),
            sds((2, R, W, C)),
            sds((2, R + 8, W, C)),
        ),
        [VMEM, VMEM, VMEM] + W_SPECS + [VMEM] + [VMEM],
        [
            pltpu.VMEM((6, R + 12, W, C), BF),
            pltpu.VMEM((4, R + 10, W, C), BF),
            pltpu.VMEM((2, TAP, C), BF),
            pltpu.VMEM((PL, H + 8, W, C), BF),
        ],
    )(h2, h2_lo, h2_hi, *all_w, own_b, cotangent[0])

    d3_lo, d3_hi = both(d3)

    @placed
    def pack(idx, x0, x1, x2, x3, x4, own, a1, a2, a3):
        xs = (x0, x1, x2, x3)
        for k, out in enumerate((own, a1, a2, a3)):
            for t in range(4):

                @pl.when((idx[0] ^ k) == t)
                def _():
                    out[0:4] = xs[t][...]
                    out[4:6] = x4[...] if t == 3 else xs[t + 1][1:3]

    six = sds((6, R, W, C))
    h_own, *h_send = call(pack, (six,) * 4, [VMEM] * 5, [])(h0e, h1e, h2e, h3e, h4)
    h_got = [sec(h_send[k - 1], k) for k in (1, 2, 3)]

    piece = sds((2, R, W, C))

    def delta_of(g, pre, p, n, first_row, plane):
        dl = g.astype(F32) * slope(pre[p].reshape(n * W, C).astype(F32))
        dl = jnp.where(inside(n, W, C, first_row, H, plane, D), dl, 0.0)
        return dl.astype(BF).reshape(n, W, C)

    def send_all(s_, outs, values):
        for k in range(4):
            for t in range(4):

                @pl.when((s_ ^ k) == t)
                def _():
                    outs[k][...] = values[t]()

    @placed
    def k3(idx, own, lo, hi, wa, wb, pre_a, pre_b, ga, da, gb, db, x, dbuf):
        s_, d_ = idx[0], idx[1]
        assemble(x, lo, own, hi, d_, last)

        def one(p, _):
            g = conv_plane(x, p, column(wa), R + 6).astype(BF)
            dl = delta_of(g, pre_a, p, R + 6, s_ * R - 3, 2 * d_ - 1 + p)
            dbuf[p] = dl

            @pl.when((p > 0) & (p < 3))
            def _():
                ga[p - 1] = g.reshape(R + 6, W, C)[3 : 3 + R]
                da[p - 1] = dl[3 : 3 + R]

            return 0

        lax.fori_loop(0, 4, one, 0)

        def two(p, _):
            g = conv_plane(dbuf, p, column(wb), R + 4).astype(BF)
            gb[p] = g.reshape(R + 4, W, C)[2 : 2 + R]
            db[p] = delta_of(g, pre_b, p, R + 4, s_ * R - 2, 2 * d_ + p)
            return 0

        lax.fori_loop(0, 2, two, 0)

    g3, d2, g2, d1 = call(
        k3,
        (piece, piece, piece, sds((2, R + 4, W, C))),
        [VMEM, VMEM, VMEM, VMEM, VMEM, VMEM, VMEM],
        [pltpu.VMEM((6, R + 8, W, C), BF), pltpu.VMEM((4, R + 6, W, C), BF)],
    )(d3, d3_lo, d3_hi, wturn[3], wturn[2], pre2, pre1)
    d1_lo, d1_hi = both(d1)

    @placed
    def k4a(idx, own, lo, hi, wa, pre_a, e1, e2, e3, g1, dbuf, *rest):
        *sends, x = rest
        s_, d_ = idx[0], idx[1]
        assemble(x, lo, own, hi, d_, last)

        def one(p, _):
            g = conv_plane(x, p, column(wa), R + 2).astype(BF)
            dbuf[p] = delta_of(g, pre_a, p, R + 2, s_ * R - 1, 2 * d_ - 1 + p)

            @pl.when((p > 0) & (p < 3))
            def _():
                g1[p - 1] = g.reshape(R + 2, W, C)[1 : 1 + R]

            return 0

        lax.fori_loop(0, 4, one, 0)
        send_all(
            s_,
            sends,
            (
                lambda: dbuf[1:3, 1 : 1 + R],
                lambda: e1[:, 2 : 2 + R],
                lambda: e2[...],
                lambda: e3[:, 4 : 4 + R],
            ),
        )

    g1, d0, *d_send = call(
        k4a,
        (piece, sds((4, R + 2, W, C))) + (piece,) * 4,
        [VMEM, VMEM, VMEM, VMEM, VMEM, VMEM, VMEM, VMEM],
        [pltpu.VMEM((6, R + 4, W, C), BF)],
    )(d1, d1_lo, d1_hi, wturn[1], pre0, d1, d2, d3)
    d_got = three(sec, d_send)

    @placed
    def k4b(idx, dbuf, wb, g1, g2, g3, *rest):
        *sends, g0 = rest

        def two(p, _):
            g0[p] = conv_plane(dbuf, p, column(wb), R).astype(BF).reshape(R, W, C)
            return 0

        lax.fori_loop(0, 2, two, 0)
        send_all(idx[0], sends, (lambda: g0[...], lambda: g1[...], lambda: g2[...], lambda: g3[...]))

    g_send = call(
        k4b, (piece,) * 4, [VMEM, VMEM, VMEM, VMEM, VMEM], [pltpu.VMEM(piece.shape, BF)]
    )(d0, wturn[0], g1, g2, g3)
    g_got = []
    for k in (1, 2, 3):
        g_got.append(sec(g_send[k], k))

    @placed
    def kx(idx, x0, x1, x2, x3, x):
        x[:, 0] = jnp.zeros((4, W, C), BF)
        x[:, H + 1] = jnp.zeros((4, W, C), BF)
        for k, xs in enumerate((x0, x1, x2, x3)):
            x[:, pl.ds((idx[0] ^ k) * R + 1, R)] = xs[0:4]

    x_all = call(kx, sds((4, H + 2, W, C)), [VMEM] * 4, [], VMEM)(h_own, *h_got)

    ROWS = TAP + C

    @placed
    def kw(idx, x, e0, e1, e2, e3, keep, away, dl, wide, out):
        s_ = idx[0]
        for k, es in enumerate((e0, e1, e2, e3)):
            dl[:, pl.ds((s_ ^ k) * R, R)] = es[...]
        m = 4 * W
        pos = lax.broadcasted_iota(jnp.int32, (m, C), 0) % W

        def spread(i, acc):
            for p in range(2):
                v16 = dl[p, pl.ds(i * 4, 4)].reshape(m, C)
                v = v16.astype(F32)
                at = pl.ds(pl.multiple_of(i * m, m), m)
                wide[p, at, 0:C] = jnp.where(pos == W - 1, 0.0, pltpu.roll(v, m - 1, 0)).astype(BF)
                wide[p, at, C : 2 * C] = v16
                wide[p, at, 2 * C :] = jnp.where(pos == 0, 0.0, pltpu.roll(v, 1, 0)).astype(BF)
                acc = acc + jnp.sum(v.reshape(m // 8, 8, C), axis=0)
            return acc

        acc_b = jnp.sum(lax.fori_loop(0, H // 4, spread, jnp.zeros((8, C), F32)), axis=0, keepdims=True)

        def one(a, _):
            acc = jnp.zeros((3 * C, 3 * C), F32)
            for p in range(2):
                lhs = jnp.concatenate([x[p + a, b : b + H].reshape(H * W, C) for b in range(3)], axis=1)
                acc = acc + lax.dot_general(
                    lhs, wide[p], (((0,), (0,)), ((), ())), preferred_element_type=F32
                )
            for b in range(3):
                for j in range(3):
                    out[9 * a + 3 * b + j] = acc[b * C : (b + 1) * C, j * C : (j + 1) * C]
            return 0

        lax.fori_loop(0, 3, one, 0)
        first = lax.broadcasted_iota(jnp.int32, (C, C), 0) == 0
        out[27] = jnp.where(first, jnp.broadcast_to(acc_b, (C, C)), 0.0)
        keep[...] = out[pl.ds(idx[2] * 14, 14)].reshape(RH, C)
        away[...] = out[pl.ds((1 - idx[2]) * 14, 14)].reshape(RH, C).astype(BF)

    RH, RQ = ROWS // 2, ROWS // 8
    keep, away = call(
        kw,
        (sds((RH, C), F32), sds((RH, C))),
        [VMEM] * 5,
        [
            pltpu.VMEM((2, H, W, C), BF),
            pltpu.VMEM((2, H * W, 3 * C), BF),
            pltpu.VMEM((28, C, C), F32),
        ],
    )(x_all, d_send[0], *d_got)

    recv = swap(away)

    @placed
    def split(idx, keep, recv, mine, q1, q2, q3, buf):
        x = idx[1] % 4
        buf[...] = keep[...].reshape(4, RQ, C) + recv[...].reshape(4, RQ, C).astype(F32)
        mine[...] = buf[x]
        for k, q in enumerate((q1, q2, q3), 1):
            q[...] = buf[x ^ k].astype(BF)

    quart = sds((RQ, C))
    q, *qs = call(
        split, (sds((RQ, C), F32), quart, quart, quart), [VMEM, VMEM], [pltpu.VMEM((4, RQ, C), F32)]
    )(keep, recv)
    xs = three(xdep, [None, *qs])
    for v in xs:
        q = q + v.astype(F32)
    q = q.astype(BF)
    ys = three(ydep, [q] * 4)

    @placed
    def ordered(idx, q0, q1, q2, q3, out, buf):
        y = idx[1] // 4
        for k, r in enumerate((q0, q1, q2, q3)):
            buf[k] = r[...].astype(F32)
        acc = buf[y]
        for j in range(1, 4):
            acc = acc + buf[y ^ j]
        out[...] = acc.astype(BF)

    q = call(ordered, sds((RQ, C)), [VMEM] * 4, [pltpu.VMEM((4, RQ, C), F32)], VMEM)(q, *ys)
    qs = [q] + three(xdep, [q] * 4)

    others = [swap(v) for v in qs]

    def fill(buf, x, pieces):
        for k, q in enumerate(pieces):
            buf[pl.ds(pl.multiple_of((x ^ k) * RQ, 8), RQ)] = q[...].astype(F32) * grad_scale

    @placed
    def place(idx, a0, a1, a2, a3, b0, b1, b2, b3, q0, q1, q2, q3, oa, ob, w_out, b_own, buf, sem):
        copies = []
        for k, (va, vb) in enumerate(((a0, b0), (a1, b1), (a2, b2), (a3, b3))):
            row = (idx[0] ^ k) * R
            copies.append(pltpu.make_async_copy(va.at[4:6], oa.at[:, pl.ds(row, R)], sem.at[2 * k]))
            copies.append(pltpu.make_async_copy(vb, ob.at[:, pl.ds(row, R)], sem.at[2 * k + 1]))
        for cp in copies:
            cp.start()
        fill(buf, idx[1] % 4, (q0, q1, q2, q3))
        b_own[...] = buf[TAP - RH : TAP - RH + 8]
        for c_, n in ((0, RH), (1, TAP - RH)):

            @pl.when(idx[2] == c_)
            def _():
                cp = pltpu.make_async_copy(
                    buf.at[pl.ds(0, n)], w_out.at[pl.ds(c_ * RH, n)], sem.at[8]
                )
                cp.start()
                cp.wait()

        for cp in copies:
            cp.wait()

    full = sds((2, H, W, C))
    out_h, out_g, w_part, b_own = call(
        place,
        (full, full, sds((TAP, C), F32), sds((8, C), F32)),
        [ANY] * 8 + [VMEM] * 4,
        [pltpu.VMEM((RH, C), F32), pltpu.SemaphoreType.DMA((9,))],
        (ANY, ANY, ANY, VMEM),
    )(h_own, *h_got, g_send[0], *g_got, *qs)

    @placed
    def finish(idx, q0, q1, q2, q3, b_own, w_in, w_out, b_out, buf, sem):
        parts = 4
        row = TAP - RH
        c_ = idx[2]
        step = RH // parts
        fill(buf, idx[1] % 4, (q0, q1, q2, q3))
        for i in range(parts):
            n = min(step, row - i * step)

            @pl.when(c_ == 1)
            def _():
                pltpu.make_async_copy(
                    buf.at[pl.ds(i * step, step)], w_out.at[pl.ds(i * step, step)], sem.at[i]
                ).start()

            @pl.when(c_ == 0)
            def _():
                pltpu.make_async_copy(
                    buf.at[pl.ds(i * step, n)], w_out.at[pl.ds(RH + i * step, n)], sem.at[i]
                ).start()

        b_out[...] = jnp.where(c_ == 1, b_own[...], buf[row : row + 8])[0:1]
        for i in range(parts):
            n = min(step, row - i * step)

            @pl.when(c_ == 1)
            def _():
                pltpu.make_async_copy(
                    buf.at[pl.ds(i * step, step)], w_out.at[pl.ds(i * step, step)], sem.at[i]
                ).wait()

            @pl.when(c_ == 0)
            def _():
                pltpu.make_async_copy(
                    buf.at[pl.ds(i * step, n)], w_out.at[pl.ds(RH + i * step, n)], sem.at[i]
                ).wait()

    w_grad, b_grad = pl.pallas_call(
        finish,
        name="finish",
        grid=(1,),
        out_shape=(sds((TAP, C), F32), sds((1, C), F32)),
        in_specs=[VMEM] * 5 + [ANY],
        out_specs=(ANY, VMEM),
        scratch_shapes=[pltpu.VMEM((RH, C), F32), pltpu.SemaphoreType.DMA((4,))],
        input_output_aliases={5: 0},
        compiler_params=pltpu.CompilerParams(vmem_limit_bytes=20 * 1024 * 1024),
    )(*others, b_own, w_part)
    return out_h[None, None], out_g[None, None], w_grad[None], b_grad


def solution(mesh):
    in_specs = (
        P("dp", "depth", None, None, None),
        P("section", None, None),
        P("section", None),
        P("dp", "depth", None, None, None),
    )
    out_specs = (
        P("section", "dp", "depth", None, None, None),
        P("section", "dp", "depth", None, None, None),
        P("section", None, None),
        P("section", None),
    )

    return jax.shard_map(shards, mesh=mesh, in_specs=in_specs, out_specs=out_specs, check_vma=False)
```

```python
import math

import jax
import jax.numpy as jnp
from jax import lax
from jax.experimental import pallas as pl
from jax.experimental.pallas import tpu as pltpu
from jax.sharding import PartitionSpec as P


BF = jnp.bfloat16
F32 = jnp.float32

VMEM = pl.BlockSpec(memory_space=pltpu.VMEM)
ANY = pl.BlockSpec(memory_space=pl.ANY)
HBM = pl.BlockSpec(memory_space=pltpu.HBM)


def in_hbm(x):
    return pltpu.with_memory_space_constraint(x, pltpu.HBM)


def sds(shape, dtype=BF):
    return jax.ShapeDtypeStruct(shape, dtype)


def placed(body):
    def inner(*refs):
        return body(tuple(lax.axis_index(name) for name in ("section", "depth", "dp")), *refs)

    return inner


def call(body, out, in_specs, scratch, out_specs=None):
    return pl.pallas_call(
        body,
        grid=(1,),
        out_shape=out,
        in_specs=in_specs,
        out_specs=out_specs if out_specs is not None else jax.tree.map(lambda _: VMEM, out),
        scratch_shapes=scratch,
        compiler_params=pltpu.CompilerParams(vmem_limit_bytes=20 * 1024 * 1024),
    )


def column(w_ref, C=128):
    return jnp.concatenate(
        [
            jnp.concatenate([w_ref[(3 * k + c) * C : (3 * k + c + 1) * C] for c in range(3)], axis=1)
            for k in range(9)
        ],
        axis=0,
    )


def conv_plane(x_ref, p, wide, nr):
    W, C = x_ref.shape[2], x_ref.shape[3]
    m = nr * W
    lhs = jnp.concatenate(
        [x_ref[p + a, b : b + nr].reshape(m, C) for a in range(3) for b in range(3)], axis=1
    )
    y = jnp.dot(lhs, wide, preferred_element_type=F32)
    x_pos = lax.broadcasted_iota(jnp.int32, (m, C), 0) % W
    left = jnp.where(x_pos == 0, 0.0, pltpu.roll(y[:, :C], 1, 0))
    right = jnp.where(x_pos == W - 1, 0.0, pltpu.roll(y[:, 2 * C :], m - 1, 0))
    return y[:, C : 2 * C] + left + right


def inside(nr, W, C, first_row, H, plane, D):
    row = first_row + lax.broadcasted_iota(jnp.int32, (nr * W, C), 0) // W
    return (row >= 0) & (row < H) & (plane >= 0) & (plane < D)


def slope(pre):
    q = jax.nn.sigmoid(pre)
    return q * (1.0 + pre * (1.0 - q))


def assemble(dst, far, own, near, d, last):
    odd = d % 2
    zero = jnp.zeros(far.shape, BF)
    dst[pl.ds(4 * odd, 2)] = jnp.where((d > 0) & (d < last), far[...], zero)
    dst[2:4] = own[...]
    dst[pl.ds(4 - 4 * odd, 2)] = near[...]


def load_layer(s, c, t, own, got, swp, dst, rows):
    k = (s + 4 - t) % 4

    @pl.when(k == 0)
    def _():
        dst[...] = own[...]

    for i in range(3):

        @pl.when(k == i + 1)
        def _():
            for j in range(2):
                dst[pl.ds(pl.multiple_of((2 * c + j) * rows, 16), rows)] = got[2 * i + j][0:rows]
                dst[pl.ds(pl.multiple_of((2 - 2 * c + j) * rows, 16), rows)] = swp[2 * i + j][0:rows]


def bias_of(s, t, own_bias, got, rows):
    k = (s + 4 - t) % 4
    row = own_bias[0:1].astype(F32)
    for i in range(3):
        row = jnp.where(k == i + 1, got[2 * i][rows : rows + 1].astype(F32), row)
    return row


def shards(volume, weights, biases, cotangent):
    n_sec = lax.axis_size("section")
    n_dep = lax.axis_size("depth")
    n_dp = lax.axis_size("dp")
    assert n_sec == 4 and n_dep == 16 and n_dp == 2
    PL, H, W, C = volume.shape[1:]
    assert PL == 2
    R = H // n_sec
    D = PL * n_dep
    last = n_dep - 1
    grad_scale = 1.0 / math.sqrt(n_dp * D * H * W)
    TAP = 27 * C
    HALF = TAP // 2
    QR = HALF // 2
    QB = QR + 16

    def sec(v, k):
        return lax.ppermute(v, "section", [(i, i ^ k) for i in range(n_sec)])

    def three(send, values):
        got = {}
        for k in (2, 1, 3):
            got[k] = send(values[k], k)
        return [got[k] for k in (1, 2, 3)]

    def both(v):
        result = []
        for first in (1, 0):
            pairs = [(i, i + 1) for i in range(first, n_dep - 1, 2)]
            result.append(lax.ppermute(v, "depth", pairs + [(b, a) for a, b in pairs]))
        return result

    def swap(v):
        return lax.ppermute(v, "dp", [(0, 1), (1, 0)])

    def xdep(v, k):
        return lax.ppermute(v, "depth", [(i, i ^ k) for i in range(n_dep)])

    def ydep(v, k):
        return lax.ppermute(v, "depth", [(i, i ^ (4 * k)) for i in range(n_dep)])

    own_w = weights[0]

    def prepare(w, b, part_a, part_b, own_b, row, sem):
        c_ = lax.axis_index("dp")
        pulls = [
            pltpu.make_async_copy(w.at[2 * c_], part_a.at[pl.ds(0, QR)], sem.at[0]),
            pltpu.make_async_copy(w.at[2 * c_ + 1], part_b.at[pl.ds(0, QR)], sem.at[1]),
            pltpu.make_async_copy(b, row, sem.at[2]),
        ]
        for cp in pulls:
            cp.start()
        for cp in pulls:
            cp.wait()
        bias = jnp.broadcast_to(row[...], (16, C))
        part_a[QR:] = bias
        part_b[QR:] = bias
        own_b[...] = bias

    part_a, part_b, own_b = call(
        prepare,
        (sds((QB, C)), sds((QB, C)), sds((16, C))),
        [HBM, HBM],
        [pltpu.VMEM((1, C), BF), pltpu.SemaphoreType.DMA((3,))],
    )(in_hbm(own_w.reshape(4, QR, C)), in_hbm(biases))

    def rows_of(vol, h0, pad, sem):
        pull = pltpu.make_async_copy(vol, pad.at[:, pl.ds(8, H)], sem)
        pull.start()
        pad[:, 0:8] = jnp.zeros((PL, 8, W, C), BF)
        pad[:, H + 8 :] = jnp.zeros((PL, 8, W, C), BF)
        pull.wait()
        h0[...] = pad[:, pl.ds(lax.axis_index("section") * R, R + 16)]

    h0 = call(
        rows_of, sds((PL, R + 16, W, C)), [HBM], [pltpu.VMEM((PL, H + 16, W, C), BF), pltpu.SemaphoreType.DMA], VMEM
    )(in_hbm(volume[0]))
    h0_lo, h0_hi = both(h0)

    def ring(v, k):
        return lax.ppermute(v, "section", [(i, (i + k) % n_sec) for i in range(n_sec)])

    a1, b3 = ring(part_a, 1), ring(part_b, 3)
    b1, a3 = ring(part_b, 1), ring(part_a, 3)
    a2, b2 = ring(a1, 1), ring(b3, 3)
    got = (a1, b1, a2, b2, a3, b3)
    swapped = [swap(g) for g in got]
    all_w = (own_w, *got, *swapped)
    W_SPECS = [VMEM] * 13

    @placed
    def turn(idx, own, *rest):
        got_, swp_, (*outs, buf) = rest[:6], rest[6:12], rest[12:]
        for t in (3, 2, 1, 0):
            load_layer(idx[0], idx[2], t, own, got_, swp_, buf.at[t], QR)

            def one(j, _):
                outs[t][pl.ds(pl.multiple_of(j * C, C), C)] = buf[t, pl.ds(pl.multiple_of((26 - j) * C, C), C)].T
                return 0

            lax.fori_loop(0, 27, one, 0, unroll=3)

    @placed
    def k1(idx, own, lo, hi, ow, *rest):
        got_, swp_, rest = rest[:6], rest[6:12], rest[12:]
        ob, h0e, pre0, h1e, pre1, h2, x, h1, w = rest
        s_, d_ = idx[0], idx[1]
        for t in range(2):
            load_layer(s_, idx[2], t, ow, got_, swp_, w.at[t], QR)
        assemble(x, lo, own, hi, d_, last)
        h0e[...] = x[1:5, 8 : 8 + R]
        b0 = bias_of(s_, 0, ob, got_, QR)

        def one(p, _):
            pre = conv_plane(x, p, column(w.at[0]), R + 14) + b0
            h = jnp.where(inside(R + 14, W, C, s_ * R - 7, H, 2 * d_ - 1 + p, D), pre * jax.nn.sigmoid(pre), 0.0)
            h = h.astype(BF).reshape(R + 14, W, C)
            h1[p] = h
            h1e[p] = h[7 : 7 + R]
            pre0[p] = pre[6 * W : (16 + 0) * W].astype(BF).reshape(R + 2, W, C)
            return 0

        lax.fori_loop(0, 4, one, 0)
        b1 = bias_of(s_, 1, ob, got_, QR)

        def two(p, _):
            pre = conv_plane(h1, p, column(w.at[1]), R + 12) + b1
            h = jnp.where(inside(R + 12, W, C, s_ * R - 6, H, 2 * d_ + p, D), pre * jax.nn.sigmoid(pre), 0.0)
            h2[p] = h.astype(BF).reshape(R + 12, W, C)
            pre1[p] = pre[4 * W : 16 * W].astype(BF).reshape(R + 4, W, C)
            return 0

        lax.fori_loop(0, 2, two, 0)

    h0e, pre0, h1e, pre1, h2 = call(
        k1,
        (
            sds((4, R, W, C)),
            sds((4, R + 2, W, C)),
            sds((4, R, W, C)),
            sds((2, R + 4, W, C)),
            sds((2, R + 12, W, C)),
        ),
        [VMEM, VMEM, VMEM] + W_SPECS + [VMEM],
        [
            pltpu.VMEM((6, R + 16, W, C), BF),
            pltpu.VMEM((4, R + 14, W, C), BF),
            pltpu.VMEM((2, TAP, C), BF),
        ],
    )(h0, h0_lo, h0_hi, *all_w, own_b)

    h2_lo, h2_hi = both(h2)

    wturn = call(turn, (sds((TAP, C)),) * 4, W_SPECS, [pltpu.VMEM((4, TAP, C), BF)])(*all_w)
    h2_lo, h2_hi, *wturn = lax.optimization_barrier((h2_lo, h2_hi, *wturn))

    @placed
    def k2(idx, own, lo, hi, ow, *rest):
        got_, swp_, rest = rest[:6], rest[6:12], rest[12:]
        ob, cot, h2e, pre2, h3e, h4, d3, x, h3, w, gpad = rest
        s_, d_ = idx[0], idx[1]
        for t in range(2):
            load_layer(s_, idx[2], t + 2, ow, got_, swp_, w.at[t], QR)
        assemble(x, lo, own, hi, d_, last)
        h2e[...] = x[1:5, 6 : 6 + R]
        gpad[:, 4 : 4 + H] = cot[...]
        b0 = bias_of(s_, 2, ob, got_, QR)

        def one(p, _):
            pre = conv_plane(x, p, column(w.at[0]), R + 10) + b0
            h = jnp.where(inside(R + 10, W, C, s_ * R - 5, H, 2 * d_ - 1 + p, D), pre * jax.nn.sigmoid(pre), 0.0)
            h = h.astype(BF).reshape(R + 10, W, C)
            h3[p] = h
            h3e[p] = h[5 : 5 + R]
            pre2[p] = pre[2 * W : 16 * W].astype(BF).reshape(R + 6, W, C)
            return 0

        lax.fori_loop(0, 4, one, 0)
        b1 = bias_of(s_, 3, ob, got_, QR)

        def two(p, _):
            pre = conv_plane(h3, p, column(w.at[1]), R + 8) + b1
            h = (pre * jax.nn.sigmoid(pre)).astype(BF).reshape(R + 8, W, C)
            h4[p] = h[4 : 4 + R]
            g = gpad[p, pl.ds(s_ * R, R + 8)].reshape((R + 8) * W, C).astype(F32)
            dl = g * slope(pre.astype(BF).astype(F32))
            dl = jnp.where(inside(R + 8, W, C, s_ * R - 4, H, 2 * d_ + p, D), dl, 0.0)
            d3[p] = dl.astype(BF).reshape(R + 8, W, C)
            return 0

        lax.fori_loop(0, 2, two, 0)

    h2e, pre2, h3e, h4, d3 = call(
        k2,
        (
            sds((4, R, W, C)),
            sds((4, R + 6, W, C)),
            sds((4, R, W, C)),
            sds((2, R, W, C)),
            sds((2, R + 8, W, C)),
        ),
        [VMEM, VMEM, VMEM] + W_SPECS + [VMEM] + [VMEM],
        [
            pltpu.VMEM((6, R + 12, W, C), BF),
            pltpu.VMEM((4, R + 10, W, C), BF),
            pltpu.VMEM((2, TAP, C), BF),
            pltpu.VMEM((PL, H + 8, W, C), BF),
        ],
    )(h2, h2_lo, h2_hi, *all_w, own_b, cotangent[0])

    d3_lo, d3_hi = both(d3)

    @placed
    def pack(idx, x0, x1, x2, x3, x4, own, a1, a2, a3):
        xs = (x0, x1, x2, x3)
        for k, out in enumerate((own, a1, a2, a3)):
            for t in range(4):

                @pl.when((idx[0] ^ k) == t)
                def _():
                    out[0:4] = xs[t][...]
                    out[4:6] = x4[...] if t == 3 else xs[t + 1][1:3]

    six = sds((6, R, W, C))
    h_own, *h_send = call(pack, (six,) * 4, [VMEM] * 5, [])(h0e, h1e, h2e, h3e, h4)
    h_got = [sec(h_send[k - 1], k) for k in (1, 2, 3)]

    piece = sds((2, R, W, C))

    def delta_of(g, pre, p, n, first_row, plane):
        dl = g.astype(F32) * slope(pre[p].reshape(n * W, C).astype(F32))
        dl = jnp.where(inside(n, W, C, first_row, H, plane, D), dl, 0.0)
        return dl.astype(BF).reshape(n, W, C)

    def send_all(s_, outs, values):
        for k in range(4):
            for t in range(4):

                @pl.when((s_ ^ k) == t)
                def _():
                    outs[k][...] = values[t]()

    @placed
    def k3(idx, own, lo, hi, wa, wb, pre_a, pre_b, ga, da, gb, db, x, dbuf):
        s_, d_ = idx[0], idx[1]
        assemble(x, lo, own, hi, d_, last)

        def one(p, _):
            g = conv_plane(x, p, column(wa), R + 6).astype(BF)
            dl = delta_of(g, pre_a, p, R + 6, s_ * R - 3, 2 * d_ - 1 + p)
            dbuf[p] = dl

            @pl.when((p > 0) & (p < 3))
            def _():
                ga[p - 1] = g.reshape(R + 6, W, C)[3 : 3 + R]
                da[p - 1] = dl[3 : 3 + R]

            return 0

        lax.fori_loop(0, 4, one, 0)

        def two(p, _):
            g = conv_plane(dbuf, p, column(wb), R + 4).astype(BF)
            gb[p] = g.reshape(R + 4, W, C)[2 : 2 + R]
            db[p] = delta_of(g, pre_b, p, R + 4, s_ * R - 2, 2 * d_ + p)
            return 0

        lax.fori_loop(0, 2, two, 0)

    g3, d2, g2, d1 = call(
        k3,
        (piece, piece, piece, sds((2, R + 4, W, C))),
        [VMEM, VMEM, VMEM, VMEM, VMEM, VMEM, VMEM],
        [pltpu.VMEM((6, R + 8, W, C), BF), pltpu.VMEM((4, R + 6, W, C), BF)],
    )(d3, d3_lo, d3_hi, wturn[3], wturn[2], pre2, pre1)
    d1_lo, d1_hi = both(d1)

    @placed
    def k4a(idx, own, lo, hi, wa, pre_a, e1, e2, e3, g1, dbuf, *rest):
        *sends, x = rest
        s_, d_ = idx[0], idx[1]
        assemble(x, lo, own, hi, d_, last)

        def one(p, _):
            g = conv_plane(x, p, column(wa), R + 2).astype(BF)
            dbuf[p] = delta_of(g, pre_a, p, R + 2, s_ * R - 1, 2 * d_ - 1 + p)

            @pl.when((p > 0) & (p < 3))
            def _():
                g1[p - 1] = g.reshape(R + 2, W, C)[1 : 1 + R]

            return 0

        lax.fori_loop(0, 4, one, 0)
        send_all(
            s_,
            sends,
            (
                lambda: dbuf[1:3, 1 : 1 + R],
                lambda: e1[:, 2 : 2 + R],
                lambda: e2[...],
                lambda: e3[:, 4 : 4 + R],
            ),
        )

    g1, d0, *d_send = call(
        k4a,
        (piece, sds((4, R + 2, W, C))) + (piece,) * 4,
        [VMEM, VMEM, VMEM, VMEM, VMEM, VMEM, VMEM, VMEM],
        [pltpu.VMEM((6, R + 4, W, C), BF)],
    )(d1, d1_lo, d1_hi, wturn[1], pre0, d1, d2, d3)
    d_got = three(sec, d_send)

    @placed
    def k4b(idx, dbuf, wb, g1, g2, g3, *rest):
        *sends, g0 = rest

        def two(p, _):
            g0[p] = conv_plane(dbuf, p, column(wb), R).astype(BF).reshape(R, W, C)
            return 0

        lax.fori_loop(0, 2, two, 0)
        send_all(idx[0], sends, (lambda: g0[...], lambda: g1[...], lambda: g2[...], lambda: g3[...]))

    g_send = call(
        k4b, (piece,) * 4, [VMEM, VMEM, VMEM, VMEM, VMEM], [pltpu.VMEM(piece.shape, BF)]
    )(d0, wturn[0], g1, g2, g3)
    g_got = []
    for k in (1, 2, 3):
        g_got.append(sec(g_send[k], k))

    @placed
    def kx(idx, x0, x1, x2, x3, x):
        x[:, 0] = jnp.zeros((4, W, C), BF)
        x[:, H + 1] = jnp.zeros((4, W, C), BF)
        for k, xs in enumerate((x0, x1, x2, x3)):
            x[:, pl.ds((idx[0] ^ k) * R + 1, R)] = xs[0:4]

    x_all = call(kx, sds((4, H + 2, W, C)), [VMEM] * 4, [], VMEM)(h_own, *h_got)

    ROWS = TAP + C

    @placed
    def kw(idx, x, e0, e1, e2, e3, keep, away, dl, wide, out):
        s_ = idx[0]
        for k, es in enumerate((e0, e1, e2, e3)):
            dl[:, pl.ds((s_ ^ k) * R, R)] = es[...]
        m = 4 * W
        pos = lax.broadcasted_iota(jnp.int32, (m, C), 0) % W

        def spread(i, acc):
            for p in range(2):
                v16 = dl[p, pl.ds(i * 4, 4)].reshape(m, C)
                v = v16.astype(F32)
                at = pl.ds(pl.multiple_of(i * m, m), m)
                wide[p, at, 0:C] = jnp.where(pos == W - 1, 0.0, pltpu.roll(v, m - 1, 0)).astype(BF)
                wide[p, at, C : 2 * C] = v16
                wide[p, at, 2 * C :] = jnp.where(pos == 0, 0.0, pltpu.roll(v, 1, 0)).astype(BF)
                acc = acc + jnp.sum(v.reshape(m // 8, 8, C), axis=0)
            return acc

        acc_b = jnp.sum(lax.fori_loop(0, H // 4, spread, jnp.zeros((8, C), F32)), axis=0, keepdims=True)

        def one(a, _):
            acc = jnp.zeros((3 * C, 3 * C), F32)
            for p in range(2):
                lhs = jnp.concatenate([x[p + a, b : b + H].reshape(H * W, C) for b in range(3)], axis=1)
                acc = acc + lax.dot_general(
                    lhs, wide[p], (((0,), (0,)), ((), ())), preferred_element_type=F32
                )
            for b in range(3):
                for j in range(3):
                    out[9 * a + 3 * b + j] = acc[b * C : (b + 1) * C, j * C : (j + 1) * C]
            return 0

        lax.fori_loop(0, 3, one, 0)
        first = lax.broadcasted_iota(jnp.int32, (C, C), 0) == 0
        out[27] = jnp.where(first, jnp.broadcast_to(acc_b, (C, C)), 0.0)
        keep[...] = out[pl.ds(idx[2] * 14, 14)].reshape(RH, C)
        away[...] = out[pl.ds((1 - idx[2]) * 14, 14)].reshape(RH, C).astype(BF)

    RH, RQ = ROWS // 2, ROWS // 8
    keep, away = call(
        kw,
        (sds((RH, C), F32), sds((RH, C))),
        [VMEM] * 5,
        [
            pltpu.VMEM((2, H, W, C), BF),
            pltpu.VMEM((2, H * W, 3 * C), BF),
            pltpu.VMEM((28, C, C), F32),
        ],
    )(x_all, d_send[0], *d_got)

    recv = swap(away)

    @placed
    def split(idx, keep, recv, mine, q1, q2, q3, buf):
        x = idx[1] % 4
        buf[...] = keep[...].reshape(4, RQ, C) + recv[...].reshape(4, RQ, C).astype(F32)
        mine[...] = buf[x]
        for k, q in enumerate((q1, q2, q3), 1):
            q[...] = buf[x ^ k].astype(BF)

    quart = sds((RQ, C))
    q, *qs = call(
        split, (sds((RQ, C), F32), quart, quart, quart), [VMEM, VMEM], [pltpu.VMEM((4, RQ, C), F32)]
    )(keep, recv)
    xs = three(xdep, [None, *qs])

    def add(own, q1, q2, q3, out):
        acc = own[...]
        for r in (q1, q2, q3):
            acc = acc + r[...].astype(F32)
        out[...] = acc.astype(BF)

    q = call(add, quart, [VMEM] * 4, [], VMEM)(q, *xs)
    ys = three(ydep, [q] * 4)

    @placed
    def ordered(idx, q0, q1, q2, q3, out, buf):
        y = idx[1] // 4
        for k, r in enumerate((q0, q1, q2, q3)):
            buf[k] = r[...].astype(F32)
        acc = buf[y]
        for j in range(1, 4):
            acc = acc + buf[y ^ j]
        out[...] = acc.astype(BF)

    q = call(ordered, sds((RQ, C)), [VMEM] * 4, [pltpu.VMEM((4, RQ, C), F32)], VMEM)(q, *ys)
    qs = [q] + three(xdep, [q] * 4)

    others = [swap(v) for v in qs]

    def fill(buf, x, pieces):
        for k, q in enumerate(pieces):
            buf[pl.ds(pl.multiple_of((x ^ k) * RQ, 8), RQ)] = q[...].astype(F32) * grad_scale

    @placed
    def place(idx, a0, a1, a2, a3, b0, b1, b2, b3, q0, q1, q2, q3, oa, ob, w_out, b_own, buf, sem):
        copies = []
        for k, (va, vb) in enumerate(((a0, b0), (a1, b1), (a2, b2), (a3, b3))):
            row = (idx[0] ^ k) * R
            copies.append(pltpu.make_async_copy(va.at[4:6], oa.at[:, pl.ds(row, R)], sem.at[2 * k]))
            copies.append(pltpu.make_async_copy(vb, ob.at[:, pl.ds(row, R)], sem.at[2 * k + 1]))
        for cp in copies:
            cp.start()
        fill(buf, idx[1] % 4, (q0, q1, q2, q3))
        b_own[...] = buf[TAP - RH : TAP - RH + 8]
        for c_, n in ((0, RH), (1, TAP - RH)):

            @pl.when(idx[2] == c_)
            def _():
                cp = pltpu.make_async_copy(
                    buf.at[pl.ds(0, n)], w_out.at[pl.ds(c_ * RH, n)], sem.at[8]
                )
                cp.start()
                cp.wait()

        for cp in copies:
            cp.wait()

    full = sds((2, H, W, C))
    out_h, out_g, w_part, b_own = call(
        place,
        (full, full, sds((TAP, C), F32), sds((8, C), F32)),
        [ANY] * 8 + [VMEM] * 4,
        [pltpu.VMEM((RH, C), F32), pltpu.SemaphoreType.DMA((9,))],
        (ANY, ANY, ANY, VMEM),
    )(h_own, *h_got, g_send[0], *g_got, *qs)

    @placed
    def finish(idx, q0, q1, q2, q3, b_own, w_in, w_out, b_out, buf, sem):
        parts = 4
        row = TAP - RH
        c_ = idx[2]
        step = RH // parts
        fill(buf, idx[1] % 4, (q0, q1, q2, q3))
        for i in range(parts):
            n = min(step, row - i * step)

            @pl.when(c_ == 1)
            def _():
                pltpu.make_async_copy(
                    buf.at[pl.ds(i * step, step)], w_out.at[pl.ds(i * step, step)], sem.at[i]
                ).start()

            @pl.when(c_ == 0)
            def _():
                pltpu.make_async_copy(
                    buf.at[pl.ds(i * step, n)], w_out.at[pl.ds(RH + i * step, n)], sem.at[i]
                ).start()

        b_out[...] = jnp.where(c_ == 1, b_own[...], buf[row : row + 8])[0:1]
        for i in range(parts):
            n = min(step, row - i * step)

            @pl.when(c_ == 1)
            def _():
                pltpu.make_async_copy(
                    buf.at[pl.ds(i * step, step)], w_out.at[pl.ds(i * step, step)], sem.at[i]
                ).wait()

            @pl.when(c_ == 0)
            def _():
                pltpu.make_async_copy(
                    buf.at[pl.ds(i * step, n)], w_out.at[pl.ds(RH + i * step, n)], sem.at[i]
                ).wait()

    w_grad, b_grad = pl.pallas_call(
        finish,
        name="finish",
        grid=(1,),
        out_shape=(sds((TAP, C), F32), sds((1, C), F32)),
        in_specs=[VMEM] * 5 + [ANY],
        out_specs=(ANY, VMEM),
        scratch_shapes=[pltpu.VMEM((RH, C), F32), pltpu.SemaphoreType.DMA((4,))],
        input_output_aliases={5: 0},
        compiler_params=pltpu.CompilerParams(vmem_limit_bytes=20 * 1024 * 1024),
    )(*others, b_own, w_part)
    return out_h[None, None], out_g[None, None], w_grad[None], b_grad


def solution(mesh):
    in_specs = (
        P("dp", "depth", None, None, None),
        P("section", None, None),
        P("section", None),
        P("dp", "depth", None, None, None),
    )
    out_specs = (
        P("section", "dp", "depth", None, None, None),
        P("section", "dp", "depth", None, None, None),
        P("section", None, None),
        P("section", None),
    )

    return jax.shard_map(shards, mesh=mesh, in_specs=in_specs, out_specs=out_specs, check_vma=False)
```
